256 devices in a mesh: dec: 16 (over x_hi, z), ra: 16 (over y, x_lo, core).
Axes of the slice: x: 4 (x_hi: 2, x_lo: 2; x = x_hi * 2 + x_lo), y: 4, z: 8, core: 2. Of those that a mesh axis runs over, the one named last changes fastest.
Arguments:
- split_maps: bfloat16 [6, 4096, 4096], P(None, 'dec', 'ra'), may hold values from -40 to 40
- white_noise: bfloat16 [8192, 8192], P('dec', 'ra'), may hold values from -6 to 6
Outputs:
- noise_realization: float32 [4096, 4096], P('dec', 'ra')
The draws below stay inside these ranges and needn't reach their ends.
All inputs are finite; a program needn't handle non-finite values.
Results may differ from the reference program's by a relative error of at most 0.0035.
The reference program's roundings to bfloat16 on the way (of `differ`) count: a program that leaves them out, or rounds other values in their place, can miss the bound.
Values may be sent and summed in bfloat16 or wider, within the bound.
No kernel may reach another device: no remote copies, remote signals or barrier semaphores. Data moves between devices by JAX's collectives and lax.ppermute only.
A program may use at most 64 MiB of HBM per device.

```python
import jax
import jax.numpy as jnp
from jax import lax

CORE = 256
SPLITS = 6
SMOOTH = 4
EXT = 512
NDEC = 4096
NRA = 4096
N_DEC = 16
N_RA = 16


def split_waves(key, count):
    subkeys = jax.random.split(key, 3)
    periods = CORE * jnp.exp(jax.random.uniform(subkeys[0], (SPLITS, 2), jnp.float32, jnp.log(2.0), jnp.log(6.0)))
    offsets = jax.random.uniform(subkeys[1], (SPLITS, 2), jnp.float32, 0.0, 2.0 * jnp.pi)
    heights = jax.random.uniform(subkeys[2], (SPLITS, 2), jnp.float32, 2.5, 5.0)
    places = jnp.arange(count, dtype=jnp.float32)
    phases = 2.0 * jnp.pi * places[None, None, :] / periods[:, :, None] + offsets[:, :, None]
    return jnp.sum(heights[:, :, None] * jnp.sin(phases), axis=1)


def draw_split_maps(key, part):
    subkeys = jax.random.split(key, 6)
    block_side = CORE // 4
    low_level, high_level = (0.4, 2.5)
    levels = jnp.exp(jax.random.uniform(subkeys[0], (NDEC // block_side, NRA // block_side), jnp.float32, jnp.log(low_level), jnp.log(high_level)))
    levels = jnp.repeat(jnp.repeat(levels, block_side, axis=0), block_side, axis=1)
    pixel_scale = jnp.exp(jax.random.uniform(subkeys[1], (NDEC, NRA), jnp.float32, jnp.log(0.7), jnp.log(1.4)))
    white_part = jax.random.normal(subkeys[2], (SPLITS, NDEC, NRA), jnp.float32)
    signal = 2.0 * jax.random.normal(subkeys[3], (NDEC, NRA), jnp.float32)
    banded = white_part + 0.8 * jnp.roll(white_part, 1, axis=2)
    along_rows = split_waves(subkeys[4], NDEC)
    along_cols = split_waves(subkeys[5], NRA)
    drifts = along_rows[:, :, None] + along_cols[:, None, :]
    values = signal[None] + drifts + (levels * pixel_scale)[None] * banded
    return jnp.clip(values, -40.0, 40.0).astype(jnp.bfloat16)


def shard_levels(rng, shape, cuts, least, high):
    loudness, own = 1.0, jax.random.fold_in(rng, 6)
    for dim, shards_of in cuts:
        steps = jnp.exp(jax.random.uniform(jax.random.fold_in(own, dim), (shards_of,), jnp.float32, least / len(cuts), high / len(cuts)))
        loudness = loudness * jnp.repeat(steps, shape[dim] // shards_of).reshape([-1 if axis == dim else 1 for axis in range(len(shape))])
    return loudness


def bell_draw(own_key, dims, width, limit, cuts=(), kind=jnp.bfloat16):
    values = jax.random.normal(own_key, dims, jnp.float32) * width
    if len(cuts) > 0:
        values = shard_levels(own_key, dims, cuts, -0.22, 0.18) * values
    return jnp.clip(values, min=-limit, max=limit).astype(kind)


def setup_inputs(seed: int = 0) -> dict:
    streams_of = jax.random.split(jax.random.key(seed), 3)
    return {
        "split_maps": draw_split_maps(jax.random.fold_in(streams_of[2], 71), 0),
        "white_noise": bell_draw(streams_of[1], (EXT * N_DEC, EXT * N_RA), 1.0, 6.0, ((0, 16), (1, 16))),
    }


def make_tables(length):
    indices = jnp.arange(length, dtype=jnp.int32)
    phases = indices[:, None] * indices[None, :] % length
    angles = phases.astype(jnp.float32) * (2.0 * jnp.pi / length)
    cos_table = jnp.cos(angles).astype(jnp.bfloat16)
    sin_table = jnp.sin(angles).astype(jnp.bfloat16)
    forward_left = jnp.concatenate([cos_table, sin_table], axis=0)
    forward_right = jnp.concatenate([jnp.concatenate([cos_table, -sin_table], axis=1), jnp.concatenate([-sin_table, -cos_table], axis=1)], axis=0)
    inverse_left = jnp.concatenate([jnp.concatenate([cos_table, -sin_table], axis=1), jnp.concatenate([sin_table, cos_table], axis=1)], axis=0)
    inverse_right = jnp.concatenate([cos_table, -sin_table], axis=0)
    profile = jnp.sin(jnp.pi * (indices.astype(jnp.float32) + 0.5) / length) ** 2
    window = profile[:, None] * profile[None, :]
    distance = jnp.abs(indices[:, None] - indices[None, :])
    distance = jnp.minimum(distance, length - distance)
    smoother = jnp.where(distance <= SMOOTH, 1.0 / (2 * SMOOTH + 1), 0.0).astype(jnp.float32)
    return (forward_left, forward_right, inverse_left, inverse_right, window, smoother)

def forward(tile, forward_left, forward_right):
    length = tile.shape[0]
    halves = jnp.dot(forward_left, tile, preferred_element_type=jnp.float32).astype(jnp.bfloat16)
    joined = jnp.concatenate([halves[:length], halves[length:]], axis=1)
    return jnp.dot(joined, forward_right, preferred_element_type=jnp.float32)

def tile_model(extended, noise_tile, tables):
    forward_left, forward_right, inverse_left, inverse_right, window, smoother = tables
    length = noise_tile.shape[0]
    splits = extended.shape[0]
    coadded = lax.optimization_barrier(jnp.mean(extended.astype(jnp.float32), axis=0))

    def accumulate(number, summed):
        member = lax.dynamic_index_in_dim(extended, number, 0, keepdims=False)
        differ = (window * (member.astype(jnp.float32) - coadded)).astype(jnp.bfloat16)
        spectra = forward(differ, forward_left, forward_right)
        return summed + spectra[:, :length] ** 2 + spectra[:, length:] ** 2
    spectrum_power = lax.fori_loop(0, splits, accumulate, jnp.zeros((length, length), jnp.float32))
    spectrum_power = spectrum_power / ((splits - 1) * jnp.sum(window * window))
    smooth = jnp.dot(jnp.dot(smoother, spectrum_power, precision=lax.Precision.HIGHEST), smoother, precision=lax.Precision.HIGHEST)
    filter_gain = jnp.sqrt(smooth)
    spectra = forward(noise_tile, forward_left, forward_right)
    shaped = jnp.concatenate([filter_gain * spectra[:, :length], filter_gain * spectra[:, length:]], axis=0).astype(jnp.bfloat16)
    mixture = jnp.dot(inverse_left, shaped, preferred_element_type=jnp.float32).astype(jnp.bfloat16)
    joined = jnp.concatenate([mixture[:length], mixture[length:]], axis=1)
    real_part = jnp.dot(joined, inverse_right, preferred_element_type=jnp.float32)
    return window * real_part / (length * length)

def reference(split_maps, white_noise):
    splits = split_maps.shape[0]
    margin = CORE // 2
    length = 2 * CORE
    tables = make_tables(length)
    padded = jnp.pad(split_maps, ((0, 0), (margin, margin), (margin, margin)))
    tile_rows = split_maps.shape[1] // CORE
    tile_cols = split_maps.shape[2] // CORE
    anchor = jnp.zeros((), jnp.int32)

    def one_tile(position):
        tile_row = (position // tile_cols).astype(jnp.int32)
        tile_col = (position % tile_cols).astype(jnp.int32)
        extended = lax.dynamic_slice(padded, (anchor, tile_row * CORE, tile_col * CORE), (splits, length, length))
        noise_tile = lax.dynamic_slice(white_noise, (tile_row * length, tile_col * length), (length, length))
        return tile_model(extended, noise_tile, tables)
    results = lax.map(one_tile, jnp.arange(tile_rows * tile_cols, dtype=jnp.int32))
    results = results.reshape(tile_rows, tile_cols, 2, CORE, 2, CORE)
    summed = jnp.zeros((tile_rows + 1, CORE, tile_cols + 1, CORE), jnp.float32)
    for row_half in range(2):
        for col_half in range(2):
            quarter = results[:, :, row_half, :, col_half, :].transpose(0, 2, 1, 3)
            summed = summed + jnp.pad(quarter, ((row_half, 1 - row_half), (0, 0), (col_half, 1 - col_half), (0, 0)))
    summed = summed.reshape((tile_rows + 1) * CORE, (tile_cols + 1) * CORE)
    return summed[margin:margin + tile_rows * CORE, margin:margin + tile_cols * CORE]
```

```python
import functools

import jax
import jax.numpy as jnp
import numpy as np
from jax import lax
from jax.experimental import pallas as pl
from jax.experimental.pallas import tpu as pltpu
from jax.sharding import PartitionSpec as P

import ml_dtypes

SMOOTH = 4
BF16 = jnp.bfloat16
F32 = jnp.float32


def host_tables(length):
    half = length // 2
    index = np.arange(length)
    phase = np.outer(index, index) % length
    cos = np.cos(2 * np.pi * phase / length)
    sin = np.sin(2 * np.pi * phase / length)
    sin[phase % half == 0] = 0.0
    cos = cos.astype(ml_dtypes.bfloat16).astype(np.float64)
    sin = sin.astype(ml_dtypes.bfloat16).astype(np.float64)

    def packed(rows):
        return np.ascontiguousarray(rows).astype(ml_dtypes.bfloat16)

    left = np.zeros((length + 16, length))
    left[:half] = cos[:half]
    left[half:length] = sin[:half]
    left[length] = cos[half]
    right = np.concatenate([cos[:, :half], sin[:, :half]], axis=1)
    right[:, half] = cos[:, half]
    inverse_right = np.concatenate([2 * cos[:half], -2 * sin[:half]], axis=0)
    inverse_right[0] = cos[0]
    inverse_right[half] = cos[half]
    order = np.concatenate([index[:half], [half], -index[1:half]])

    def near(first, second):
        apart = np.abs(first[:, None] - second[None, :]) % length
        return (np.minimum(apart, length - apart) <= SMOOTH).astype(np.float64)

    band_columns = near(order, order)
    band_rows = np.zeros((half + 16, half + 128))
    targets = np.arange(half + 1)
    band_rows[: half + 1, : half + 1] = near(targets, targets)
    first, last = half + 8, half + 16
    band_rows[: half + 1, first + 1 : first + 8] = near(targets, -np.arange(1, 8))
    band_rows[: half + 1, last : last + 8] = near(targets, -np.arange(half - 8, half))
    profile = np.sin(np.pi * (index + 0.5) / length) ** 2
    energy = np.sum(profile**2) ** 2
    return dict(
        left=packed(left),
        right=packed(right),
        inverse_right=packed(inverse_right),
        band_columns=packed(band_columns),
        band_rows=packed(band_rows),
        profile=profile.astype(np.float32),
        energy=float(energy),
    )


def dot(a, b):
    return jnp.dot(a, b, preferred_element_type=F32)


def first_column(shape):
    return lax.broadcasted_iota(jnp.int32, shape, 1) == 0


def three_parts(values):
    high = values.astype(BF16)
    rest = values - high.astype(F32)
    middle = rest.astype(BF16)
    low = (rest - middle.astype(F32)).astype(BF16)
    return high, middle, low


def quarters(spectra, half):
    length = 2 * half
    return (
        spectra[:half, :half],
        spectra[:half, half:],
        spectra[half:length, :half],
        spectra[half:length, half:],
        spectra[length : length + 8, :half],
        spectra[length : length + 8, half:],
    )


def noise_kernel(half, noise_ref, left_ref, right_ref, re_ref, im_ref):
    halves = dot(left_ref[...], noise_ref[...]).astype(BF16)
    spectra = dot(halves, right_ref[...])
    cc, cs, sc, ss, nc, ns = quarters(spectra, half)
    edge = first_column((half, half))
    re_ref[:half, :half] = jnp.where(edge, cc, cc - ss)
    re_ref[:half, half:] = jnp.where(edge, cs, cc + ss)
    im_ref[:half, :half] = -jnp.where(edge, sc, cs + sc)
    im_ref[:half, half:] = jnp.where(edge, -ss, cs - sc)
    edge = first_column((8, half))
    re_ref[half : half + 8, :half] = nc
    re_ref[half : half + 8, half:] = jnp.where(edge, ns, nc)
    im_ref[half : half + 8, :half] = jnp.where(edge, 0.0, -ns)
    im_ref[half : half + 8, half:] = jnp.where(edge, 0.0, ns)


def main_kernel(
    half, scale,
    core_ref, up_ref, down_ref, before_ref, after_ref, re_ref, im_ref,
    rows_ref, cols_ref, left_ref, right_ref, band_rows_ref, band_columns_ref,
    inverse_right_ref,
    top_ref, inside_ref, bottom_ref,
    tile, power, stacked,
):
    length = 2 * half
    margin = half // 2
    splits = core_ref.shape[0]

    def fill(source, row, col):
        height, width = source.shape[1:]
        step = 32
        pc = cols_ref[:1, col : col + width]

        def strip(number, carry):
            start = pl.multiple_of(number * step, step)
            target = pl.multiple_of(row + start, step)
            members = [source[s, pl.ds(start, step), :].astype(F32) for s in range(splits)]
            mean = functools.reduce(lambda a, b: a + b, members) * (1.0 / splits)
            weights = rows_ref[pl.ds(target, step), :1] * pc
            for s in range(splits):
                tile[s, pl.ds(target, step), col : col + width] = (
                    weights * (members[s] - mean)
                ).astype(BF16)
            return carry

        lax.fori_loop(0, height // step, strip, 0)

    fill(up_ref, 0, margin)
    fill(core_ref, margin, margin)
    fill(down_ref, margin + half, margin)
    fill(before_ref, 0, 0)
    fill(after_ref, 0, margin + half)

    power[...] = jnp.zeros_like(power)
    edge = first_column((half, half))
    edge8 = first_column((8, half))

    def accumulate(s, carry):
        halves = dot(left_ref[...], tile[s]).astype(BF16)
        spectra = dot(halves, right_ref[...])
        cc, cs, sc, ss, nc, ns = quarters(spectra, half)
        e = jnp.where(edge, cc, cc - ss)
        f = jnp.where(edge, sc, cs + sc)
        g = jnp.where(edge, cs, cc + ss)
        h = jnp.where(edge, ss, cs - sc)
        power[:half, :half] += e * e + f * f
        power[:half, half:] += g * g + h * h
        nc, ns = nc * nc, ns * ns
        power[half : half + 8, :half] += jnp.where(edge8, nc, nc + ns)
        power[half : half + 8, half:] += jnp.where(edge8, ns, nc + ns)
        return carry

    lax.fori_loop(0, splits, accumulate, 0)

    stack_rows = half + 128
    stacked[...] = jnp.zeros_like(stacked)
    for part, values in enumerate(three_parts(power[...])):
        stacked[part, : half + 8, :] = values
    for place, start in ((half + 8, 0), (half + 16, half - 8)):
        a = power[start : start + 8, :half]
        b = power[start : start + 8, half:]
        mirrored = jnp.concatenate(
            [jnp.where(edge8, a, b), jnp.where(edge8, b, a)], axis=1
        )
        for part, values in enumerate(three_parts(mirrored)):
            stacked[part, place : place + 8, :] = values
    smooth = (
        dot(band_rows_ref[...], stacked[2])
        + dot(band_rows_ref[...], stacked[1])
        + dot(band_rows_ref[...], stacked[0])
    )
    high, middle, low = three_parts(smooth)
    smooth = (
        dot(low, band_columns_ref[...])
        + dot(middle, band_columns_ref[...])
        + dot(high, band_columns_ref[...])
    )
    gain = jnp.sqrt(jnp.maximum(smooth[: half + 8], 0.0) * scale)
    gr = (gain * re_ref[...]).astype(BF16)
    gi = (gain * im_ref[...]).astype(BF16)
    er, fr = gr[:half, :half], gr[:half, half:]
    ei, fi = gi[:half, :half], gi[:half, half:]
    start = lax.broadcasted_iota(jnp.int32, (half, half), 0) == 0
    nyquist_u = gr[half : half + 1, :half]
    nyquist_v = jnp.where(edge8[:1], gr[half : half + 1, half:], gi[half : half + 1, :half])
    zero = jnp.zeros((), BF16)
    near_u = jnp.concatenate([er, jnp.where(start, nyquist_u, -ei)], axis=0)
    far_u = jnp.concatenate(
        [jnp.where(edge, er, fr), -jnp.where(edge, ei, fi)], axis=0
    )
    near_v = jnp.concatenate(
        [jnp.where(edge, fr, ei), jnp.where(start, nyquist_v, jnp.where(edge, -fi, er))], axis=0
    )
    far_v = jnp.concatenate(
        [jnp.where(edge, fr, -fi), -jnp.where(edge, fi, fr)], axis=0
    )
    start = lax.broadcasted_iota(jnp.int32, (length, half), 0) % half == 0
    far_u, far_v = jnp.where(start, zero, far_u), jnp.where(start, zero, far_v)
    u = dot(right_ref[...], near_u) + dot(right_ref[...], far_u)
    v = dot(right_ref[...], near_v) + dot(right_ref[...], far_v)
    joined = jnp.concatenate([u.astype(BF16), v.astype(BF16)], axis=1)
    real_part = dot(joined, inverse_right_ref[...])
    window = rows_ref[:, :1] * cols_ref[:1, :]
    values = window * real_part * (1.0 / (length * length))
    top_ref[...] = values[:margin].astype(BF16)
    bottom_ref[...] = values[margin + half :].astype(BF16)
    inside_ref[...] = values[margin : margin + half]


def steps(axis):
    count = lax.axis_size(axis)
    forward = [(i, i + 1) for i in range(count - 1)]
    backward = [(target, source) for source, target in forward]
    return forward, backward


def exchange(last, first, axis):
    forward, backward = steps(axis)
    return lax.ppermute(last, axis, forward), lax.ppermute(first, axis, backward)


def whole(count):
    return [pl.BlockSpec(memory_space=pltpu.VMEM)] * count


def shards(tables, split_maps, white_noise):
    splits, core_side, _ = split_maps.shape
    half = core_side
    margin = core_side // 2
    length = 2 * core_side
    constant = {k: jnp.asarray(v) for k, v in tables.items() if k != "energy"}
    profile = tables["profile"]
    rows = jnp.asarray(np.ascontiguousarray(np.broadcast_to(profile[:, None], (length, 128))))
    cols = jnp.asarray(np.ascontiguousarray(np.broadcast_to(profile[None, :], (8, length))))
    scale = 1.0 / ((2 * SMOOTH + 1) ** 2 * (splits - 1) * tables["energy"])

    spectrum = jax.ShapeDtypeStruct((half + 8, length), F32)
    re, im = pl.pallas_call(
        functools.partial(noise_kernel, half),
        out_shape=(spectrum, spectrum),
        in_specs=whole(3),
        out_specs=tuple(whole(2)),
        cost_estimate=pl.CostEstimate(flops=4 * length**3, bytes_accessed=6 * length**2, transcendentals=0),
        name="noise_spectrum",
    )(white_noise, constant["left"], constant["right"])

    up, down = exchange(split_maps[:, core_side - margin :], split_maps[:, :margin], "dec")
    tall = jnp.concatenate([up, split_maps, down], axis=1)
    before, after = exchange(tall[:, :, core_side - margin :], tall[:, :, :margin], "ra")

    strip = jax.ShapeDtypeStruct((margin, length), BF16)
    top, inside, bottom = pl.pallas_call(
        functools.partial(main_kernel, half, scale),
        out_shape=(strip, jax.ShapeDtypeStruct((half, length), F32), strip),
        in_specs=whole(14),
        out_specs=tuple(whole(3)),
        scratch_shapes=[
            pltpu.VMEM((splits, length, length), BF16),
            pltpu.VMEM((half + 8, length), F32),
            pltpu.VMEM((3, half + 128, length), BF16),
        ],
        cost_estimate=pl.CostEstimate(flops=36 * length**3, bytes_accessed=20 * length**2, transcendentals=0),
        name="tile_model",
    )(
        split_maps, up, down, before, after, re, im, rows, cols,
        constant["left"], constant["right"], constant["band_rows"], constant["band_columns"],
        constant["inverse_right"],
    )

    from_up, from_down = exchange(bottom, top, "dec")
    inside = inside + jnp.concatenate([from_up, from_down], axis=0).astype(F32)
    from_before, from_after = exchange(
        inside[:, length - margin :].astype(BF16), inside[:, :margin].astype(BF16), "ra"
    )
    return inside[:, margin : margin + core_side] + jnp.concatenate(
        [from_before, from_after], axis=1
    ).astype(F32)


def solution(mesh):
    tables = host_tables(512)
    placed = (P(None, "dec", "ra"), P("dec", "ra"))
    return jax.shard_map(
        functools.partial(shards, tables), mesh=mesh, in_specs=placed, out_specs=P("dec", "ra"), check_vma=False
    )
```

```python
import functools

import jax
import jax.numpy as jnp
import numpy as np
from jax import lax
from jax.experimental import pallas as pl
from jax.experimental.pallas import tpu as pltpu
from jax.sharding import PartitionSpec as P

import ml_dtypes

SMOOTH = 4
BF16 = jnp.bfloat16
F32 = jnp.float32


def host_tables(length):
    half = length // 2
    index = np.arange(length)
    phase = np.outer(index, index) % length
    cos = np.cos(2 * np.pi * phase / length)
    sin = np.sin(2 * np.pi * phase / length)
    sin[phase % half == 0] = 0.0
    cos = cos.astype(ml_dtypes.bfloat16).astype(np.float64)
    sin = sin.astype(ml_dtypes.bfloat16).astype(np.float64)

    def packed(rows):
        return np.ascontiguousarray(rows).astype(ml_dtypes.bfloat16)

    left = np.zeros((length + 16, length))
    left[:half] = cos[:half]
    left[half:length] = sin[:half]
    left[length] = cos[half]
    right = np.concatenate([cos[:, :half], sin[:, :half]], axis=1)
    right[:, half] = cos[:, half]
    margin = half // 2
    right = np.roll(right, -margin, axis=0)
    right = np.concatenate([right[:half], np.roll(right[half:], margin, axis=0)], axis=0)
    inverse_right = np.concatenate([2 * cos[:half], -2 * sin[:half]], axis=0)
    inverse_right[0] = cos[0]
    inverse_right[half] = cos[half]
    order = np.concatenate([index[:half], [half], -index[1:half]])

    def near(first, second):
        apart = np.abs(first[:, None] - second[None, :]) % length
        return (np.minimum(apart, length - apart) <= SMOOTH).astype(np.float64)

    band_columns = near(order, order)
    band_rows = np.zeros((half + 16, half + 128))
    targets = np.arange(half + 1)
    band_rows[: half + 1, : half + 1] = near(targets, targets)
    first, last = half + 8, half + 16
    band_rows[: half + 1, first + 1 : first + 8] = near(targets, -np.arange(1, 8))
    band_rows[: half + 1, last : last + 8] = near(targets, -np.arange(half - 8, half))
    profile = np.sin(np.pi * (index + 0.5) / length) ** 2
    energy = np.sum(profile**2) ** 2
    return dict(
        left=packed(left),
        right=packed(right),
        inverse_right=packed(inverse_right),
        band_columns=packed(band_columns),
        band_rows=packed(band_rows),
        profile=profile.astype(np.float32),
        energy=float(energy),
    )


def dot(a, b):
    return jnp.dot(a, b, preferred_element_type=F32)


def first_column(shape):
    return lax.broadcasted_iota(jnp.int32, shape, 1) == 0


def three_parts(values):
    high = values.astype(BF16)
    rest = values - high.astype(F32)
    middle = rest.astype(BF16)
    low = (rest - middle.astype(F32)).astype(BF16)
    return high, middle, low


def quarters(spectra, half):
    length = 2 * half
    return (
        spectra[:half, :half],
        spectra[:half, half:],
        spectra[half:length, :half],
        spectra[half:length, half:],
        spectra[length : length + 8, :half],
        spectra[length : length + 8, half:],
    )


def noise_kernel(half, noise_ref, left_ref, right_ref, re_ref, im_ref):
    margin = half // 2
    halves = dot(left_ref[...], noise_ref[...]).astype(BF16)
    spectra = (
        dot(halves[:, margin : margin + half], right_ref[:half])
        + dot(halves[:, :margin], right_ref[half : half + margin])
        + dot(halves[:, margin + half :], right_ref[half + margin :])
    )
    cc, cs, sc, ss, nc, ns = quarters(spectra, half)
    edge = first_column((half, half))
    re_ref[:half, :half] = jnp.where(edge, cc, cc - ss)
    re_ref[:half, half:] = jnp.where(edge, cs, cc + ss)
    im_ref[:half, :half] = -jnp.where(edge, sc, cs + sc)
    im_ref[:half, half:] = jnp.where(edge, -ss, cs - sc)
    edge = first_column((8, half))
    re_ref[half : half + 8, :half] = nc
    re_ref[half : half + 8, half:] = jnp.where(edge, ns, nc)
    im_ref[half : half + 8, :half] = jnp.where(edge, 0.0, -ns)
    im_ref[half : half + 8, half:] = jnp.where(edge, 0.0, ns)


def aligned(offset, step):
    return offset if isinstance(offset, int) else pl.multiple_of(offset, step)


def fill(tile, source, rows_ref, cols_ref, source_row, height, row, col, tile_col):
    splits, width = source.shape[0], source.shape[2]
    step = 32
    pc = cols_ref[:1, pl.ds(aligned(col, 128), width)]

    def strip(number, carry):
        start = pl.multiple_of(source_row + number * step, step)
        target = pl.multiple_of(row + number * step, step)
        members = [source[s, pl.ds(start, step), :].astype(F32) for s in range(splits)]
        mean = functools.reduce(lambda a, b: a + b, members) * (1.0 / splits)
        weights = rows_ref[pl.ds(target, step), :1] * pc
        for s in range(splits):
            tile[s, pl.ds(target, step), pl.ds(aligned(tile_col, 128), width)] = (
                weights * (members[s] - mean)
            ).astype(BF16)
        return carry

    lax.fori_loop(0, height // step, strip, 0)


def sides(half):
    far = half + half // 2
    first = jnp.where(lax.axis_index("dec") % 2 == 0, far, 0)
    outer = jnp.where(lax.axis_index("ra") % 2 == 0, 0, far)
    return first, far - first, outer, far - outer


def core_kernel(half, core_ref, first_ref, second_ref, rows_ref, cols_ref, left_ref, halves_ref, tile):
    margin = half // 2
    splits = core_ref.shape[0]
    first, second, _, _ = sides(half)
    fill(tile, core_ref, rows_ref, cols_ref, 0, half, margin, margin, 0)
    fill(tile, first_ref, rows_ref, cols_ref, 0, margin, first, margin, 0)
    fill(tile, second_ref, rows_ref, cols_ref, 0, margin, second, margin, 0)

    def transform(s, carry):
        halves_ref[s] = dot(left_ref[...], tile[s]).astype(BF16)
        return carry

    lax.fori_loop(0, splits, transform, 0)


def main_kernel(
    half, scale,
    core_ref, outer_ref, first_ref, second_ref, inner_ref, re_ref, im_ref,
    rows_ref, cols_ref, left_ref, right_ref, band_rows_ref, band_columns_ref,
    inverse_right_ref,
    first_out_ref, second_out_ref, inside_ref,
    tile, power, stacked, strips,
):
    length = 2 * half
    margin = half // 2
    splits = core_ref.shape[0]
    first, second, outer, inner = sides(half)
    outer_col = jnp.where(outer == 0, 0, margin)
    inner_col = margin - outer_col
    fill(tile, outer_ref, rows_ref, cols_ref, 0, half, margin, outer, outer_col)
    fill(tile, first_ref, rows_ref, cols_ref, 0, margin, first, outer, outer_col)
    fill(tile, second_ref, rows_ref, cols_ref, 0, margin, second, outer, outer_col)
    fill(tile, inner_ref, rows_ref, cols_ref, 0, margin, first, inner, inner_col)
    fill(tile, inner_ref, rows_ref, cols_ref, margin, half, margin, inner, inner_col)
    fill(tile, inner_ref, rows_ref, cols_ref, margin + half, margin, second, inner, inner_col)

    edge = first_column((half, half))
    edge8 = first_column((8, half))

    def accumulate(s, carry):
        halves = jnp.concatenate(
            [core_ref[s], dot(left_ref[...], tile[s]).astype(BF16)], axis=1
        )
        spectra = dot(halves, right_ref[...])
        cc, cs, sc, ss, nc, ns = quarters(spectra, half)
        e = jnp.where(edge, cc, cc - ss)
        f = jnp.where(edge, sc, cs + sc)
        g = jnp.where(edge, cs, cc + ss)
        h = jnp.where(edge, ss, cs - sc)
        nc, ns = nc * nc, ns * ns
        terms = (
            e * e + f * f, g * g + h * h, jnp.where(edge8, nc, nc + ns), jnp.where(edge8, ns, nc + ns)
        )
        places = (
            (slice(0, half), slice(0, half)), (slice(0, half), slice(half, length)),
            (slice(half, half + 8), slice(0, half)), (slice(half, half + 8), slice(half, length)),
        )
        for term, place in zip(terms, places):
            power[place] = term if carry else power[place] + term

    accumulate(0, True)
    for s in range(1, splits):
        accumulate(s, False)

    stacked[:, half + 24 :, :] = jnp.zeros((3, stacked.shape[1] - half - 24, length), BF16)
    for part, values in enumerate(three_parts(power[...])):
        stacked[part, : half + 8, :] = values
    for place, start in ((half + 8, 0), (half + 16, half - 8)):
        a = power[start : start + 8, :half]
        b = power[start : start + 8, half:]
        mirrored = jnp.concatenate(
            [jnp.where(edge8, a, b), jnp.where(edge8, b, a)], axis=1
        )
        for part, values in enumerate(three_parts(mirrored)):
            stacked[part, place : place + 8, :] = values
    smooth = (
        dot(band_rows_ref[...], stacked[2])
        + dot(band_rows_ref[...], stacked[1])
        + dot(band_rows_ref[...], stacked[0])
    )
    high, middle, low = three_parts(smooth)
    smooth = (
        dot(low, band_columns_ref[...])
        + dot(middle, band_columns_ref[...])
        + dot(high, band_columns_ref[...])
    )
    gain = jnp.sqrt(jnp.maximum(smooth[: half + 8], 0.0) * scale)
    gr = (gain * re_ref[...]).astype(BF16)
    gi = (gain * im_ref[...]).astype(BF16)
    er, fr = gr[:half, :half], gr[:half, half:]
    ei, fi = gi[:half, :half], gi[:half, half:]
    start = lax.broadcasted_iota(jnp.int32, (half, half), 0) == 0
    nyquist_u = gr[half : half + 1, :half]
    nyquist_v = jnp.where(edge8[:1], gr[half : half + 1, half:], gi[half : half + 1, :half])
    zero = jnp.zeros((), BF16)
    near_u = jnp.concatenate([er, jnp.where(start, nyquist_u, -ei)], axis=0)
    far_u = jnp.concatenate(
        [jnp.where(edge, er, fr), -jnp.where(edge, ei, fi)], axis=0
    )
    near_v = jnp.concatenate(
        [jnp.where(edge, fr, ei), jnp.where(start, nyquist_v, jnp.where(edge, -fi, er))], axis=0
    )
    far_v = jnp.concatenate(
        [jnp.where(edge, fr, -fi), -jnp.where(edge, fi, fr)], axis=0
    )
    start = lax.broadcasted_iota(jnp.int32, (length, half), 0) % half == 0
    far_u, far_v = jnp.where(start, zero, far_u), jnp.where(start, zero, far_v)
    u = dot(right_ref[...], near_u) + dot(right_ref[...], far_u)
    v = dot(right_ref[...], near_v) + dot(right_ref[...], far_v)
    joined = jnp.concatenate([u.astype(BF16), v.astype(BF16)], axis=1)
    real_part = dot(joined, inverse_right_ref[...])
    norm = 1.0 / (length * length)
    pc = cols_ref[:1, :]
    inside_ref[...] = rows_ref[margin : margin + half, :1] * pc * real_part[:half] * norm
    strips[:margin] = (rows_ref[:margin, :1] * pc * real_part[half : half + margin] * norm).astype(BF16)
    strips[margin:] = (rows_ref[margin + half :, :1] * pc * real_part[half + margin :] * norm).astype(BF16)
    place = pl.multiple_of(jnp.where(first == 0, 0, margin), margin)
    first_out_ref[...] = strips[pl.ds(place, margin), :]
    second_out_ref[...] = strips[pl.ds(pl.multiple_of(margin - place, margin), margin), :]


def fold_rows_kernel(half, inside_ref, first_ref, second_ref, center_ref, outer_ref, inner_ref, total):
    margin = half // 2
    first, second, outer, inner = sides(half)
    for source, place in ((first_ref, first), (second_ref, second)):
        rows = pl.ds(pl.multiple_of(jnp.where(place == 0, 0, margin), margin), margin)
        total[rows, :] = inside_ref[rows, :] + source[...].astype(F32)
    center_ref[...] = total[:, margin : margin + half]
    outer_ref[...] = total[:, pl.ds(pl.multiple_of(outer, margin), margin)].astype(BF16)
    inner_ref[...] = total[:, pl.ds(pl.multiple_of(inner, margin), margin)].astype(BF16)


def fold_columns_kernel(half, center_ref, outer_ref, inner_ref, out_ref):
    margin = half // 2
    _, _, outer, inner = sides(half)
    for source, place in ((outer_ref, outer), (inner_ref, inner)):
        columns = pl.ds(pl.multiple_of(jnp.where(place == 0, 0, margin), margin), margin)
        out_ref[:, columns] = center_ref[:, columns] + source[...].astype(F32)


def swap(values, axis, offset):
    count = lax.axis_size(axis)
    pairs = [(i, i + 1) for i in range(offset, count - 1, 2)]
    return lax.ppermute(values, axis, pairs + [(b, a) for a, b in pairs])


def whole(count):
    return [pl.BlockSpec(memory_space=pltpu.VMEM)] * count


def kernel_call(body, name, outs, count, scratch=(), flops=0):
    return pl.pallas_call(
        body,
        out_shape=outs,
        in_specs=whole(count),
        out_specs=jax.tree.map(lambda _: pl.BlockSpec(memory_space=pltpu.VMEM), outs),
        scratch_shapes=list(scratch),
        cost_estimate=pl.CostEstimate(flops=flops, bytes_accessed=1 << 20, transcendentals=0),
        name=name,
    )


def shards(tables, split_maps, white_noise):
    splits, core_side, _ = split_maps.shape
    half = core_side
    margin = core_side // 2
    length = 2 * core_side
    constant = {k: jnp.asarray(v) for k, v in tables.items() if k != "energy"}
    profile = tables["profile"]
    rows = jnp.asarray(np.ascontiguousarray(np.broadcast_to(profile[:, None], (length, 128))))
    cols = jnp.asarray(np.ascontiguousarray(np.broadcast_to(profile[None, :], (8, length))))
    scale = 1.0 / ((2 * SMOOTH + 1) ** 2 * (splits - 1) * tables["energy"])
    odd_row = lax.axis_index("dec") % 2
    odd_col = lax.axis_index("ra") % 2
    cube = length**3

    outer_columns = lax.dynamic_slice_in_dim(split_maps, odd_col * margin, margin, axis=2)
    first_rows = lax.dynamic_slice_in_dim(split_maps, (1 - odd_row) * margin, margin, axis=1)
    second_rows = lax.dynamic_slice_in_dim(split_maps, odd_row * margin, margin, axis=1)
    outer = swap(outer_columns, "ra", 1)
    first = swap(first_rows, "dec", 0)
    second = swap(second_rows, "dec", 1)

    spectrum = jax.ShapeDtypeStruct((half + 8, length), F32)
    re, im = kernel_call(
        functools.partial(noise_kernel, half), "noise_spectrum", (spectrum, spectrum), 3, flops=3 * cube
    )(white_noise, constant["left"], constant["right"])

    first_corner = swap(lax.dynamic_slice_in_dim(outer, (1 - odd_row) * margin, margin, axis=1), "dec", 0)
    second_corner = swap(lax.dynamic_slice_in_dim(outer, odd_row * margin, margin, axis=1), "dec", 1)
    inner = swap(
        jnp.concatenate(
            [
                lax.dynamic_slice_in_dim(block, (1 - odd_col) * margin, margin, axis=2)
                for block in (first, split_maps, second)
            ],
            axis=1,
        ),
        "ra",
        0,
    )
    halves = kernel_call(
        functools.partial(core_kernel, half),
        "core_columns",
        jax.ShapeDtypeStruct((splits, length + 16, half), BF16),
        6,
        [pltpu.VMEM((splits, length, half), BF16)],
        flops=6 * cube,
    )(split_maps, first, second, rows, cols, constant["left"])

    strip = jax.ShapeDtypeStruct((margin, length), BF16)
    first, second, inside = kernel_call(
        functools.partial(main_kernel, half, scale),
        "tile_model",
        (strip, strip, jax.ShapeDtypeStruct((half, length), F32)),
        14,
        [
            pltpu.VMEM((splits, length, half), BF16),
            pltpu.VMEM((half + 8, length), F32),
            pltpu.VMEM((3, half + 128, length), BF16),
            pltpu.VMEM((half, length), BF16),
        ],
        flops=20 * cube,
    )(
        halves, outer, first_corner, second_corner, inner, re, im, rows, cols,
        constant["left"], constant["right"], constant["band_rows"], constant["band_columns"],
        constant["inverse_right"],
    )

    first = swap(first, "dec", 0)
    second = swap(second, "dec", 1)
    column = jax.ShapeDtypeStruct((half, margin), BF16)
    block = jax.ShapeDtypeStruct((half, half), F32)
    center, outer, inner = kernel_call(
        functools.partial(fold_rows_kernel, half), "fold_rows", (block, column, column), 3,
        [pltpu.VMEM((half, length), F32)],
    )(inside, first, second)
    outer = swap(outer, "ra", 1)
    inner = swap(inner, "ra", 0)
    return kernel_call(functools.partial(fold_columns_kernel, half), "fold_columns", block, 3)(
        center, outer, inner
    )


def solution(mesh):
    tables = host_tables(512)
    placed = (P(None, "dec", "ra"), P("dec", "ra"))
    return jax.shard_map(
        functools.partial(shards, tables), mesh=mesh, in_specs=placed, out_specs=P("dec", "ra"), check_vma=False
    )
```

```python
import functools

import jax
import jax.numpy as jnp
import numpy as np
from jax import lax
from jax.experimental import pallas as pl
from jax.experimental.pallas import tpu as pltpu
from jax.sharding import PartitionSpec as P

import ml_dtypes

SMOOTH = 4
BF16 = jnp.bfloat16
F32 = jnp.float32


def host_tables(length):
    half = length // 2
    index = np.arange(length)
    phase = np.outer(index, index) % length
    cos = np.cos(2 * np.pi * phase / length)
    sin = np.sin(2 * np.pi * phase / length)
    sin[phase % half == 0] = 0.0
    cos = cos.astype(ml_dtypes.bfloat16).astype(np.float64)
    sin = sin.astype(ml_dtypes.bfloat16).astype(np.float64)

    def packed(rows):
        return np.ascontiguousarray(rows).astype(ml_dtypes.bfloat16)

    left = np.zeros((length + 16, length))
    left[:half] = cos[:half]
    left[half:length] = sin[:half]
    left[length] = cos[half]
    right = np.concatenate([cos[:, :half], sin[:, :half]], axis=1)
    right[:, half] = cos[:, half]
    margin = half // 2
    right = np.roll(right, -margin, axis=0)
    right = np.concatenate([right[:half], np.roll(right[half:], margin, axis=0)], axis=0)
    inverse_right = np.concatenate([2 * cos[:half], -2 * sin[:half]], axis=0)
    inverse_right[0] = cos[0]
    inverse_right[half] = cos[half]
    order = np.concatenate([index[:half], [half], -index[1:half]])

    def near(first, second):
        apart = np.abs(first[:, None] - second[None, :]) % length
        return (np.minimum(apart, length - apart) <= SMOOTH).astype(np.float64)

    band_columns = near(order, order)
    band_rows = np.zeros((half + 16, half + 128))
    targets = np.arange(half + 1)
    band_rows[: half + 1, : half + 1] = near(targets, targets)
    first, last = half + 8, half + 16
    band_rows[: half + 1, first + 1 : first + 8] = near(targets, -np.arange(1, 8))
    band_rows[: half + 1, last : last + 8] = near(targets, -np.arange(half - 8, half))
    profile = np.sin(np.pi * (index + 0.5) / length) ** 2
    energy = np.sum(profile**2) ** 2
    return dict(
        left=packed(left),
        right=packed(right),
        inverse_right=packed(inverse_right),
        band_columns=packed(band_columns),
        band_rows=packed(band_rows),
        profile=profile.astype(np.float32),
        energy=float(energy),
    )


def dot(a, b):
    return jnp.dot(a, b, preferred_element_type=F32)


def first_column(shape):
    return lax.broadcasted_iota(jnp.int32, shape, 1) == 0


def three_parts(values):
    high = values.astype(BF16)
    rest = values - high.astype(F32)
    middle = rest.astype(BF16)
    low = (rest - middle.astype(F32)).astype(BF16)
    return high, middle, low


def quarters(spectra, half):
    length = 2 * half
    return (
        spectra[:half, :half],
        spectra[:half, half:],
        spectra[half:length, :half],
        spectra[half:length, half:],
        spectra[length : length + 8, :half],
        spectra[length : length + 8, half:],
    )


def noise_kernel(half, noise_ref, left_ref, right_ref, re_ref, im_ref):
    margin = half // 2
    halves = dot(left_ref[...], noise_ref[...]).astype(BF16)
    spectra = (
        dot(halves[:, margin : margin + half], right_ref[:half])
        + dot(halves[:, :margin], right_ref[half : half + margin])
        + dot(halves[:, margin + half :], right_ref[half + margin :])
    )
    cc, cs, sc, ss, nc, ns = quarters(spectra, half)
    edge = first_column((half, half))
    re_ref[:half, :half] = jnp.where(edge, cc, cc - ss)
    re_ref[:half, half:] = jnp.where(edge, cs, cc + ss)
    im_ref[:half, :half] = -jnp.where(edge, sc, cs + sc)
    im_ref[:half, half:] = jnp.where(edge, -ss, cs - sc)
    edge = first_column((8, half))
    re_ref[half : half + 8, :half] = nc
    re_ref[half : half + 8, half:] = jnp.where(edge, ns, nc)
    im_ref[half : half + 8, :half] = jnp.where(edge, 0.0, -ns)
    im_ref[half : half + 8, half:] = jnp.where(edge, 0.0, ns)


def aligned(offset, step):
    return offset if isinstance(offset, int) else pl.multiple_of(offset, step)


def fill(tile, source, rows_ref, cols_ref, source_row, height, row, col, tile_col):
    splits, width = source.shape[0], source.shape[2]
    step = 32
    pc = cols_ref[:1, pl.ds(aligned(col, 128), width)]

    def strip(number, carry):
        start = pl.multiple_of(source_row + number * step, step)
        target = pl.multiple_of(row + number * step, step)
        members = [source[s, pl.ds(start, step), :].astype(F32) for s in range(splits)]
        mean = functools.reduce(lambda a, b: a + b, members) * (1.0 / splits)
        weights = rows_ref[pl.ds(target, step), :1] * pc
        for s in range(splits):
            tile[s, pl.ds(target, step), pl.ds(aligned(tile_col, 128), width)] = (
                weights * (members[s] - mean)
            ).astype(BF16)
        return carry

    lax.fori_loop(0, height // step, strip, 0)


def sides(half):
    far = half + half // 2
    first = jnp.where(lax.axis_index("dec") % 2 == 0, far, 0)
    outer = jnp.where(lax.axis_index("ra") % 2 == 0, 0, far)
    return first, far - first, outer, far - outer


def core_kernel(half, core_ref, first_ref, second_ref, rows_ref, cols_ref, left_ref, halves_ref, tile):
    margin = half // 2
    splits = core_ref.shape[0]
    first, second, _, _ = sides(half)
    fill(tile, core_ref, rows_ref, cols_ref, 0, half, margin, margin, 0)
    fill(tile, first_ref, rows_ref, cols_ref, 0, margin, first, margin, 0)
    fill(tile, second_ref, rows_ref, cols_ref, 0, margin, second, margin, 0)

    for s in range(splits):
        halves_ref[s] = dot(left_ref[...], tile[s]).astype(BF16)


def main_kernel(
    half, scale,
    core_ref, outer_ref, first_ref, second_ref, inner_ref, re_ref, im_ref,
    rows_ref, cols_ref, left_ref, right_ref, band_rows_ref, band_columns_ref,
    inverse_right_ref,
    first_out_ref, second_out_ref, inside_ref,
    tile, power, stacked, strips,
):
    length = 2 * half
    margin = half // 2
    splits = core_ref.shape[0]
    first, second, outer, inner = sides(half)
    outer_col = jnp.where(outer == 0, 0, margin)
    inner_col = margin - outer_col
    fill(tile, outer_ref, rows_ref, cols_ref, 0, half, margin, outer, outer_col)
    fill(tile, first_ref, rows_ref, cols_ref, 0, margin, first, outer, outer_col)
    fill(tile, second_ref, rows_ref, cols_ref, 0, margin, second, outer, outer_col)
    fill(tile, inner_ref, rows_ref, cols_ref, 0, margin, first, inner, inner_col)
    fill(tile, inner_ref, rows_ref, cols_ref, margin, half, margin, inner, inner_col)
    fill(tile, inner_ref, rows_ref, cols_ref, margin + half, margin, second, inner, inner_col)

    edge = first_column((half, half))
    edge8 = first_column((8, half))

    def accumulate(s, carry):
        halves = jnp.concatenate(
            [core_ref[s], dot(left_ref[...], tile[s]).astype(BF16)], axis=1
        )
        spectra = dot(halves, right_ref[...])
        cc, cs, sc, ss, nc, ns = quarters(spectra, half)
        e = jnp.where(edge, cc, cc - ss)
        f = jnp.where(edge, sc, cs + sc)
        g = jnp.where(edge, cs, cc + ss)
        h = jnp.where(edge, ss, cs - sc)
        nc, ns = nc * nc, ns * ns
        terms = (
            e * e + f * f, g * g + h * h, jnp.where(edge8, nc, nc + ns), jnp.where(edge8, ns, nc + ns)
        )
        places = (
            (slice(0, half), slice(0, half)), (slice(0, half), slice(half, length)),
            (slice(half, half + 8), slice(0, half)), (slice(half, half + 8), slice(half, length)),
        )
        for term, place in zip(terms, places):
            power[place] = term if carry else power[place] + term

    accumulate(0, True)
    for s in range(1, splits):
        accumulate(s, False)

    stacked[:, half + 24 :, :] = jnp.zeros((3, stacked.shape[1] - half - 24, length), BF16)
    for part, values in enumerate(three_parts(power[...])):
        stacked[part, : half + 8, :] = values
    for place, start in ((half + 8, 0), (half + 16, half - 8)):
        a = power[start : start + 8, :half]
        b = power[start : start + 8, half:]
        mirrored = jnp.concatenate(
            [jnp.where(edge8, a, b), jnp.where(edge8, b, a)], axis=1
        )
        for part, values in enumerate(three_parts(mirrored)):
            stacked[part, place : place + 8, :] = values
    smooth = (
        dot(band_rows_ref[...], stacked[2])
        + dot(band_rows_ref[...], stacked[1])
        + dot(band_rows_ref[...], stacked[0])
    )
    high, middle, low = three_parts(smooth)
    smooth = (
        dot(low, band_columns_ref[...])
        + dot(middle, band_columns_ref[...])
        + dot(high, band_columns_ref[...])
    )
    gain = jnp.sqrt(jnp.maximum(smooth[: half + 8], 0.0) * scale)
    gr = (gain * re_ref[...]).astype(BF16)
    gi = (gain * im_ref[...]).astype(BF16)
    er, fr = gr[:half, :half], gr[:half, half:]
    ei, fi = gi[:half, :half], gi[:half, half:]
    start = lax.broadcasted_iota(jnp.int32, (half, half), 0) == 0
    nyquist_u = gr[half : half + 1, :half]
    nyquist_v = jnp.where(edge8[:1], gr[half : half + 1, half:], gi[half : half + 1, :half])
    zero = jnp.zeros((), BF16)
    near_u = jnp.concatenate([er, jnp.where(start, nyquist_u, -ei)], axis=0)
    far_u = jnp.concatenate(
        [jnp.where(edge, er, fr), -jnp.where(edge, ei, fi)], axis=0
    )
    near_v = jnp.concatenate(
        [jnp.where(edge, fr, ei), jnp.where(start, nyquist_v, jnp.where(edge, -fi, er))], axis=0
    )
    far_v = jnp.concatenate(
        [jnp.where(edge, fr, -fi), -jnp.where(edge, fi, fr)], axis=0
    )
    start = lax.broadcasted_iota(jnp.int32, (length, half), 0) % half == 0
    far_u, far_v = jnp.where(start, zero, far_u), jnp.where(start, zero, far_v)
    u = dot(right_ref[...], near_u) + dot(right_ref[...], far_u)
    v = dot(right_ref[...], near_v) + dot(right_ref[...], far_v)
    joined = jnp.concatenate([u.astype(BF16), v.astype(BF16)], axis=1)
    real_part = dot(joined, inverse_right_ref[...])
    norm = 1.0 / (length * length)
    pc = cols_ref[:1, :]
    inside_ref[...] = rows_ref[margin : margin + half, :1] * pc * real_part[:half] * norm
    strips[:margin] = (rows_ref[:margin, :1] * pc * real_part[half : half + margin] * norm).astype(BF16)
    strips[margin:] = (rows_ref[margin + half :, :1] * pc * real_part[half + margin :] * norm).astype(BF16)
    place = pl.multiple_of(jnp.where(first == 0, 0, margin), margin)
    first_out_ref[...] = strips[pl.ds(place, margin), :]
    second_out_ref[...] = strips[pl.ds(pl.multiple_of(margin - place, margin), margin), :]


def fold_rows_kernel(half, inside_ref, first_ref, second_ref, center_ref, outer_ref, inner_ref, total):
    margin = half // 2
    first, second, outer, inner = sides(half)
    for source, place in ((first_ref, first), (second_ref, second)):
        rows = pl.ds(pl.multiple_of(jnp.where(place == 0, 0, margin), margin), margin)
        total[rows, :] = inside_ref[rows, :] + source[...].astype(F32)
    center_ref[...] = total[:, margin : margin + half]
    outer_ref[...] = total[:, pl.ds(pl.multiple_of(outer, margin), margin)].astype(BF16)
    inner_ref[...] = total[:, pl.ds(pl.multiple_of(inner, margin), margin)].astype(BF16)


def fold_columns_kernel(half, center_ref, outer_ref, inner_ref, out_ref):
    margin = half // 2
    _, _, outer, inner = sides(half)
    for source, place in ((outer_ref, outer), (inner_ref, inner)):
        columns = pl.ds(pl.multiple_of(jnp.where(place == 0, 0, margin), margin), margin)
        out_ref[:, columns] = center_ref[:, columns] + source[...].astype(F32)


def swap(values, axis, offset):
    count = lax.axis_size(axis)
    pairs = [(i, i + 1) for i in range(offset, count - 1, 2)]
    return lax.ppermute(values, axis, pairs + [(b, a) for a, b in pairs])


def whole(count):
    return [pl.BlockSpec(memory_space=pltpu.VMEM)] * count


def kernel_call(body, name, outs, count, scratch=(), flops=0, vmem=24):
    return pl.pallas_call(
        body,
        out_shape=outs,
        in_specs=whole(count),
        out_specs=jax.tree.map(lambda _: pl.BlockSpec(memory_space=pltpu.VMEM), outs),
        scratch_shapes=list(scratch),
        cost_estimate=pl.CostEstimate(flops=flops, bytes_accessed=1 << 20, transcendentals=0),
        compiler_params=pltpu.CompilerParams(vmem_limit_bytes=vmem << 20),
        name=name,
    )


def shards(tables, split_maps, white_noise):
    splits, core_side, _ = split_maps.shape
    half = core_side
    margin = core_side // 2
    length = 2 * core_side
    constant = {k: jnp.asarray(v) for k, v in tables.items() if k != "energy"}
    profile = tables["profile"]
    rows = jnp.asarray(np.ascontiguousarray(np.broadcast_to(profile[:, None], (length, 128))))
    cols = jnp.asarray(np.ascontiguousarray(np.broadcast_to(profile[None, :], (8, length))))
    scale = 1.0 / ((2 * SMOOTH + 1) ** 2 * (splits - 1) * tables["energy"])
    odd_row = lax.axis_index("dec") % 2
    odd_col = lax.axis_index("ra") % 2
    cube = length**3

    outer_columns = lax.dynamic_slice_in_dim(split_maps, odd_col * margin, margin, axis=2)
    first_rows = lax.dynamic_slice_in_dim(split_maps, (1 - odd_row) * margin, margin, axis=1)
    second_rows = lax.dynamic_slice_in_dim(split_maps, odd_row * margin, margin, axis=1)
    outer = swap(outer_columns, "ra", 1)
    first = swap(first_rows, "dec", 0)
    second = swap(second_rows, "dec", 1)

    spectrum = jax.ShapeDtypeStruct((half + 8, length), F32)
    re, im = kernel_call(
        functools.partial(noise_kernel, half), "noise_spectrum", (spectrum, spectrum), 3, flops=3 * cube
    )(white_noise, constant["left"], constant["right"])

    outer, first, second, re, im = lax.optimization_barrier((outer, first, second, re, im))

    first_corner = swap(lax.dynamic_slice_in_dim(outer, (1 - odd_row) * margin, margin, axis=1), "dec", 0)
    second_corner = swap(lax.dynamic_slice_in_dim(outer, odd_row * margin, margin, axis=1), "dec", 1)
    inner = swap(
        jnp.concatenate(
            [
                lax.dynamic_slice_in_dim(block, (1 - odd_col) * margin, margin, axis=2)
                for block in (first, split_maps, second)
            ],
            axis=1,
        ),
        "ra",
        0,
    )
    halves = kernel_call(
        functools.partial(core_kernel, half),
        "core_columns",
        jax.ShapeDtypeStruct((splits, length + 16, half), BF16),
        6,
        [pltpu.VMEM((splits, length, half), BF16)],
        flops=6 * cube,
    )(split_maps, first, second, rows, cols, constant["left"])

    strip = jax.ShapeDtypeStruct((margin, length), BF16)
    first, second, inside = kernel_call(
        functools.partial(main_kernel, half, scale),
        "tile_model",
        (strip, strip, jax.ShapeDtypeStruct((half, length), F32)),
        14,
        [
            pltpu.VMEM((splits, length, half), BF16),
            pltpu.VMEM((half + 8, length), F32),
            pltpu.VMEM((3, half + 128, length), BF16),
            pltpu.VMEM((half, length), BF16),
        ],
        flops=20 * cube,
    )(
        halves, outer, first_corner, second_corner, inner, re, im, rows, cols,
        constant["left"], constant["right"], constant["band_rows"], constant["band_columns"],
        constant["inverse_right"],
    )

    first = swap(first, "dec", 0)
    second = swap(second, "dec", 1)
    column = jax.ShapeDtypeStruct((half, margin), BF16)
    block = jax.ShapeDtypeStruct((half, half), F32)
    center, outer, inner = kernel_call(
        functools.partial(fold_rows_kernel, half), "fold_rows", (block, column, column), 3,
        [pltpu.VMEM((half, length), F32)],
    )(inside, first, second)
    outer = swap(outer, "ra", 1)
    inner = swap(inner, "ra", 0)
    return kernel_call(functools.partial(fold_columns_kernel, half), "fold_columns", block, 3)(
        center, outer, inner
    )


def solution(mesh):
    tables = host_tables(512)
    placed = (P(None, "dec", "ra"), P("dec", "ra"))
    return jax.shard_map(
        functools.partial(shards, tables), mesh=mesh, in_specs=placed, out_specs=P("dec", "ra"), check_vma=False
    )
```

```python
import functools

import jax
import jax.numpy as jnp
import numpy as np
from jax import lax
from jax.experimental import pallas as pl
from jax.experimental.pallas import tpu as pltpu
from jax.sharding import PartitionSpec as P

import ml_dtypes

SMOOTH = 4
BF16 = jnp.bfloat16
F32 = jnp.float32


def host_tables(length):
    half = length // 2
    index = np.arange(length)
    phase = np.outer(index, index) % length
    cos = np.cos(2 * np.pi * phase / length)
    sin = np.sin(2 * np.pi * phase / length)
    sin[phase % half == 0] = 0.0
    cos = cos.astype(ml_dtypes.bfloat16).astype(np.float64)
    sin = sin.astype(ml_dtypes.bfloat16).astype(np.float64)

    def packed(rows):
        return np.ascontiguousarray(rows).astype(ml_dtypes.bfloat16)

    left = np.zeros((length + 16, length))
    left[:half] = cos[:half]
    left[half:length] = sin[:half]
    left[length] = cos[half]
    right = np.concatenate([cos[:, :half], sin[:, :half]], axis=1)
    right[:, half] = cos[:, half]
    margin = half // 2
    right = np.roll(right, -margin, axis=0)
    right = np.concatenate([right[:half], np.roll(right[half:], margin, axis=0)], axis=0)
    inverse_right = np.concatenate([2 * cos[:half], -2 * sin[:half]], axis=0)
    inverse_right[0] = cos[0]
    inverse_right[half] = cos[half]
    order = np.concatenate([index[:half], [half], -index[1:half]])

    def near(first, second):
        apart = np.abs(first[:, None] - second[None, :]) % length
        return (np.minimum(apart, length - apart) <= SMOOTH).astype(np.float64)

    band_columns = near(order, order)
    band_rows = np.zeros((half + 16, half + 128))
    targets = np.arange(half + 1)
    band_rows[: half + 1, : half + 1] = near(targets, targets)
    first, last = half + 8, half + 16
    band_rows[: half + 1, first + 1 : first + 8] = near(targets, -np.arange(1, 8))
    band_rows[: half + 1, last : last + 8] = near(targets, -np.arange(half - 8, half))
    profile = np.sin(np.pi * (index + 0.5) / length) ** 2
    energy = np.sum(profile**2) ** 2
    return dict(
        left=packed(left),
        right=packed(right),
        inverse_right=packed(inverse_right),
        band_columns=packed(band_columns),
        band_rows=packed(band_rows),
        profile=profile.astype(np.float32),
        energy=float(energy),
    )


def dot(a, b):
    return jnp.dot(a, b, preferred_element_type=F32)


def first_column(shape):
    return lax.broadcasted_iota(jnp.int32, shape, 1) == 0


def three_parts(values):
    high = values.astype(BF16)
    rest = values - high.astype(F32)
    middle = rest.astype(BF16)
    low = (rest - middle.astype(F32)).astype(BF16)
    return high, middle, low


def quarters(spectra, half):
    length = 2 * half
    return (
        spectra[:half, :half],
        spectra[:half, half:],
        spectra[half:length, :half],
        spectra[half:length, half:],
        spectra[length : length + 8, :half],
        spectra[length : length + 8, half:],
    )


def noise_kernel(half, noise_ref, left_ref, right_ref, re_ref, im_ref):
    margin = half // 2
    halves = dot(left_ref[...], noise_ref[...]).astype(BF16)
    spectra = (
        dot(halves[:, margin : margin + half], right_ref[:half])
        + dot(halves[:, :margin], right_ref[half : half + margin])
        + dot(halves[:, margin + half :], right_ref[half + margin :])
    )
    cc, cs, sc, ss, nc, ns = quarters(spectra, half)
    edge = first_column((half, half))
    re_ref[:half, :half] = jnp.where(edge, cc, cc - ss)
    re_ref[:half, half:] = jnp.where(edge, cs, cc + ss)
    im_ref[:half, :half] = -jnp.where(edge, sc, cs + sc)
    im_ref[:half, half:] = jnp.where(edge, -ss, cs - sc)
    edge = first_column((8, half))
    re_ref[half : half + 8, :half] = nc
    re_ref[half : half + 8, half:] = jnp.where(edge, ns, nc)
    im_ref[half : half + 8, :half] = jnp.where(edge, 0.0, -ns)
    im_ref[half : half + 8, half:] = jnp.where(edge, 0.0, ns)


def aligned(offset, step):
    return offset if isinstance(offset, int) else pl.multiple_of(offset, step)


def fill(tile, source, rows_ref, cols_ref, source_row, height, row, col, tile_col):
    splits, width = source.shape[0], source.shape[2]
    step = 32
    pc = cols_ref[:1, pl.ds(aligned(col, 128), width)]

    def strip(number, carry):
        start = pl.multiple_of(source_row + number * step, step)
        target = pl.multiple_of(row + number * step, step)
        members = [source[s, pl.ds(start, step), :].astype(F32) for s in range(splits)]
        mean = functools.reduce(lambda a, b: a + b, members) * (1.0 / splits)
        weights = rows_ref[pl.ds(target, step), :1] * pc
        for s in range(splits):
            tile[s, pl.ds(target, step), pl.ds(aligned(tile_col, 128), width)] = (
                weights * (members[s] - mean)
            ).astype(BF16)
        return carry

    lax.fori_loop(0, height // step, strip, 0)


def sides(half):
    far = half + half // 2
    first = jnp.where(lax.axis_index("dec") % 2 == 0, far, 0)
    outer = jnp.where(lax.axis_index("ra") % 2 == 0, 0, far)
    return first, far - first, outer, far - outer


def core_kernel(half, core_ref, first_ref, second_ref, rows_ref, cols_ref, left_ref, halves_ref, tile):
    margin = half // 2
    splits = core_ref.shape[0]
    first, second, _, _ = sides(half)
    fill(tile, core_ref, rows_ref, cols_ref, 0, half, margin, margin, 0)
    fill(tile, first_ref, rows_ref, cols_ref, 0, margin, first, margin, 0)
    fill(tile, second_ref, rows_ref, cols_ref, 0, margin, second, margin, 0)

    for s in range(splits):
        halves_ref[s] = dot(left_ref[...], tile[s]).astype(BF16)


def inner_kernel(half, after_ref, inner_ref, rows_ref, cols_ref, left_ref, halves_ref, tile):
    del after_ref
    margin = half // 2
    first, second, _, inner = sides(half)
    fill(tile, inner_ref, rows_ref, cols_ref, 0, margin, first, inner, 0)
    fill(tile, inner_ref, rows_ref, cols_ref, margin, half, margin, inner, 0)
    fill(tile, inner_ref, rows_ref, cols_ref, margin + half, margin, second, inner, 0)
    for s in range(inner_ref.shape[0]):
        halves_ref[s] = dot(left_ref[...], tile[s]).astype(BF16)


def outer_kernel(half, after_ref, outer_ref, first_ref, second_ref, rows_ref, cols_ref, left_ref, halves_ref, tile):
    del after_ref
    margin = half // 2
    first, second, outer, _ = sides(half)
    fill(tile, outer_ref, rows_ref, cols_ref, 0, half, margin, outer, 0)
    fill(tile, first_ref, rows_ref, cols_ref, 0, margin, first, outer, 0)
    fill(tile, second_ref, rows_ref, cols_ref, 0, margin, second, outer, 0)
    for s in range(outer_ref.shape[0]):
        halves_ref[s] = dot(left_ref[...], tile[s]).astype(BF16)


def main_kernel(
    half, scale,
    core_ref, inner_ref, outer_ref, re_ref, im_ref,
    rows_ref, cols_ref, right_ref, band_rows_ref, band_columns_ref,
    inverse_right_ref,
    first_out_ref, second_out_ref, inside_ref,
    table, power, stacked, strips,
):
    length = 2 * half
    margin = half // 2
    splits = core_ref.shape[0]
    first, _, _, inner = sides(half)
    place = pl.multiple_of(half + jnp.where(inner == 0, 0, margin), margin)
    table[:margin] = right_ref[pl.ds(place, margin), :]
    table[margin:] = right_ref[pl.ds(pl.multiple_of(length + margin - place, margin), margin), :]

    edge = first_column((half, half))
    edge8 = first_column((8, half))

    def accumulate(s, carry):
        halves = jnp.concatenate([inner_ref[s], outer_ref[s]], axis=1)
        spectra = dot(core_ref[s], right_ref[:half]) + dot(halves, table[...])
        cc, cs, sc, ss, nc, ns = quarters(spectra, half)
        e = jnp.where(edge, cc, cc - ss)
        f = jnp.where(edge, sc, cs + sc)
        g = jnp.where(edge, cs, cc + ss)
        h = jnp.where(edge, ss, cs - sc)
        nc, ns = nc * nc, ns * ns
        terms = (
            e * e + f * f, g * g + h * h, jnp.where(edge8, nc, nc + ns), jnp.where(edge8, ns, nc + ns)
        )
        places = (
            (slice(0, half), slice(0, half)), (slice(0, half), slice(half, length)),
            (slice(half, half + 8), slice(0, half)), (slice(half, half + 8), slice(half, length)),
        )
        for term, place in zip(terms, places):
            power[place] = term if carry else power[place] + term

    accumulate(0, True)
    for s in range(1, splits):
        accumulate(s, False)

    stacked[:, half + 24 :, :] = jnp.zeros((3, stacked.shape[1] - half - 24, length), BF16)
    for part, values in enumerate(three_parts(power[...])):
        stacked[part, : half + 8, :] = values
    for place, start in ((half + 8, 0), (half + 16, half - 8)):
        a = power[start : start + 8, :half]
        b = power[start : start + 8, half:]
        mirrored = jnp.concatenate(
            [jnp.where(edge8, a, b), jnp.where(edge8, b, a)], axis=1
        )
        for part, values in enumerate(three_parts(mirrored)):
            stacked[part, place : place + 8, :] = values
    smooth = (
        dot(band_rows_ref[...], stacked[2])
        + dot(band_rows_ref[...], stacked[1])
        + dot(band_rows_ref[...], stacked[0])
    )
    high, middle, low = three_parts(smooth)
    smooth = (
        dot(low, band_columns_ref[...])
        + dot(middle, band_columns_ref[...])
        + dot(high, band_columns_ref[...])
    )
    gain = jnp.sqrt(jnp.maximum(smooth[: half + 8], 0.0) * scale)
    gr = (gain * re_ref[...]).astype(BF16)
    gi = (gain * im_ref[...]).astype(BF16)
    er, fr = gr[:half, :half], gr[:half, half:]
    ei, fi = gi[:half, :half], gi[:half, half:]
    start = lax.broadcasted_iota(jnp.int32, (half, half), 0) == 0
    nyquist_u = gr[half : half + 1, :half]
    nyquist_v = jnp.where(edge8[:1], gr[half : half + 1, half:], gi[half : half + 1, :half])
    zero = jnp.zeros((), BF16)
    near_u = jnp.concatenate([er, jnp.where(start, nyquist_u, -ei)], axis=0)
    far_u = jnp.concatenate(
        [jnp.where(edge, er, fr), -jnp.where(edge, ei, fi)], axis=0
    )
    near_v = jnp.concatenate(
        [jnp.where(edge, fr, ei), jnp.where(start, nyquist_v, jnp.where(edge, -fi, er))], axis=0
    )
    far_v = jnp.concatenate(
        [jnp.where(edge, fr, -fi), -jnp.where(edge, fi, fr)], axis=0
    )
    start = lax.broadcasted_iota(jnp.int32, (length, half), 0) % half == 0
    far_u, far_v = jnp.where(start, zero, far_u), jnp.where(start, zero, far_v)
    u = dot(right_ref[...], near_u) + dot(right_ref[...], far_u)
    v = dot(right_ref[...], near_v) + dot(right_ref[...], far_v)
    joined = jnp.concatenate([u.astype(BF16), v.astype(BF16)], axis=1)
    real_part = dot(joined, inverse_right_ref[...])
    norm = 1.0 / (length * length)
    pc = cols_ref[:1, :]
    inside_ref[...] = rows_ref[margin : margin + half, :1] * pc * real_part[:half] * norm
    strips[:margin] = (rows_ref[:margin, :1] * pc * real_part[half : half + margin] * norm).astype(BF16)
    strips[margin:] = (rows_ref[margin + half :, :1] * pc * real_part[half + margin :] * norm).astype(BF16)
    place = pl.multiple_of(jnp.where(first == 0, 0, margin), margin)
    first_out_ref[...] = strips[pl.ds(place, margin), :]
    second_out_ref[...] = strips[pl.ds(pl.multiple_of(margin - place, margin), margin), :]


def fold_rows_kernel(half, inside_ref, first_ref, second_ref, center_ref, outer_ref, inner_ref, total):
    margin = half // 2
    first, second, outer, inner = sides(half)
    for source, place in ((first_ref, first), (second_ref, second)):
        rows = pl.ds(pl.multiple_of(jnp.where(place == 0, 0, margin), margin), margin)
        total[rows, :] = inside_ref[rows, :] + source[...].astype(F32)
    center_ref[...] = total[:, margin : margin + half]
    outer_ref[...] = total[:, pl.ds(pl.multiple_of(outer, margin), margin)].astype(BF16)
    inner_ref[...] = total[:, pl.ds(pl.multiple_of(inner, margin), margin)].astype(BF16)


def fold_columns_kernel(half, center_ref, outer_ref, inner_ref, out_ref):
    margin = half // 2
    _, _, outer, inner = sides(half)
    for source, place in ((outer_ref, outer), (inner_ref, inner)):
        columns = pl.ds(pl.multiple_of(jnp.where(place == 0, 0, margin), margin), margin)
        out_ref[:, columns] = center_ref[:, columns] + source[...].astype(F32)


def swap(values, axis, offset):
    count = lax.axis_size(axis)
    pairs = [(i, i + 1) for i in range(offset, count - 1, 2)]
    return lax.ppermute(values, axis, pairs + [(b, a) for a, b in pairs])


def whole(count):
    return [pl.BlockSpec(memory_space=pltpu.VMEM)] * count


def kernel_call(body, name, outs, count, scratch=(), flops=0, vmem=24):
    return pl.pallas_call(
        body,
        out_shape=outs,
        in_specs=whole(count),
        out_specs=jax.tree.map(lambda _: pl.BlockSpec(memory_space=pltpu.VMEM), outs),
        scratch_shapes=list(scratch),
        cost_estimate=pl.CostEstimate(flops=flops, bytes_accessed=1 << 20, transcendentals=0),
        compiler_params=pltpu.CompilerParams(vmem_limit_bytes=vmem << 20),
        name=name,
    )


def shards(tables, split_maps, white_noise):
    splits, core_side, _ = split_maps.shape
    half = core_side
    margin = core_side // 2
    length = 2 * core_side
    constant = {k: jnp.asarray(v) for k, v in tables.items() if k != "energy"}
    profile = tables["profile"]
    rows = jnp.asarray(np.ascontiguousarray(np.broadcast_to(profile[:, None], (length, 128))))
    cols = jnp.asarray(np.ascontiguousarray(np.broadcast_to(profile[None, :], (8, length))))
    scale = 1.0 / ((2 * SMOOTH + 1) ** 2 * (splits - 1) * tables["energy"])
    odd_row = lax.axis_index("dec") % 2
    odd_col = lax.axis_index("ra") % 2
    cube = length**3

    outer_columns = lax.dynamic_slice_in_dim(split_maps, odd_col * margin, margin, axis=2)
    first_rows = lax.dynamic_slice_in_dim(split_maps, (1 - odd_row) * margin, margin, axis=1)
    second_rows = lax.dynamic_slice_in_dim(split_maps, odd_row * margin, margin, axis=1)
    outer = swap(outer_columns, "ra", 1)
    first = swap(first_rows, "dec", 0)
    second = swap(second_rows, "dec", 1)

    spectrum = jax.ShapeDtypeStruct((half + 8, length), F32)
    re, im = kernel_call(
        functools.partial(noise_kernel, half), "noise_spectrum", (spectrum, spectrum), 3, flops=3 * cube
    )(white_noise, constant["left"], constant["right"])

    outer, re, im = lax.optimization_barrier((outer, re, im))
    first_corner = lax.dynamic_slice_in_dim(outer, (1 - odd_row) * margin, margin, axis=1)
    second_corner = lax.dynamic_slice_in_dim(outer, odd_row * margin, margin, axis=1)
    first, second, _, _ = lax.optimization_barrier((first, second, first_corner, second_corner))
    first_corner = swap(first_corner, "dec", 0)
    second_corner = swap(second_corner, "dec", 1)
    inner = swap(
        jnp.concatenate(
            [
                lax.dynamic_slice_in_dim(block, (1 - odd_col) * margin, margin, axis=2)
                for block in (first, split_maps, second)
            ],
            axis=1,
        ),
        "ra",
        0,
    )
    def columns(body, name, width, count, flops):
        return kernel_call(
            functools.partial(body, half),
            name,
            jax.ShapeDtypeStruct((splits, length + 16, width), BF16),
            count,
            [pltpu.VMEM((splits, length, width), BF16)],
            flops=flops,
        )

    left = constant["left"]
    core = columns(core_kernel, "core_columns", half, 6, cube)(split_maps, first, second, rows, cols, left)
    outer = columns(outer_kernel, "outer_columns", margin, 7, 400000 * cube // 1000)(
        core, outer, first_corner, second_corner, rows, cols, left
    )
    inner = columns(inner_kernel, "inner_columns", margin, 5, cube)(outer, inner, rows, cols, left)

    strip = jax.ShapeDtypeStruct((margin, length), BF16)
    first, second, inside = kernel_call(
        functools.partial(main_kernel, half, scale),
        "tile_model",
        (strip, strip, jax.ShapeDtypeStruct((half, length), F32)),
        11,
        [
            pltpu.VMEM((half, length), BF16),
            pltpu.VMEM((half + 8, length), F32),
            pltpu.VMEM((3, half + 128, length), BF16),
            pltpu.VMEM((half, length), BF16),
        ],
        flops=20 * cube,
    )(
        core, inner, outer, re, im, rows, cols,
        constant["right"], constant["band_rows"], constant["band_columns"],
        constant["inverse_right"],
    )

    first = swap(first, "dec", 0)
    second = swap(second, "dec", 1)
    column = jax.ShapeDtypeStruct((half, margin), BF16)
    block = jax.ShapeDtypeStruct((half, half), F32)
    center, outer, inner = kernel_call(
        functools.partial(fold_rows_kernel, half), "fold_rows", (block, column, column), 3,
        [pltpu.VMEM((half, length), F32)],
    )(inside, first, second)
    outer = swap(outer, "ra", 1)
    inner = swap(inner, "ra", 0)
    return kernel_call(functools.partial(fold_columns_kernel, half), "fold_columns", block, 3)(
        center, outer, inner
    )


def solution(mesh):
    tables = host_tables(512)
    placed = (P(None, "dec", "ra"), P("dec", "ra"))
    return jax.shard_map(
        functools.partial(shards, tables), mesh=mesh, in_specs=placed, out_specs=P("dec", "ra"), check_vma=False
    )
```

```python
import functools

import jax
import jax.numpy as jnp
import numpy as np
from jax import lax
from jax.experimental import pallas as pl
from jax.experimental.pallas import tpu as pltpu
from jax.sharding import PartitionSpec as P

import ml_dtypes

SMOOTH = 4
BF16 = jnp.bfloat16
F32 = jnp.float32


def host_tables(length):
    half = length // 2
    index = np.arange(length)
    phase = np.outer(index, index) % length
    cos = np.cos(2 * np.pi * phase / length)
    sin = np.sin(2 * np.pi * phase / length)
    sin[phase % half == 0] = 0.0
    cos = cos.astype(ml_dtypes.bfloat16).astype(np.float64)
    sin = sin.astype(ml_dtypes.bfloat16).astype(np.float64)

    def packed(rows):
        return np.ascontiguousarray(rows).astype(ml_dtypes.bfloat16)

    left = np.zeros((length + 16, length))
    left[:half] = cos[:half]
    left[half:length] = sin[:half]
    left[length] = cos[half]
    right = np.concatenate([cos[:, :half], sin[:, :half]], axis=1)
    right[:, half] = cos[:, half]
    margin = half // 2
    right = np.roll(right, -margin, axis=0)
    right = np.concatenate([right[:half], np.roll(right[half:], margin, axis=0)], axis=0)
    inverse_right = np.concatenate([2 * cos[:half], -2 * sin[:half]], axis=0)
    inverse_right[0] = cos[0]
    inverse_right[half] = cos[half]
    order = np.concatenate([index[:half], [half], -index[1:half]])

    def near(first, second):
        apart = np.abs(first[:, None] - second[None, :]) % length
        return (np.minimum(apart, length - apart) <= SMOOTH).astype(np.float64)

    band_columns = near(order, order)
    band_rows = np.zeros((half + 16, half + 128))
    targets = np.arange(half + 1)
    band_rows[: half + 1, : half + 1] = near(targets, targets)
    first, last = half + 8, half + 16
    band_rows[: half + 1, first + 1 : first + 8] = near(targets, -np.arange(1, 8))
    band_rows[: half + 1, last : last + 8] = near(targets, -np.arange(half - 8, half))
    profile = np.sin(np.pi * (index + 0.5) / length) ** 2
    energy = np.sum(profile**2) ** 2
    return dict(
        left=packed(left),
        right=packed(right),
        inverse_right=packed(inverse_right),
        band_columns=packed(band_columns),
        band_rows=packed(band_rows),
        profile=profile.astype(np.float32),
        energy=float(energy),
    )


def dot(a, b):
    return jnp.dot(a, b, preferred_element_type=F32)


def first_column(shape):
    return lax.broadcasted_iota(jnp.int32, shape, 1) == 0


def two_parts(values):
    high = values.astype(BF16)
    return high, (values - high.astype(F32)).astype(BF16)


def quarters(spectra, half):
    length = 2 * half
    return (
        spectra[:half, :half],
        spectra[:half, half:],
        spectra[half:length, :half],
        spectra[half:length, half:],
        spectra[length : length + 8, :half],
        spectra[length : length + 8, half:],
    )


def noise_kernel(half, noise_ref, left_ref, right_ref, re_ref, im_ref):
    margin = half // 2
    halves = dot(left_ref[...], noise_ref[...]).astype(BF16)
    spectra = (
        dot(halves[:, margin : margin + half], right_ref[:half])
        + dot(halves[:, :margin], right_ref[half : half + margin])
        + dot(halves[:, margin + half :], right_ref[half + margin :])
    )
    cc, cs, sc, ss, nc, ns = quarters(spectra, half)
    edge = first_column((half, half))
    re_ref[:half, :half] = jnp.where(edge, cc, cc - ss)
    re_ref[:half, half:] = jnp.where(edge, cs, cc + ss)
    im_ref[:half, :half] = -jnp.where(edge, sc, cs + sc)
    im_ref[:half, half:] = jnp.where(edge, -ss, cs - sc)
    edge = first_column((8, half))
    re_ref[half : half + 8, :half] = nc
    re_ref[half : half + 8, half:] = jnp.where(edge, ns, nc)
    im_ref[half : half + 8, :half] = jnp.where(edge, 0.0, -ns)
    im_ref[half : half + 8, half:] = jnp.where(edge, 0.0, ns)


def aligned(offset, step):
    return offset if isinstance(offset, int) else pl.multiple_of(offset, step)


def fill(tile, source, rows_ref, cols_ref, source_row, height, row, col, tile_col):
    splits, width = source.shape[0], source.shape[2]
    step = 32
    pc = cols_ref[:1, pl.ds(aligned(col, 128), width)]

    def strip(number, carry):
        start = pl.multiple_of(source_row + number * step, step)
        target = pl.multiple_of(row + number * step, step)
        members = [source[s, pl.ds(start, step), :].astype(F32) for s in range(splits)]
        mean = functools.reduce(lambda a, b: a + b, members) * (1.0 / splits)
        weights = jnp.concatenate([rows_ref[pl.ds(target, step), :]] * (width // 128), axis=1) * pc
        for s in range(splits):
            tile[s, pl.ds(target, step), pl.ds(aligned(tile_col, 128), width)] = (
                weights * (members[s] - mean)
            ).astype(BF16)
        return carry

    lax.fori_loop(0, height // step, strip, 0)


def sides(half):
    far = half + half // 2
    first = jnp.where(lax.axis_index("dec") % 2 == 0, far, 0)
    outer = jnp.where(lax.axis_index("ra") % 2 == 0, 0, far)
    return first, far - first, outer, far - outer


def core_kernel(half, core_ref, first_ref, second_ref, rows_ref, cols_ref, left_ref, right_ref, spectra_ref, tile):
    margin = half // 2
    splits = core_ref.shape[0]
    first, second, _, _ = sides(half)
    fill(tile, core_ref, rows_ref, cols_ref, 0, half, margin, margin, 0)
    fill(tile, first_ref, rows_ref, cols_ref, 0, margin, first, margin, 0)
    fill(tile, second_ref, rows_ref, cols_ref, 0, margin, second, margin, 0)

    for s in range(splits):
        halves = dot(left_ref[...], tile[s]).astype(BF16)
        spectra_ref[s] = dot(halves, right_ref[:half])


def transform_pairs(tile, left_ref, halves_ref):
    splits, _, width = tile.shape
    for s in range(0, splits, 2):
        halves = dot(left_ref[...], jnp.concatenate([tile[s], tile[s + 1]], axis=1)).astype(BF16)
        halves_ref[s] = halves[:, :width]
        halves_ref[s + 1] = halves[:, width:]


def inner_kernel(half, after_ref, inner_ref, rows_ref, cols_ref, left_ref, halves_ref, tile):
    del after_ref
    margin = half // 2
    first, second, _, inner = sides(half)
    fill(tile, inner_ref, rows_ref, cols_ref, 0, margin, first, inner, 0)
    fill(tile, inner_ref, rows_ref, cols_ref, margin, half, margin, inner, 0)
    fill(tile, inner_ref, rows_ref, cols_ref, margin + half, margin, second, inner, 0)
    transform_pairs(tile, left_ref, halves_ref)


def outer_kernel(half, after_ref, outer_ref, first_ref, second_ref, rows_ref, cols_ref, left_ref, halves_ref, tile):
    del after_ref
    margin = half // 2
    first, second, outer, _ = sides(half)
    fill(tile, outer_ref, rows_ref, cols_ref, 0, half, margin, outer, 0)
    fill(tile, first_ref, rows_ref, cols_ref, 0, margin, first, outer, 0)
    fill(tile, second_ref, rows_ref, cols_ref, 0, margin, second, outer, 0)
    transform_pairs(tile, left_ref, halves_ref)


def main_kernel(
    half, scale,
    core_ref, inner_ref, outer_ref, re_ref, im_ref,
    rows_ref, cols_ref, right_ref, band_rows_ref, band_columns_ref,
    inverse_right_ref,
    first_out_ref, second_out_ref, inside_ref,
    table, power, stacked, strips,
):
    length = 2 * half
    margin = half // 2
    splits = core_ref.shape[0]
    first, _, _, inner = sides(half)
    place = pl.multiple_of(half + jnp.where(inner == 0, 0, margin), margin)
    table[:margin] = right_ref[pl.ds(place, margin), :]
    table[margin:] = right_ref[pl.ds(pl.multiple_of(length + margin - place, margin), margin), :]

    edge = first_column((half, half))
    edge8 = first_column((8, half))

    def accumulate(s, carry):
        halves = jnp.concatenate([inner_ref[s], outer_ref[s]], axis=1)
        spectra = core_ref[s] + dot(halves, table[...])
        cc, cs, sc, ss, nc, ns = quarters(spectra, half)
        e = jnp.where(edge, cc, cc - ss)
        f = jnp.where(edge, sc, cs + sc)
        g = jnp.where(edge, cs, cc + ss)
        h = jnp.where(edge, ss, cs - sc)
        nc, ns = nc * nc, ns * ns
        terms = (
            e * e + f * f, g * g + h * h, jnp.where(edge8, nc, nc + ns), jnp.where(edge8, ns, nc + ns)
        )
        places = (
            (slice(0, half), slice(0, half)), (slice(0, half), slice(half, length)),
            (slice(half, half + 8), slice(0, half)), (slice(half, half + 8), slice(half, length)),
        )
        for term, place in zip(terms, places):
            power[place] = term if carry else power[place] + term

    accumulate(0, True)
    for s in range(1, splits):
        accumulate(s, False)

    stacked[:, half + 24 :, :] = jnp.zeros((2, stacked.shape[1] - half - 24, length), BF16)
    for part, values in enumerate(two_parts(power[...])):
        stacked[part, : half + 8, :] = values
    for place, start in ((half + 8, 0), (half + 16, half - 8)):
        a = power[start : start + 8, :half]
        b = power[start : start + 8, half:]
        mirrored = jnp.concatenate(
            [jnp.where(edge8, a, b), jnp.where(edge8, b, a)], axis=1
        )
        for part, values in enumerate(two_parts(mirrored)):
            stacked[part, place : place + 8, :] = values
    smooth = (
        dot(band_rows_ref[...], stacked[1]) + dot(band_rows_ref[...], stacked[0])
    )
    high, low = two_parts(smooth)
    smooth = dot(low, band_columns_ref[...]) + dot(high, band_columns_ref[...])
    gain = jnp.sqrt(jnp.maximum(smooth[: half + 8], 0.0) * scale)
    gr = (gain * re_ref[...]).astype(BF16)
    gi = (gain * im_ref[...]).astype(BF16)
    er, fr = gr[:half, :half], gr[:half, half:]
    ei, fi = gi[:half, :half], gi[:half, half:]
    start = lax.broadcasted_iota(jnp.int32, (half, half), 0) == 0
    nyquist_u = gr[half : half + 1, :half]
    nyquist_v = jnp.where(edge8[:1], gr[half : half + 1, half:], gi[half : half + 1, :half])
    zero = jnp.zeros((), BF16)
    near_u = jnp.concatenate([er, jnp.where(start, nyquist_u, -ei)], axis=0)
    far_u = jnp.concatenate(
        [jnp.where(edge, er, fr), -jnp.where(edge, ei, fi)], axis=0
    )
    near_v = jnp.concatenate(
        [jnp.where(edge, fr, ei), jnp.where(start, nyquist_v, jnp.where(edge, -fi, er))], axis=0
    )
    far_v = jnp.concatenate(
        [jnp.where(edge, fr, -fi), -jnp.where(edge, fi, fr)], axis=0
    )
    start = lax.broadcasted_iota(jnp.int32, (length, half), 0) % half == 0
    far_u, far_v = jnp.where(start, zero, far_u), jnp.where(start, zero, far_v)
    u = dot(right_ref[...], near_u) + dot(right_ref[...], far_u)
    v = dot(right_ref[...], near_v) + dot(right_ref[...], far_v)
    joined = jnp.concatenate([u.astype(BF16), v.astype(BF16)], axis=1)
    real_part = dot(joined, inverse_right_ref[...])
    pc = cols_ref[:1, :] * (1.0 / (length * length))

    def windowed(row, place, count):
        profile = jnp.concatenate([rows_ref[row : row + count, :]] * (length // 128), axis=1)
        return profile * pc * real_part[place : place + count]

    inside_ref[...] = windowed(margin, 0, half)
    strips[:margin] = windowed(0, half, margin).astype(BF16)
    strips[margin:] = windowed(margin + half, half + margin, margin).astype(BF16)
    place = pl.multiple_of(jnp.where(first == 0, 0, margin), margin)
    first_out_ref[...] = strips[pl.ds(place, margin), :]
    second_out_ref[...] = strips[pl.ds(pl.multiple_of(margin - place, margin), margin), :]


def fold_rows_kernel(half, inside_ref, first_ref, second_ref, center_ref, outer_ref, inner_ref, total):
    margin = half // 2
    first, second, outer, inner = sides(half)
    for source, place in ((first_ref, first), (second_ref, second)):
        rows = pl.ds(pl.multiple_of(jnp.where(place == 0, 0, margin), margin), margin)
        total[rows, :] = inside_ref[rows, :] + source[...].astype(F32)
    center_ref[...] = total[:, margin : margin + half]
    outer_ref[...] = total[:, pl.ds(pl.multiple_of(outer, margin), margin)].astype(BF16)
    inner_ref[...] = total[:, pl.ds(pl.multiple_of(inner, margin), margin)].astype(BF16)


def fold_columns_kernel(half, center_ref, outer_ref, inner_ref, out_ref):
    margin = half // 2
    _, _, outer, inner = sides(half)
    for source, place in ((outer_ref, outer), (inner_ref, inner)):
        columns = pl.ds(pl.multiple_of(jnp.where(place == 0, 0, margin), margin), margin)
        out_ref[:, columns] = center_ref[:, columns] + source[...].astype(F32)


def swap(values, axis, offset):
    count = lax.axis_size(axis)
    pairs = [(i, i + 1) for i in range(offset, count - 1, 2)]
    return lax.ppermute(values, axis, pairs + [(b, a) for a, b in pairs])


def whole(count):
    return [pl.BlockSpec(memory_space=pltpu.VMEM)] * count


def kernel_call(body, name, outs, count, scratch=(), flops=0, vmem=24):
    return pl.pallas_call(
        body,
        out_shape=outs,
        in_specs=whole(count),
        out_specs=jax.tree.map(lambda _: pl.BlockSpec(memory_space=pltpu.VMEM), outs),
        scratch_shapes=list(scratch),
        cost_estimate=pl.CostEstimate(flops=flops, bytes_accessed=1 << 20, transcendentals=0),
        compiler_params=pltpu.CompilerParams(vmem_limit_bytes=vmem << 20),
        name=name,
    )


def shards(tables, split_maps, white_noise):
    splits, core_side, _ = split_maps.shape
    half = core_side
    margin = core_side // 2
    length = 2 * core_side
    constant = {k: jnp.asarray(v) for k, v in tables.items() if k != "energy"}
    profile = tables["profile"]
    rows = jnp.asarray(np.ascontiguousarray(np.broadcast_to(profile[:, None], (length, 128))))
    cols = jnp.asarray(np.ascontiguousarray(np.broadcast_to(profile[None, :], (8, length))))
    scale = 1.0 / ((2 * SMOOTH + 1) ** 2 * (splits - 1) * tables["energy"])
    odd_row = lax.axis_index("dec") % 2
    odd_col = lax.axis_index("ra") % 2
    cube = length**3

    outer_columns = lax.dynamic_slice_in_dim(split_maps, odd_col * margin, margin, axis=2)
    first_rows = lax.dynamic_slice_in_dim(split_maps, (1 - odd_row) * margin, margin, axis=1)
    second_rows = lax.dynamic_slice_in_dim(split_maps, odd_row * margin, margin, axis=1)
    outer = swap(outer_columns, "ra", 1)
    first = swap(first_rows, "dec", 0)
    second = swap(second_rows, "dec", 1)

    spectrum = jax.ShapeDtypeStruct((half + 8, length), F32)
    re, im = kernel_call(
        functools.partial(noise_kernel, half), "noise_spectrum", (spectrum, spectrum), 3, flops=3 * cube
    )(white_noise, constant["left"], constant["right"])

    outer, re, im = lax.optimization_barrier((outer, re, im))
    first_corner = lax.dynamic_slice_in_dim(outer, (1 - odd_row) * margin, margin, axis=1)
    second_corner = lax.dynamic_slice_in_dim(outer, odd_row * margin, margin, axis=1)
    first, second, _, _ = lax.optimization_barrier((first, second, first_corner, second_corner))
    first_corner = swap(first_corner, "dec", 0)
    second_corner = swap(second_corner, "dec", 1)
    inner = swap(
        jnp.concatenate(
            [
                lax.dynamic_slice_in_dim(block, (1 - odd_col) * margin, margin, axis=2)
                for block in (first, split_maps, second)
            ],
            axis=1,
        ),
        "ra",
        0,
    )
    def columns(body, name, count, flops):
        return kernel_call(
            functools.partial(body, half),
            name,
            jax.ShapeDtypeStruct((splits, length + 16, margin), BF16),
            count,
            [pltpu.VMEM((splits, length, margin), BF16)],
            flops=flops,
        )

    left, right = constant["left"], constant["right"]
    core = kernel_call(
        functools.partial(core_kernel, half),
        "core_columns",
        jax.ShapeDtypeStruct((splits, length + 16, length), F32),
        7,
        [pltpu.VMEM((splits, length, half), BF16)],
        flops=cube,
    )(split_maps, first, second, rows, cols, left, right)
    outer = columns(outer_kernel, "outer_columns", 7, 400000 * cube // 1000)(
        core, outer, first_corner, second_corner, rows, cols, left
    )
    inner = columns(inner_kernel, "inner_columns", 5, cube)(outer, inner, rows, cols, left)

    strip = jax.ShapeDtypeStruct((margin, length), BF16)
    first, second, inside = kernel_call(
        functools.partial(main_kernel, half, scale),
        "tile_model",
        (strip, strip, jax.ShapeDtypeStruct((half, length), F32)),
        11,
        [
            pltpu.VMEM((half, length), BF16),
            pltpu.VMEM((half + 8, length), F32),
            pltpu.VMEM((2, half + 128, length), BF16),
            pltpu.VMEM((half, length), BF16),
        ],
        flops=20 * cube,
    )(
        core, inner, outer, re, im, rows, cols,
        constant["right"], constant["band_rows"], constant["band_columns"],
        constant["inverse_right"],
    )

    second = swap(second, "dec", 1)
    first = swap(first, "dec", 0)
    column = jax.ShapeDtypeStruct((half, margin), BF16)
    block = jax.ShapeDtypeStruct((half, half), F32)
    center, outer, inner = kernel_call(
        functools.partial(fold_rows_kernel, half), "fold_rows", (block, column, column), 3,
        [pltpu.VMEM((half, length), F32)],
    )(inside, first, second)
    outer = swap(outer, "ra", 1)
    inner = swap(inner, "ra", 0)
    return kernel_call(functools.partial(fold_columns_kernel, half), "fold_columns", block, 3)(
        center, outer, inner
    )


def solution(mesh):
    tables = host_tables(512)
    placed = (P(None, "dec", "ra"), P("dec", "ra"))
    return jax.shard_map(
        functools.partial(shards, tables), mesh=mesh, in_specs=placed, out_specs=P("dec", "ra"), check_vma=False
    )
```

```python
import functools

import jax
import jax.numpy as jnp
import numpy as np
from jax import lax
from jax.experimental import pallas as pl
from jax.experimental.pallas import tpu as pltpu
from jax.sharding import PartitionSpec as P

import ml_dtypes

SMOOTH = 4
BF16 = jnp.bfloat16
F32 = jnp.float32


def host_tables(length):
    half = length // 2
    index = np.arange(length)
    phase = np.outer(index, index) % length
    cos = np.cos(2 * np.pi * phase / length)
    sin = np.sin(2 * np.pi * phase / length)
    sin[phase % half == 0] = 0.0
    cos = cos.astype(ml_dtypes.bfloat16).astype(np.float64)
    sin = sin.astype(ml_dtypes.bfloat16).astype(np.float64)

    def packed(rows):
        return np.ascontiguousarray(rows).astype(ml_dtypes.bfloat16)

    left = np.zeros((length + 16, length))
    left[:half] = cos[:half]
    left[half:length] = sin[:half]
    left[length] = cos[half]
    right = np.concatenate([cos[:, :half], sin[:, :half]], axis=1)
    right[:, half] = cos[:, half]
    margin = half // 2
    right = np.roll(right, -margin, axis=0)
    right = np.concatenate([right[:half], np.roll(right[half:], margin, axis=0)], axis=0)
    inverse_right = np.concatenate([2 * cos[:half], -2 * sin[:half]], axis=0)
    inverse_right[0] = cos[0]
    inverse_right[half] = cos[half]
    order = np.concatenate([index[:half], [half], -index[1:half]])

    def near(first, second):
        apart = np.abs(first[:, None] - second[None, :]) % length
        return (np.minimum(apart, length - apart) <= SMOOTH).astype(np.float64)

    band_columns = near(order, order)
    band_rows = np.zeros((half + 16, half + 128))
    targets = np.arange(half + 1)
    band_rows[: half + 1, : half + 1] = near(targets, targets)
    first, last = half + 8, half + 16
    band_rows[: half + 1, first + 1 : first + 8] = near(targets, -np.arange(1, 8))
    band_rows[: half + 1, last : last + 8] = near(targets, -np.arange(half - 8, half))
    profile = np.sin(np.pi * (index + 0.5) / length) ** 2
    energy = np.sum(profile**2) ** 2
    return dict(
        left=packed(left),
        right=packed(right),
        inverse_right=packed(inverse_right),
        band_columns=packed(band_columns),
        band_rows=packed(band_rows),
        profile=profile.astype(np.float32),
        energy=float(energy),
    )


def dot(a, b):
    return jnp.dot(a, b, preferred_element_type=F32)


def first_column(shape):
    return lax.broadcasted_iota(jnp.int32, shape, 1) == 0


def two_parts(values):
    high = values.astype(BF16)
    return high, (values - high.astype(F32)).astype(BF16)


def quarters(spectra, half):
    length = 2 * half
    return (
        spectra[:half, :half],
        spectra[:half, half:],
        spectra[half:length, :half],
        spectra[half:length, half:],
        spectra[length : length + 8, :half],
        spectra[length : length + 8, half:],
    )


def noise_kernel(half, noise_ref, left_ref, right_ref, re_ref, im_ref):
    margin = half // 2
    halves = dot(left_ref[...], noise_ref[...]).astype(BF16)
    spectra = (
        dot(halves[:, margin : margin + half], right_ref[:half])
        + dot(halves[:, :margin], right_ref[half : half + margin])
        + dot(halves[:, margin + half :], right_ref[half + margin :])
    )
    cc, cs, sc, ss, nc, ns = quarters(spectra, half)
    edge = first_column((half, half))
    re_ref[:half, :half] = jnp.where(edge, cc, cc - ss)
    re_ref[:half, half:] = jnp.where(edge, cs, cc + ss)
    im_ref[:half, :half] = -jnp.where(edge, sc, cs + sc)
    im_ref[:half, half:] = jnp.where(edge, -ss, cs - sc)
    edge = first_column((8, half))
    re_ref[half : half + 8, :half] = nc
    re_ref[half : half + 8, half:] = jnp.where(edge, ns, nc)
    im_ref[half : half + 8, :half] = jnp.where(edge, 0.0, -ns)
    im_ref[half : half + 8, half:] = jnp.where(edge, 0.0, ns)


def aligned(offset, step):
    return offset if isinstance(offset, int) else pl.multiple_of(offset, step)


def fill(tile, source, rows_ref, cols_ref, source_row, height, row, col, tile_col):
    splits, width = source.shape[0], source.shape[2]
    step = 32
    pc = cols_ref[:1, pl.ds(aligned(col, 128), width)]

    def strip(number, carry):
        start = pl.multiple_of(source_row + number * step, step)
        target = pl.multiple_of(row + number * step, step)
        members = [source[s, pl.ds(start, step), :].astype(F32) for s in range(splits)]
        mean = functools.reduce(lambda a, b: a + b, members) * (1.0 / splits)
        weights = jnp.concatenate([rows_ref[pl.ds(target, step), :]] * (width // 128), axis=1) * pc
        for s in range(splits):
            tile[s, pl.ds(target, step), pl.ds(aligned(tile_col, 128), width)] = (
                weights * (members[s] - mean)
            ).astype(BF16)
        return carry

    lax.fori_loop(0, height // step, strip, 0)


def sides(half):
    far = half + half // 2
    first = jnp.where(lax.axis_index("dec") % 2 == 0, far, 0)
    outer = jnp.where(lax.axis_index("ra") % 2 == 0, 0, far)
    return first, far - first, outer, far - outer


def cut_kernel(half, maps_ref, first_ref, second_ref, semaphores):
    margin = half // 2
    first, second, outer, _ = sides(half)
    columns = pl.ds(pl.multiple_of(jnp.where(outer == 0, 0, margin), margin), margin)
    copies = []
    for number, (target, place) in enumerate(((first_ref, first), (second_ref, second))):
        rows = pl.ds(pl.multiple_of(jnp.where(place == 0, 0, margin), margin), margin)
        for s in range(target.shape[0]):
            copies.append(
                pltpu.make_async_copy(maps_ref.at[s, rows, columns], target.at[s], semaphores.at[number, s])
            )
    for copy in copies:
        copy.start()
    for copy in copies:
        copy.wait()


def core_kernel(half, core_ref, first_ref, second_ref, rows_ref, cols_ref, left_ref, right_ref, spectra_ref, tile):
    margin = half // 2
    splits = core_ref.shape[0]
    first, second, _, _ = sides(half)
    fill(tile, core_ref, rows_ref, cols_ref, 0, half, margin, margin, 0)
    fill(tile, first_ref, rows_ref, cols_ref, 0, margin, first, margin, 0)
    fill(tile, second_ref, rows_ref, cols_ref, 0, margin, second, margin, 0)

    for s in range(splits):
        halves = dot(left_ref[...], tile[s]).astype(BF16)
        spectra_ref[s] = dot(halves, right_ref[:half])


def transform_pairs(tile, left_ref, halves_ref):
    splits, _, width = tile.shape
    for s in range(0, splits, 2):
        halves = dot(left_ref[...], jnp.concatenate([tile[s], tile[s + 1]], axis=1)).astype(BF16)
        halves_ref[s] = halves[:, :width]
        halves_ref[s + 1] = halves[:, width:]


def inner_kernel(half, after_ref, inner_ref, rows_ref, cols_ref, left_ref, halves_ref, tile):
    del after_ref
    margin = half // 2
    first, second, _, inner = sides(half)
    fill(tile, inner_ref, rows_ref, cols_ref, 0, margin, first, inner, 0)
    fill(tile, inner_ref, rows_ref, cols_ref, margin, half, margin, inner, 0)
    fill(tile, inner_ref, rows_ref, cols_ref, margin + half, margin, second, inner, 0)
    transform_pairs(tile, left_ref, halves_ref)


def outer_kernel(
    half, after_ref, outer_first_ref, outer_second_ref, first_ref, second_ref, rows_ref, cols_ref, left_ref,
    halves_ref, tile,
):
    del after_ref
    margin = half // 2
    first, second, outer, _ = sides(half)
    for source, place in ((outer_first_ref, first), (outer_second_ref, second)):
        row = jnp.where(place == 0, margin, half)
        fill(tile, source, rows_ref, cols_ref, 0, margin, row, outer, 0)
    fill(tile, first_ref, rows_ref, cols_ref, 0, margin, first, outer, 0)
    fill(tile, second_ref, rows_ref, cols_ref, 0, margin, second, outer, 0)
    transform_pairs(tile, left_ref, halves_ref)


def main_kernel(
    half, scale,
    core_ref, inner_ref, outer_ref, re_ref, im_ref,
    rows_ref, cols_ref, right_ref, band_rows_ref, band_columns_ref,
    inverse_right_ref,
    first_out_ref, second_out_ref, inside_ref,
    table, power, stacked, strips,
):
    length = 2 * half
    margin = half // 2
    splits = core_ref.shape[0]
    first, _, _, inner = sides(half)
    place = pl.multiple_of(half + jnp.where(inner == 0, 0, margin), margin)
    table[:margin] = right_ref[pl.ds(place, margin), :]
    table[margin:] = right_ref[pl.ds(pl.multiple_of(length + margin - place, margin), margin), :]

    edge = first_column((half, half))
    edge8 = first_column((8, half))

    def accumulate(s, carry):
        halves = jnp.concatenate([inner_ref[s], outer_ref[s]], axis=1)
        spectra = core_ref[s] + dot(halves, table[...])
        cc, cs, sc, ss, nc, ns = quarters(spectra, half)
        e = jnp.where(edge, cc, cc - ss)
        f = jnp.where(edge, sc, cs + sc)
        g = jnp.where(edge, cs, cc + ss)
        h = jnp.where(edge, ss, cs - sc)
        nc, ns = nc * nc, ns * ns
        terms = (
            e * e + f * f, g * g + h * h, jnp.where(edge8, nc, nc + ns), jnp.where(edge8, ns, nc + ns)
        )
        places = (
            (slice(0, half), slice(0, half)), (slice(0, half), slice(half, length)),
            (slice(half, half + 8), slice(0, half)), (slice(half, half + 8), slice(half, length)),
        )
        for term, place in zip(terms, places):
            power[place] = term if carry else power[place] + term

    accumulate(0, True)
    for s in range(1, splits):
        accumulate(s, False)

    stacked[:, half + 24 :, :] = jnp.zeros((2, stacked.shape[1] - half - 24, length), BF16)
    for part, values in enumerate(two_parts(power[...])):
        stacked[part, : half + 8, :] = values
    for place, start in ((half + 8, 0), (half + 16, half - 8)):
        a = power[start : start + 8, :half]
        b = power[start : start + 8, half:]
        mirrored = jnp.concatenate(
            [jnp.where(edge8, a, b), jnp.where(edge8, b, a)], axis=1
        )
        for part, values in enumerate(two_parts(mirrored)):
            stacked[part, place : place + 8, :] = values
    smooth = (
        dot(band_rows_ref[...], stacked[1]) + dot(band_rows_ref[...], stacked[0])
    )
    high, low = two_parts(smooth)
    smooth = dot(low, band_columns_ref[...]) + dot(high, band_columns_ref[...])
    gain = jnp.sqrt(jnp.maximum(smooth[: half + 8], 0.0) * scale)
    gr = (gain * re_ref[...]).astype(BF16)
    gi = (gain * im_ref[...]).astype(BF16)
    er, fr = gr[:half, :half], gr[:half, half:]
    ei, fi = gi[:half, :half], gi[:half, half:]
    start = lax.broadcasted_iota(jnp.int32, (half, half), 0) == 0
    nyquist_u = gr[half : half + 1, :half]
    nyquist_v = jnp.where(edge8[:1], gr[half : half + 1, half:], gi[half : half + 1, :half])
    zero = jnp.zeros((), BF16)
    near_u = jnp.concatenate([er, jnp.where(start, nyquist_u, -ei)], axis=0)
    far_u = jnp.concatenate(
        [jnp.where(edge, er, fr), -jnp.where(edge, ei, fi)], axis=0
    )
    near_v = jnp.concatenate(
        [jnp.where(edge, fr, ei), jnp.where(start, nyquist_v, jnp.where(edge, -fi, er))], axis=0
    )
    far_v = jnp.concatenate(
        [jnp.where(edge, fr, -fi), -jnp.where(edge, fi, fr)], axis=0
    )
    start = lax.broadcasted_iota(jnp.int32, (length, half), 0) % half == 0
    far_u, far_v = jnp.where(start, zero, far_u), jnp.where(start, zero, far_v)
    u = dot(right_ref[...], near_u) + dot(right_ref[...], far_u)
    v = dot(right_ref[...], near_v) + dot(right_ref[...], far_v)
    joined = jnp.concatenate([u.astype(BF16), v.astype(BF16)], axis=1)
    real_part = dot(joined, inverse_right_ref[...])
    pc = cols_ref[:1, :] * (1.0 / (length * length))

    def windowed(row, place, count):
        profile = jnp.concatenate([rows_ref[row : row + count, :]] * (length // 128), axis=1)
        return profile * pc * real_part[place : place + count]

    inside_ref[...] = windowed(margin, 0, half)
    strips[:margin] = windowed(0, half, margin).astype(BF16)
    strips[margin:] = windowed(margin + half, half + margin, margin).astype(BF16)
    place = pl.multiple_of(jnp.where(first == 0, 0, margin), margin)
    first_out_ref[...] = strips[pl.ds(place, margin), :]
    second_out_ref[...] = strips[pl.ds(pl.multiple_of(margin - place, margin), margin), :]


def fold_rows_kernel(half, inside_ref, first_ref, second_ref, center_ref, outer_ref, inner_ref, total):
    margin = half // 2
    first, second, outer, inner = sides(half)
    for source, place in ((first_ref, first), (second_ref, second)):
        rows = pl.ds(pl.multiple_of(jnp.where(place == 0, 0, margin), margin), margin)
        total[rows, :] = inside_ref[rows, :] + source[...].astype(F32)
    center_ref[...] = total[:, margin : margin + half]
    outer_ref[...] = total[:, pl.ds(pl.multiple_of(outer, margin), margin)].astype(BF16)
    inner_ref[...] = total[:, pl.ds(pl.multiple_of(inner, margin), margin)].astype(BF16)


def fold_columns_kernel(half, center_ref, outer_ref, inner_ref, out_ref):
    margin = half // 2
    _, _, outer, inner = sides(half)
    for source, place in ((outer_ref, outer), (inner_ref, inner)):
        columns = pl.ds(pl.multiple_of(jnp.where(place == 0, 0, margin), margin), margin)
        out_ref[:, columns] = center_ref[:, columns] + source[...].astype(F32)


def swap(values, axis, offset):
    count = lax.axis_size(axis)
    pairs = [(i, i + 1) for i in range(offset, count - 1, 2)]
    return lax.ppermute(values, axis, pairs + [(b, a) for a, b in pairs])


def whole(count):
    return [pl.BlockSpec(memory_space=pltpu.VMEM)] * count


def kernel_call(body, name, outs, count, scratch=(), flops=0, vmem=24):
    return pl.pallas_call(
        body,
        out_shape=outs,
        in_specs=whole(count),
        out_specs=jax.tree.map(lambda _: pl.BlockSpec(memory_space=pltpu.VMEM), outs),
        scratch_shapes=list(scratch),
        cost_estimate=pl.CostEstimate(flops=flops, bytes_accessed=1 << 20, transcendentals=0),
        compiler_params=pltpu.CompilerParams(vmem_limit_bytes=vmem << 20),
        name=name,
    )


def shards(tables, split_maps, white_noise):
    splits, core_side, _ = split_maps.shape
    half = core_side
    margin = core_side // 2
    length = 2 * core_side
    constant = {k: jnp.asarray(v) for k, v in tables.items() if k != "energy"}
    profile = tables["profile"]
    rows = jnp.asarray(np.ascontiguousarray(np.broadcast_to(profile[:, None], (length, 128))))
    cols = jnp.asarray(np.ascontiguousarray(np.broadcast_to(profile[None, :], (8, length))))
    scale = 1.0 / ((2 * SMOOTH + 1) ** 2 * (splits - 1) * tables["energy"])
    odd_row = lax.axis_index("dec") % 2
    odd_col = lax.axis_index("ra") % 2
    cube = length**3

    piece = jax.ShapeDtypeStruct((splits, margin, margin), BF16)
    outer_first, outer_second = pl.pallas_call(
        functools.partial(cut_kernel, half),
        out_shape=(piece, piece),
        in_specs=[pl.BlockSpec(memory_space=pl.ANY)],
        out_specs=tuple(whole(2)),
        scratch_shapes=[pltpu.SemaphoreType.DMA((2, splits))],
        compiler_params=pltpu.CompilerParams(vmem_limit_bytes=4 << 20),
        name="cut_outer",
    )(split_maps)
    outer_first, outer_second, whole_core = lax.optimization_barrier((outer_first, outer_second, split_maps))
    first_rows = lax.dynamic_slice_in_dim(whole_core, (1 - odd_row) * margin, margin, axis=1)
    second_rows = lax.dynamic_slice_in_dim(whole_core, odd_row * margin, margin, axis=1)
    outer_first = swap(outer_first, "ra", 1)
    second = swap(second_rows, "dec", 1)
    first = swap(first_rows, "dec", 0)
    outer_second = swap(outer_second, "ra", 1)

    spectrum = jax.ShapeDtypeStruct((half + 8, length), F32)
    re, im = kernel_call(
        functools.partial(noise_kernel, half), "noise_spectrum", (spectrum, spectrum), 3, flops=50 * cube
    )(white_noise, constant["left"], constant["right"])

    first, second, _, _, re, im = lax.optimization_barrier((first, second, outer_first, outer_second, re, im))
    first_corner = swap(outer_first, "dec", 0)
    second_corner = swap(outer_second, "dec", 1)
    inner = swap(
        jnp.concatenate(
            [
                lax.dynamic_slice_in_dim(block, (1 - odd_col) * margin, margin, axis=2)
                for block in (first, split_maps, second)
            ],
            axis=1,
        ),
        "ra",
        0,
    )
    def columns(body, name, count, flops):
        return kernel_call(
            functools.partial(body, half),
            name,
            jax.ShapeDtypeStruct((splits, length + 16, margin), BF16),
            count,
            [pltpu.VMEM((splits, length, margin), BF16)],
            flops=flops,
        )

    left, right = constant["left"], constant["right"]
    core = kernel_call(
        functools.partial(core_kernel, half),
        "core_columns",
        jax.ShapeDtypeStruct((splits, length + 16, length), F32),
        7,
        [pltpu.VMEM((splits, length, half), BF16)],
        flops=cube,
    )(split_maps, first, second, rows, cols, left, right)
    outer = columns(outer_kernel, "outer_columns", 8, 400000 * cube // 1000)(
        core, outer_first, outer_second, first_corner, second_corner, rows, cols, left
    )
    inner = columns(inner_kernel, "inner_columns", 5, cube)(outer, inner, rows, cols, left)

    strip = jax.ShapeDtypeStruct((margin, length), BF16)
    first, second, inside = kernel_call(
        functools.partial(main_kernel, half, scale),
        "tile_model",
        (strip, strip, jax.ShapeDtypeStruct((half, length), F32)),
        11,
        [
            pltpu.VMEM((half, length), BF16),
            pltpu.VMEM((half + 8, length), F32),
            pltpu.VMEM((2, half + 128, length), BF16),
            pltpu.VMEM((half, length), BF16),
        ],
        flops=20 * cube,
    )(
        core, inner, outer, re, im, rows, cols,
        constant["right"], constant["band_rows"], constant["band_columns"],
        constant["inverse_right"],
    )

    second = swap(second, "dec", 1)
    first = swap(first, "dec", 0)
    column = jax.ShapeDtypeStruct((half, margin), BF16)
    block = jax.ShapeDtypeStruct((half, half), F32)
    center, outer, inner = kernel_call(
        functools.partial(fold_rows_kernel, half), "fold_rows", (block, column, column), 3,
        [pltpu.VMEM((half, length), F32)],
    )(inside, first, second)
    outer = swap(outer, "ra", 1)
    inner = swap(inner, "ra", 0)
    return kernel_call(functools.partial(fold_columns_kernel, half), "fold_columns", block, 3)(
        center, outer, inner
    )


def solution(mesh):
    tables = host_tables(512)
    placed = (P(None, "dec", "ra"), P("dec", "ra"))
    return jax.shard_map(
        functools.partial(shards, tables), mesh=mesh, in_specs=placed, out_specs=P("dec", "ra"), check_vma=False
    )
```

```python
import functools

import jax
import jax.numpy as jnp
import numpy as np
from jax import lax
from jax.experimental import pallas as pl
from jax.experimental.pallas import tpu as pltpu
from jax.sharding import PartitionSpec as P

import ml_dtypes

SMOOTH = 4
BF16 = jnp.bfloat16
F32 = jnp.float32


def host_tables(length):
    half = length // 2
    index = np.arange(length)
    phase = np.outer(index, index) % length
    cos = np.cos(2 * np.pi * phase / length)
    sin = np.sin(2 * np.pi * phase / length)
    sin[phase % half == 0] = 0.0
    cos = cos.astype(ml_dtypes.bfloat16).astype(np.float64)
    sin = sin.astype(ml_dtypes.bfloat16).astype(np.float64)

    def packed(rows):
        return np.ascontiguousarray(rows).astype(ml_dtypes.bfloat16)

    left = np.zeros((length + 16, length))
    left[:half] = cos[:half]
    left[half:length] = sin[:half]
    left[length] = cos[half]
    right = np.concatenate([cos[:, :half], sin[:, :half]], axis=1)
    right[:, half] = cos[:, half]
    margin = half // 2
    right = np.roll(right, -margin, axis=0)
    right = np.concatenate([right[:half], np.roll(right[half:], margin, axis=0)], axis=0)
    inverse_right = np.concatenate([2 * cos[:half], -2 * sin[:half]], axis=0)
    inverse_right[0] = cos[0]
    inverse_right[half] = cos[half]
    order = np.concatenate([index[:half], [half], -index[1:half]])

    def near(first, second):
        apart = np.abs(first[:, None] - second[None, :]) % length
        return (np.minimum(apart, length - apart) <= SMOOTH).astype(np.float64)

    band_columns = near(order, order)
    band_rows = np.zeros((half + 16, half + 128))
    targets = np.arange(half + 1)
    band_rows[: half + 1, : half + 1] = near(targets, targets)
    first, last = half + 8, half + 16
    band_rows[: half + 1, first + 1 : first + 8] = near(targets, -np.arange(1, 8))
    band_rows[: half + 1, last : last + 8] = near(targets, -np.arange(half - 8, half))
    profile = np.sin(np.pi * (index + 0.5) / length) ** 2
    energy = np.sum(profile**2) ** 2
    return dict(
        left=packed(left),
        right=packed(right),
        inverse_right=packed(inverse_right),
        band_columns=packed(band_columns),
        band_rows=packed(band_rows),
        profile=profile.astype(np.float32),
        energy=float(energy),
    )


def dot(a, b):
    return jnp.dot(a, b, preferred_element_type=F32)


def first_column(shape):
    return lax.broadcasted_iota(jnp.int32, shape, 1) == 0


def two_parts(values):
    high = values.astype(BF16)
    return high, (values - high.astype(F32)).astype(BF16)


def quarters(spectra, half):
    length = 2 * half
    return (
        spectra[:half, :half],
        spectra[:half, half:],
        spectra[half:length, :half],
        spectra[half:length, half:],
        spectra[length : length + 8, :half],
        spectra[length : length + 8, half:],
    )


def noise_kernel(half, noise_ref, left_ref, right_ref, re_ref, im_ref):
    margin = half // 2
    halves = dot(left_ref[...], noise_ref[...]).astype(BF16)
    spectra = (
        dot(halves[:, margin : margin + half], right_ref[:half])
        + dot(halves[:, :margin], right_ref[half : half + margin])
        + dot(halves[:, margin + half :], right_ref[half + margin :])
    )
    cc, cs, sc, ss, nc, ns = quarters(spectra, half)
    edge = first_column((half, half))
    re_ref[:half, :half] = jnp.where(edge, cc, cc - ss)
    re_ref[:half, half:] = jnp.where(edge, cs, cc + ss)
    im_ref[:half, :half] = -jnp.where(edge, sc, cs + sc)
    im_ref[:half, half:] = jnp.where(edge, -ss, cs - sc)
    edge = first_column((8, half))
    re_ref[half : half + 8, :half] = nc
    re_ref[half : half + 8, half:] = jnp.where(edge, ns, nc)
    im_ref[half : half + 8, :half] = jnp.where(edge, 0.0, -ns)
    im_ref[half : half + 8, half:] = jnp.where(edge, 0.0, ns)


def aligned(offset, step):
    return offset if isinstance(offset, int) else pl.multiple_of(offset, step)


def fill(tile, source, rows_ref, cols_ref, source_row, height, row, col, tile_col, exists=None):
    splits, width = source.shape[0], source.shape[2]
    step = 32
    pc = cols_ref[:1, pl.ds(aligned(col, 128), width)]
    if exists is not None:
        pc = pc * exists

    def strip(number, carry):
        start = pl.multiple_of(source_row + number * step, step)
        target = pl.multiple_of(row + number * step, step)
        members = [source[s, pl.ds(start, step), :].astype(F32) for s in range(splits)]
        mean = functools.reduce(lambda a, b: a + b, members) * (1.0 / splits)
        weights = jnp.concatenate([rows_ref[pl.ds(target, step), :]] * (width // 128), axis=1) * pc
        for s in range(splits):
            tile[s, pl.ds(target, step), pl.ds(aligned(tile_col, 128), width)] = (
                weights * (members[s] - mean)
            ).astype(BF16)
        return carry

    lax.fori_loop(0, height // step, strip, 0)


def sides(half):
    far = half + half // 2
    first = jnp.where(lax.axis_index("dec") % 2 == 0, far, 0)
    outer = jnp.where(lax.axis_index("ra") % 2 == 0, 0, far)
    return first, far - first, outer, far - outer


def inside_sky():
    flags = []
    for axis in ("dec", "ra"):
        index = lax.axis_index(axis)
        edge = jnp.logical_or(index == 0, index == lax.axis_size(axis) - 1)
        flags.append(jnp.where(edge, 0.0, 1.0).astype(F32))
    return flags


def cut_kernel(half, maps_ref, outer_first_ref, outer_second_ref, first_ref, second_ref):
    margin = half // 2
    first, second, outer, _ = sides(half)
    columns = pl.ds(pl.multiple_of(jnp.where(outer == 0, 0, margin), margin), margin)
    for piece, strip, place in (
        (outer_first_ref, first_ref, first), (outer_second_ref, second_ref, second)
    ):
        rows = pl.ds(pl.multiple_of(jnp.where(place == 0, 0, margin), margin), margin)
        for s in range(maps_ref.shape[0]):
            piece[s] = maps_ref[s, rows, columns]
            strip[s] = maps_ref[s, rows, :]


def core_kernel(half, core_ref, first_ref, second_ref, rows_ref, cols_ref, left_ref, right_ref, spectra_ref, tile):
    margin = half // 2
    splits = core_ref.shape[0]
    first, second, _, _ = sides(half)
    has_second, _ = inside_sky()
    fill(tile, core_ref, rows_ref, cols_ref, 0, half, margin, margin, 0)
    fill(tile, first_ref, rows_ref, cols_ref, 0, margin, first, margin, 0)
    fill(tile, second_ref, rows_ref, cols_ref, 0, margin, second, margin, 0, has_second)

    for s in range(splits):
        halves = dot(left_ref[...], tile[s]).astype(BF16)
        spectra_ref[s] = dot(halves, right_ref[:half])


def transform_pairs(tile, left_ref, halves_ref):
    splits, _, width = tile.shape
    for s in range(0, splits, 2):
        halves = dot(left_ref[...], jnp.concatenate([tile[s], tile[s + 1]], axis=1)).astype(BF16)
        halves_ref[s] = halves[:, :width]
        halves_ref[s + 1] = halves[:, width:]


def inner_kernel(half, after_ref, inner_ref, rows_ref, cols_ref, left_ref, halves_ref, tile):
    del after_ref
    margin = half // 2
    first, second, _, inner = sides(half)
    has_second, _ = inside_sky()
    fill(tile, inner_ref, rows_ref, cols_ref, 0, margin, first, inner, 0)
    fill(tile, inner_ref, rows_ref, cols_ref, margin, half, margin, inner, 0)
    fill(tile, inner_ref, rows_ref, cols_ref, margin + half, margin, second, inner, 0, has_second)
    transform_pairs(tile, left_ref, halves_ref)


def outer_kernel(
    half, after_ref, outer_first_ref, outer_second_ref, first_ref, second_ref, rows_ref, cols_ref, left_ref,
    halves_ref, tile,
):
    del after_ref
    margin = half // 2
    first, second, outer, _ = sides(half)
    has_second, has_outer = inside_sky()
    for source, place in ((outer_first_ref, first), (outer_second_ref, second)):
        row = jnp.where(place == 0, margin, half)
        fill(tile, source, rows_ref, cols_ref, 0, margin, row, outer, 0, has_outer)
    fill(tile, first_ref, rows_ref, cols_ref, 0, margin, first, outer, 0, has_outer)
    fill(tile, second_ref, rows_ref, cols_ref, 0, margin, second, outer, 0, has_outer * has_second)
    transform_pairs(tile, left_ref, halves_ref)


def main_kernel(
    half, scale,
    core_ref, inner_ref, outer_ref, re_ref, im_ref,
    rows_ref, cols_ref, right_ref, band_rows_ref, band_columns_ref,
    inverse_right_ref,
    first_out_ref, second_out_ref, inside_ref,
    table, power, stacked, strips,
):
    length = 2 * half
    margin = half // 2
    splits = core_ref.shape[0]
    first, _, _, inner = sides(half)
    place = pl.multiple_of(half + jnp.where(inner == 0, 0, margin), margin)
    table[:margin] = right_ref[pl.ds(place, margin), :]
    table[margin:] = right_ref[pl.ds(pl.multiple_of(length + margin - place, margin), margin), :]

    edge = first_column((half, half))
    edge8 = first_column((8, half))

    def accumulate(s, carry):
        halves = jnp.concatenate([inner_ref[s], outer_ref[s]], axis=1)
        spectra = core_ref[s] + dot(halves, table[...])
        cc, cs, sc, ss, nc, ns = quarters(spectra, half)
        e = jnp.where(edge, cc, cc - ss)
        f = jnp.where(edge, sc, cs + sc)
        g = jnp.where(edge, cs, cc + ss)
        h = jnp.where(edge, ss, cs - sc)
        nc, ns = nc * nc, ns * ns
        terms = (
            e * e + f * f, g * g + h * h, jnp.where(edge8, nc, nc + ns), jnp.where(edge8, ns, nc + ns)
        )
        places = (
            (slice(0, half), slice(0, half)), (slice(0, half), slice(half, length)),
            (slice(half, half + 8), slice(0, half)), (slice(half, half + 8), slice(half, length)),
        )
        for term, place in zip(terms, places):
            power[place] = term if carry else power[place] + term

    accumulate(0, True)
    for s in range(1, splits):
        accumulate(s, False)

    stacked[:, half + 24 :, :] = jnp.zeros((2, stacked.shape[1] - half - 24, length), BF16)
    for part, values in enumerate(two_parts(power[...])):
        stacked[part, : half + 8, :] = values
    for place, start in ((half + 8, 0), (half + 16, half - 8)):
        a = power[start : start + 8, :half]
        b = power[start : start + 8, half:]
        mirrored = jnp.concatenate(
            [jnp.where(edge8, a, b), jnp.where(edge8, b, a)], axis=1
        )
        for part, values in enumerate(two_parts(mirrored)):
            stacked[part, place : place + 8, :] = values
    smooth = (
        dot(band_rows_ref[...], stacked[1]) + dot(band_rows_ref[...], stacked[0])
    )
    high, low = two_parts(smooth)
    smooth = dot(low, band_columns_ref[...]) + dot(high, band_columns_ref[...])
    gain = jnp.sqrt(jnp.maximum(smooth[: half + 8], 0.0) * scale)
    gr = (gain * re_ref[...]).astype(BF16)
    gi = (gain * im_ref[...]).astype(BF16)
    er, fr = gr[:half, :half], gr[:half, half:]
    ei, fi = gi[:half, :half], gi[:half, half:]
    start = lax.broadcasted_iota(jnp.int32, (half, half), 0) == 0
    nyquist_u = gr[half : half + 1, :half]
    nyquist_v = jnp.where(edge8[:1], gr[half : half + 1, half:], gi[half : half + 1, :half])
    zero = jnp.zeros((), BF16)
    near_u = jnp.concatenate([er, jnp.where(start, nyquist_u, -ei)], axis=0)
    far_u = jnp.concatenate(
        [jnp.where(edge, er, fr), -jnp.where(edge, ei, fi)], axis=0
    )
    near_v = jnp.concatenate(
        [jnp.where(edge, fr, ei), jnp.where(start, nyquist_v, jnp.where(edge, -fi, er))], axis=0
    )
    far_v = jnp.concatenate(
        [jnp.where(edge, fr, -fi), -jnp.where(edge, fi, fr)], axis=0
    )
    start = lax.broadcasted_iota(jnp.int32, (length, half), 0) % half == 0
    far_u, far_v = jnp.where(start, zero, far_u), jnp.where(start, zero, far_v)
    u = dot(right_ref[...], near_u) + dot(right_ref[...], far_u)
    v = dot(right_ref[...], near_v) + dot(right_ref[...], far_v)
    joined = jnp.concatenate([u.astype(BF16), v.astype(BF16)], axis=1)
    real_part = dot(joined, inverse_right_ref[...])
    pc = cols_ref[:1, :] * (1.0 / (length * length))

    def windowed(row, place, count):
        profile = jnp.concatenate([rows_ref[row : row + count, :]] * (length // 128), axis=1)
        return profile * pc * real_part[place : place + count]

    inside_ref[...] = windowed(margin, 0, half)
    strips[:margin] = windowed(0, half, margin).astype(BF16)
    strips[margin:] = windowed(margin + half, half + margin, margin).astype(BF16)
    place = pl.multiple_of(jnp.where(first == 0, 0, margin), margin)
    first_out_ref[...] = strips[pl.ds(place, margin), :]
    second_out_ref[...] = strips[pl.ds(pl.multiple_of(margin - place, margin), margin), :]


def fold_rows_kernel(half, inside_ref, first_ref, second_ref, center_ref, outer_ref, inner_ref, total):
    margin = half // 2
    first, second, outer, inner = sides(half)
    has_second, _ = inside_sky()
    for source, place, exists in ((first_ref, first, 1.0), (second_ref, second, has_second)):
        rows = pl.ds(pl.multiple_of(jnp.where(place == 0, 0, margin), margin), margin)
        total[rows, :] = inside_ref[rows, :] + source[...].astype(F32) * exists
    center_ref[...] = total[:, margin : margin + half]
    outer_ref[...] = total[:, pl.ds(pl.multiple_of(outer, margin), margin)].astype(BF16)
    inner_ref[...] = total[:, pl.ds(pl.multiple_of(inner, margin), margin)].astype(BF16)


def fold_columns_kernel(half, center_ref, outer_ref, inner_ref, out_ref):
    margin = half // 2
    _, _, outer, inner = sides(half)
    _, has_outer = inside_sky()
    for source, place, exists in ((outer_ref, outer, has_outer), (inner_ref, inner, 1.0)):
        columns = pl.ds(pl.multiple_of(jnp.where(place == 0, 0, margin), margin), margin)
        out_ref[:, columns] = center_ref[:, columns] + source[...].astype(F32) * exists


def swap_rows(values, offset):
    rows, columns = lax.axis_size("dec"), lax.axis_size("ra")
    pairs = []
    for i in range(rows):
        partner = i + 1 if i % 2 == offset else i - 1
        for j in range(columns):
            target = partner * columns + j if 0 <= partner < rows else i * columns + (j ^ 1)
            pairs.append((i * columns + j, target))
    return lax.ppermute(values, ("dec", "ra"), pairs)


def swap_columns(values, offset):
    count = lax.axis_size("ra")
    pairs = [(i, (i + 1 if i % 2 == offset else i - 1) % count) for i in range(count)]
    return lax.ppermute(values, "ra", pairs)


def whole(count):
    return [pl.BlockSpec(memory_space=pltpu.VMEM)] * count


def kernel_call(body, name, outs, count, scratch=(), flops=0, vmem=16):
    return pl.pallas_call(
        body,
        out_shape=outs,
        in_specs=whole(count),
        out_specs=jax.tree.map(lambda _: pl.BlockSpec(memory_space=pltpu.VMEM), outs),
        scratch_shapes=list(scratch),
        cost_estimate=pl.CostEstimate(flops=flops, bytes_accessed=1 << 20, transcendentals=0),
        compiler_params=pltpu.CompilerParams(vmem_limit_bytes=vmem << 20),
        name=name,
    )


def shards(tables, split_maps, white_noise):
    splits, core_side, _ = split_maps.shape
    half = core_side
    margin = core_side // 2
    length = 2 * core_side
    constant = {k: jnp.asarray(v) for k, v in tables.items() if k != "energy"}
    profile = tables["profile"]
    rows = jnp.asarray(np.ascontiguousarray(np.broadcast_to(profile[:, None], (length, 128))))
    cols = jnp.asarray(np.ascontiguousarray(np.broadcast_to(profile[None, :], (8, length))))
    scale = 1.0 / ((2 * SMOOTH + 1) ** 2 * (splits - 1) * tables["energy"])
    odd_col = lax.axis_index("ra") % 2
    cube = length**3

    piece = jax.ShapeDtypeStruct((splits, margin, margin), BF16)
    strip = jax.ShapeDtypeStruct((splits, margin, half), BF16)
    outer_first, outer_second, first, second = kernel_call(
        functools.partial(cut_kernel, half), "cut", (piece, piece, strip, strip), 1, vmem=8
    )(split_maps)
    outer_first = swap_columns(outer_first, 1)
    second = swap_rows(second, 1)
    first = swap_rows(first, 0)
    outer_second = swap_columns(outer_second, 1)

    spectrum = jax.ShapeDtypeStruct((half + 8, length), F32)
    re, im = kernel_call(
        functools.partial(noise_kernel, half), "noise_spectrum", (spectrum, spectrum), 3, flops=50 * cube
    )(white_noise, constant["left"], constant["right"])

    first, second, _, _, re, im = lax.optimization_barrier((first, second, outer_first, outer_second, re, im))
    first_corner = swap_rows(outer_first, 0)
    second_corner = swap_rows(outer_second, 1)
    inner = swap_columns(
        jnp.concatenate(
            [
                lax.dynamic_slice_in_dim(block, (1 - odd_col) * margin, margin, axis=2)
                for block in (first, split_maps, second)
            ],
            axis=1,
        ),
        0,
    )
    def columns(body, name, count, flops):
        return kernel_call(
            functools.partial(body, half),
            name,
            jax.ShapeDtypeStruct((splits, length + 16, margin), BF16),
            count,
            [pltpu.VMEM((splits, length, margin), BF16)],
            flops=flops,
        )

    left, right = constant["left"], constant["right"]
    core = kernel_call(
        functools.partial(core_kernel, half),
        "core_columns",
        jax.ShapeDtypeStruct((splits, length + 16, length), F32),
        7,
        [pltpu.VMEM((splits, length, half), BF16)],
        flops=cube,
    )(split_maps, first, second, rows, cols, left, right)
    outer = columns(outer_kernel, "outer_columns", 8, 400000 * cube // 1000)(
        core, outer_first, outer_second, first_corner, second_corner, rows, cols, left
    )
    inner = columns(inner_kernel, "inner_columns", 5, cube)(outer, inner, rows, cols, left)

    strip = jax.ShapeDtypeStruct((margin, length), BF16)
    first, second, inside = kernel_call(
        functools.partial(main_kernel, half, scale),
        "tile_model",
        (strip, strip, jax.ShapeDtypeStruct((half, length), F32)),
        11,
        [
            pltpu.VMEM((half, length), BF16),
            pltpu.VMEM((half + 8, length), F32),
            pltpu.VMEM((2, half + 128, length), BF16),
            pltpu.VMEM((half, length), BF16),
        ],
        flops=20 * cube,
    )(
        core, inner, outer, re, im, rows, cols,
        constant["right"], constant["band_rows"], constant["band_columns"],
        constant["inverse_right"],
    )

    second = swap_rows(second, 1)
    first = swap_rows(first, 0)
    column = jax.ShapeDtypeStruct((half, margin), BF16)
    block = jax.ShapeDtypeStruct((half, half), F32)
    center, outer, inner = kernel_call(
        functools.partial(fold_rows_kernel, half), "fold_rows", (block, column, column), 3,
        [pltpu.VMEM((half, length), F32)],
    )(inside, first, second)
    outer = swap_columns(outer, 1)
    inner = swap_columns(inner, 0)
    return kernel_call(functools.partial(fold_columns_kernel, half), "fold_columns", block, 3)(
        center, outer, inner
    )


def solution(mesh):
    tables = host_tables(512)
    placed = (P(None, "dec", "ra"), P("dec", "ra"))
    return jax.shard_map(
        functools.partial(shards, tables), mesh=mesh, in_specs=placed, out_specs=P("dec", "ra"), check_vma=False
    )
```

```python
import functools

import jax
import jax.numpy as jnp
import numpy as np
from jax import lax
from jax.experimental import pallas as pl
from jax.experimental.pallas import tpu as pltpu
from jax.sharding import PartitionSpec as P

import ml_dtypes

SMOOTH = 4
BF16 = jnp.bfloat16
F32 = jnp.float32


def host_tables(length):
    half = length // 2
    index = np.arange(length)
    phase = np.outer(index, index) % length
    cos = np.cos(2 * np.pi * phase / length)
    sin = np.sin(2 * np.pi * phase / length)
    sin[phase % half == 0] = 0.0
    cos = cos.astype(ml_dtypes.bfloat16).astype(np.float64)
    sin = sin.astype(ml_dtypes.bfloat16).astype(np.float64)

    def packed(rows):
        return np.ascontiguousarray(rows).astype(ml_dtypes.bfloat16)

    left = np.zeros((length + 16, length))
    left[:half] = cos[:half]
    left[half:length] = sin[:half]
    left[length] = cos[half]
    right = np.concatenate([cos[:, :half], sin[:, :half]], axis=1)
    right[:, half] = cos[:, half]
    margin = half // 2
    right = np.roll(right, -margin, axis=0)
    right = np.concatenate([right[:half], np.roll(right[half:], margin, axis=0)], axis=0)
    inverse_right = np.concatenate([2 * cos[:half], -2 * sin[:half]], axis=0)
    inverse_right[0] = cos[0]
    inverse_right[half] = cos[half]
    order = np.concatenate([index[:half], [half], -index[1:half]])

    def near(first, second):
        apart = np.abs(first[:, None] - second[None, :]) % length
        return (np.minimum(apart, length - apart) <= SMOOTH).astype(np.float64)

    band_columns = near(order, order)
    band_rows = np.zeros((half + 16, half + 128))
    targets = np.arange(half + 1)
    band_rows[: half + 1, : half + 1] = near(targets, targets)
    first, last = half + 8, half + 16
    band_rows[: half + 1, first + 1 : first + 8] = near(targets, -np.arange(1, 8))
    band_rows[: half + 1, last : last + 8] = near(targets, -np.arange(half - 8, half))
    profile = np.sin(np.pi * (index + 0.5) / length) ** 2
    energy = np.sum(profile**2) ** 2
    return dict(
        left=packed(left),
        right=packed(right),
        inverse_right=packed(inverse_right),
        band_columns=packed(band_columns),
        band_rows=packed(band_rows),
        profile=profile.astype(np.float32),
        energy=float(energy),
    )


def dot(a, b):
    return jnp.dot(a, b, preferred_element_type=F32)


def first_column(shape):
    return lax.broadcasted_iota(jnp.int32, shape, 1) == 0


def two_parts(values):
    high = values.astype(BF16)
    return high, (values - high.astype(F32)).astype(BF16)


def quarters(spectra, half):
    length = 2 * half
    return (
        spectra[:half, :half],
        spectra[:half, half:],
        spectra[half:length, :half],
        spectra[half:length, half:],
        spectra[length : length + 8, :half],
        spectra[length : length + 8, half:],
    )


def noise_kernel(half, noise_ref, left_ref, right_ref, re_ref, im_ref):
    margin = half // 2
    halves = dot(left_ref[...], noise_ref[...]).astype(BF16)
    spectra = (
        dot(halves[:, margin : margin + half], right_ref[:half])
        + dot(halves[:, :margin], right_ref[half : half + margin])
        + dot(halves[:, margin + half :], right_ref[half + margin :])
    )
    cc, cs, sc, ss, nc, ns = quarters(spectra, half)
    edge = first_column((half, half))
    re_ref[:half, :half] = jnp.where(edge, cc, cc - ss)
    re_ref[:half, half:] = jnp.where(edge, cs, cc + ss)
    im_ref[:half, :half] = -jnp.where(edge, sc, cs + sc)
    im_ref[:half, half:] = jnp.where(edge, -ss, cs - sc)
    edge = first_column((8, half))
    re_ref[half : half + 8, :half] = nc
    re_ref[half : half + 8, half:] = jnp.where(edge, ns, nc)
    im_ref[half : half + 8, :half] = jnp.where(edge, 0.0, -ns)
    im_ref[half : half + 8, half:] = jnp.where(edge, 0.0, ns)


def aligned(offset, step):
    return offset if isinstance(offset, int) else pl.multiple_of(offset, step)


def fill(tile, source, rows_ref, cols_ref, source_row, height, row, col, tile_col, exists=None):
    splits, width = source.shape[0], source.shape[2]
    step = 32
    pc = cols_ref[:1, pl.ds(aligned(col, 128), width)]
    if exists is not None:
        pc = pc * exists

    def strip(number, carry):
        start = pl.multiple_of(source_row + number * step, step)
        target = pl.multiple_of(row + number * step, step)
        members = [source[s, pl.ds(start, step), :].astype(F32) for s in range(splits)]
        mean = functools.reduce(lambda a, b: a + b, members) * (1.0 / splits)
        weights = jnp.concatenate([rows_ref[pl.ds(target, step), :]] * (width // 128), axis=1) * pc
        for s in range(splits):
            tile[s, pl.ds(target, step), pl.ds(aligned(tile_col, 128), width)] = (
                weights * (members[s] - mean)
            ).astype(BF16)
        return carry

    lax.fori_loop(0, height // step, strip, 0)


def sides(half):
    far = half + half // 2
    first = jnp.where(lax.axis_index("dec") % 2 == 0, far, 0)
    outer = jnp.where(lax.axis_index("ra") % 2 == 0, 0, far)
    return first, far - first, outer, far - outer


def inside_sky():
    flags = []
    for axis in ("dec", "ra"):
        index = lax.axis_index(axis)
        edge = jnp.logical_or(index == 0, index == lax.axis_size(axis) - 1)
        flags.append(jnp.where(edge, 0.0, 1.0).astype(F32))
    return flags


def cut_kernel(half, maps_ref, outer_first_ref, outer_second_ref, first_ref, second_ref):
    margin = half // 2
    first, second, outer, _ = sides(half)
    columns = pl.ds(pl.multiple_of(jnp.where(outer == 0, 0, margin), margin), margin)
    for piece, strip, place in (
        (outer_first_ref, first_ref, first), (outer_second_ref, second_ref, second)
    ):
        rows = pl.ds(pl.multiple_of(jnp.where(place == 0, 0, margin), margin), margin)
        for s in range(maps_ref.shape[0]):
            piece[s] = maps_ref[s, rows, columns]
            strip[s] = maps_ref[s, rows, :]


def core_kernel(
    half, core_ref, first_ref, second_ref, outer_first_ref, outer_second_ref, rows_ref, cols_ref, left_ref, right_ref,
    spectra_ref, outer_ref, tile,
):
    margin = half // 2
    splits = core_ref.shape[0]
    first, second, outer, _ = sides(half)
    has_second, has_outer = inside_sky()
    fill(tile, core_ref, rows_ref, cols_ref, 0, half, margin, margin, 0)
    fill(tile, first_ref, rows_ref, cols_ref, 0, margin, first, margin, 0)
    fill(tile, second_ref, rows_ref, cols_ref, 0, margin, second, margin, 0, has_second)
    for s in range(splits):
        halves = dot(left_ref[...], tile[s]).astype(BF16)
        spectra_ref[s] = dot(halves, right_ref[:half])
    for source, place in ((outer_first_ref, first), (outer_second_ref, second)):
        row = jnp.where(place == 0, margin, half)
        fill(outer_ref, source, rows_ref, cols_ref, 0, margin, row, outer, 0, has_outer)


def transform_pairs(tile, left_ref, halves_ref):
    splits, _, width = tile.shape
    for s in range(0, splits, 2):
        halves = dot(left_ref[...], jnp.concatenate([tile[s], tile[s + 1]], axis=1)).astype(BF16)
        halves_ref[s] = halves[:, :width]
        halves_ref[s + 1] = halves[:, width:]


def inner_kernel(half, after_ref, inner_ref, rows_ref, cols_ref, left_ref, halves_ref, tile):
    del after_ref
    margin = half // 2
    first, second, _, inner = sides(half)
    has_second, _ = inside_sky()
    fill(tile, inner_ref, rows_ref, cols_ref, 0, margin, first, inner, 0)
    fill(tile, inner_ref, rows_ref, cols_ref, margin, half, margin, inner, 0)
    fill(tile, inner_ref, rows_ref, cols_ref, margin + half, margin, second, inner, 0, has_second)
    transform_pairs(tile, left_ref, halves_ref)


def outer_kernel(
    half, after_ref, tile, first_ref, second_ref, rows_ref, cols_ref, left_ref, halves_ref, full
):
    del after_ref
    margin = half // 2
    first, second, outer, _ = sides(half)
    has_second, has_outer = inside_sky()
    full[:, margin : margin + half, :] = tile[:, margin : margin + half, :]
    fill(full, first_ref, rows_ref, cols_ref, 0, margin, first, outer, 0, has_outer)
    fill(full, second_ref, rows_ref, cols_ref, 0, margin, second, outer, 0, has_outer * has_second)
    transform_pairs(full, left_ref, halves_ref)


def main_kernel(
    half, scale,
    core_ref, inner_ref, outer_ref, re_ref, im_ref,
    rows_ref, cols_ref, right_ref, band_rows_ref, band_columns_ref,
    inverse_right_ref,
    first_out_ref, second_out_ref, inside_ref,
    table, power, stacked, strips,
):
    length = 2 * half
    margin = half // 2
    splits = core_ref.shape[0]
    first, _, _, inner = sides(half)
    place = pl.multiple_of(half + jnp.where(inner == 0, 0, margin), margin)
    table[:margin] = right_ref[pl.ds(place, margin), :]
    table[margin:] = right_ref[pl.ds(pl.multiple_of(length + margin - place, margin), margin), :]

    edge = first_column((half, half))
    edge8 = first_column((8, half))

    def accumulate(s, carry):
        halves = jnp.concatenate([inner_ref[s], outer_ref[s]], axis=1)
        spectra = core_ref[s] + dot(halves, table[...])
        cc, cs, sc, ss, nc, ns = quarters(spectra, half)
        e = jnp.where(edge, cc, cc - ss)
        f = jnp.where(edge, sc, cs + sc)
        g = jnp.where(edge, cs, cc + ss)
        h = jnp.where(edge, ss, cs - sc)
        nc, ns = nc * nc, ns * ns
        terms = (
            e * e + f * f, g * g + h * h, jnp.where(edge8, nc, nc + ns), jnp.where(edge8, ns, nc + ns)
        )
        places = (
            (slice(0, half), slice(0, half)), (slice(0, half), slice(half, length)),
            (slice(half, half + 8), slice(0, half)), (slice(half, half + 8), slice(half, length)),
        )
        for term, place in zip(terms, places):
            power[place] = term if carry else power[place] + term

    accumulate(0, True)
    for s in range(1, splits):
        accumulate(s, False)

    stacked[:, half + 24 :, :] = jnp.zeros((2, stacked.shape[1] - half - 24, length), BF16)
    for part, values in enumerate(two_parts(power[...])):
        stacked[part, : half + 8, :] = values
    for place, start in ((half + 8, 0), (half + 16, half - 8)):
        a = power[start : start + 8, :half]
        b = power[start : start + 8, half:]
        mirrored = jnp.concatenate(
            [jnp.where(edge8, a, b), jnp.where(edge8, b, a)], axis=1
        )
        for part, values in enumerate(two_parts(mirrored)):
            stacked[part, place : place + 8, :] = values
    smooth = (
        dot(band_rows_ref[...], stacked[1]) + dot(band_rows_ref[...], stacked[0])
    )
    high, low = two_parts(smooth)
    smooth = dot(low, band_columns_ref[...]) + dot(high, band_columns_ref[...])
    gain = jnp.sqrt(jnp.maximum(smooth[: half + 8], 0.0) * scale)
    gr = (gain * re_ref[...]).astype(BF16)
    gi = (gain * im_ref[...]).astype(BF16)
    er, fr = gr[:half, :half], gr[:half, half:]
    ei, fi = gi[:half, :half], gi[:half, half:]
    start = lax.broadcasted_iota(jnp.int32, (half, half), 0) == 0
    nyquist_u = gr[half : half + 1, :half]
    nyquist_v = jnp.where(edge8[:1], gr[half : half + 1, half:], gi[half : half + 1, :half])
    zero = jnp.zeros((), BF16)
    near_u = jnp.concatenate([er, jnp.where(start, nyquist_u, -ei)], axis=0)
    far_u = jnp.concatenate(
        [jnp.where(edge, er, fr), -jnp.where(edge, ei, fi)], axis=0
    )
    near_v = jnp.concatenate(
        [jnp.where(edge, fr, ei), jnp.where(start, nyquist_v, jnp.where(edge, -fi, er))], axis=0
    )
    far_v = jnp.concatenate(
        [jnp.where(edge, fr, -fi), -jnp.where(edge, fi, fr)], axis=0
    )
    start = lax.broadcasted_iota(jnp.int32, (length, half), 0) % half == 0
    far_u, far_v = jnp.where(start, zero, far_u), jnp.where(start, zero, far_v)
    u = dot(right_ref[...], near_u) + dot(right_ref[...], far_u)
    v = dot(right_ref[...], near_v) + dot(right_ref[...], far_v)
    joined = jnp.concatenate([u.astype(BF16), v.astype(BF16)], axis=1)
    real_part = dot(joined, inverse_right_ref[...])
    pc = cols_ref[:1, :] * (1.0 / (length * length))

    def windowed(row, place, count):
        profile = jnp.concatenate([rows_ref[row : row + count, :]] * (length // 128), axis=1)
        return profile * pc * real_part[place : place + count]

    inside_ref[...] = windowed(margin, 0, half)
    strips[:margin] = windowed(0, half, margin).astype(BF16)
    strips[margin:] = windowed(margin + half, half + margin, margin).astype(BF16)
    place = pl.multiple_of(jnp.where(first == 0, 0, margin), margin)
    first_out_ref[...] = strips[pl.ds(place, margin), :]
    second_out_ref[...] = strips[pl.ds(pl.multiple_of(margin - place, margin), margin), :]


def fold_rows_kernel(half, inside_ref, first_ref, second_ref, center_ref, outer_ref, inner_ref, total):
    margin = half // 2
    first, second, outer, inner = sides(half)
    has_second, _ = inside_sky()
    for source, place, exists in ((first_ref, first, 1.0), (second_ref, second, has_second)):
        rows = pl.ds(pl.multiple_of(jnp.where(place == 0, 0, margin), margin), margin)
        total[rows, :] = inside_ref[rows, :] + source[...].astype(F32) * exists
    center_ref[...] = total[:, margin : margin + half]
    outer_ref[...] = total[:, pl.ds(pl.multiple_of(outer, margin), margin)].astype(BF16)
    inner_ref[...] = total[:, pl.ds(pl.multiple_of(inner, margin), margin)].astype(BF16)


def fold_columns_kernel(half, center_ref, outer_ref, inner_ref, out_ref):
    margin = half // 2
    _, _, outer, inner = sides(half)
    _, has_outer = inside_sky()
    for source, place, exists in ((outer_ref, outer, has_outer), (inner_ref, inner, 1.0)):
        columns = pl.ds(pl.multiple_of(jnp.where(place == 0, 0, margin), margin), margin)
        out_ref[:, columns] = center_ref[:, columns] + source[...].astype(F32) * exists


def swap_rows(values, offset):
    rows, columns = lax.axis_size("dec"), lax.axis_size("ra")
    pairs = []
    for i in range(rows):
        partner = i + 1 if i % 2 == offset else i - 1
        for j in range(columns):
            target = partner * columns + j if 0 <= partner < rows else i * columns + (j ^ 1)
            pairs.append((i * columns + j, target))
    return lax.ppermute(values, ("dec", "ra"), pairs)


def swap_columns(values, offset):
    count = lax.axis_size("ra")
    pairs = [(i, (i + 1 if i % 2 == offset else i - 1) % count) for i in range(count)]
    return lax.ppermute(values, "ra", pairs)


def whole(count):
    return [pl.BlockSpec(memory_space=pltpu.VMEM)] * count


def kernel_call(body, name, outs, count, scratch=(), flops=0, vmem=16):
    return pl.pallas_call(
        body,
        out_shape=outs,
        in_specs=whole(count),
        out_specs=jax.tree.map(lambda _: pl.BlockSpec(memory_space=pltpu.VMEM), outs),
        scratch_shapes=list(scratch),
        cost_estimate=pl.CostEstimate(flops=flops, bytes_accessed=1 << 20, transcendentals=0),
        compiler_params=pltpu.CompilerParams(vmem_limit_bytes=vmem << 20),
        name=name,
    )


def shards(tables, split_maps, white_noise):
    splits, core_side, _ = split_maps.shape
    half = core_side
    margin = core_side // 2
    length = 2 * core_side
    constant = {k: jnp.asarray(v) for k, v in tables.items() if k != "energy"}
    profile = tables["profile"]
    rows = jnp.asarray(np.ascontiguousarray(np.broadcast_to(profile[:, None], (length, 128))))
    cols = jnp.asarray(np.ascontiguousarray(np.broadcast_to(profile[None, :], (8, length))))
    scale = 1.0 / ((2 * SMOOTH + 1) ** 2 * (splits - 1) * tables["energy"])
    odd_col = lax.axis_index("ra") % 2
    cube = length**3

    piece = jax.ShapeDtypeStruct((splits, margin, margin), BF16)
    strip = jax.ShapeDtypeStruct((splits, margin, half), BF16)
    outer_first, outer_second, first, second = kernel_call(
        functools.partial(cut_kernel, half), "cut", (piece, piece, strip, strip), 1, vmem=8
    )(split_maps)
    outer_first = swap_columns(outer_first, 1)
    second = swap_rows(second, 1)
    first = swap_rows(first, 0)
    spectrum = jax.ShapeDtypeStruct((half + 8, length), F32)
    re, im = kernel_call(
        functools.partial(noise_kernel, half), "noise_spectrum", (spectrum, spectrum), 3, flops=50 * cube
    )(white_noise, constant["left"], constant["right"])

    outer_second, outer_first = lax.optimization_barrier((outer_second, outer_first))
    outer_second = swap_columns(outer_second, 1)

    first, second, _, _, re, im = lax.optimization_barrier((first, second, outer_first, outer_second, re, im))
    first_corner = swap_rows(outer_first, 0)
    second_corner = swap_rows(outer_second, 1)
    inner = swap_columns(
        jnp.concatenate(
            [
                lax.dynamic_slice_in_dim(block, (1 - odd_col) * margin, margin, axis=2)
                for block in (first, split_maps, second)
            ],
            axis=1,
        ),
        0,
    )
    def columns(body, name, count, flops):
        return kernel_call(
            functools.partial(body, half),
            name,
            jax.ShapeDtypeStruct((splits, length + 16, margin), BF16),
            count,
            [pltpu.VMEM((splits, length, margin), BF16)],
            flops=flops,
        )

    left, right = constant["left"], constant["right"]
    core, outer = kernel_call(
        functools.partial(core_kernel, half),
        "core_columns",
        (
            jax.ShapeDtypeStruct((splits, length + 16, length), F32),
            jax.ShapeDtypeStruct((splits, length, margin), BF16),
        ),
        9,
        [pltpu.VMEM((splits, length, half), BF16)],
        flops=cube,
    )(split_maps, first, second, outer_first, outer_second, rows, cols, left, right)
    outer = columns(outer_kernel, "outer_columns", 7, 400000 * cube // 1000)(
        core, outer, first_corner, second_corner, rows, cols, left
    )
    inner = columns(inner_kernel, "inner_columns", 5, cube)(outer, inner, rows, cols, left)

    strip = jax.ShapeDtypeStruct((margin, length), BF16)
    first, second, inside = kernel_call(
        functools.partial(main_kernel, half, scale),
        "tile_model",
        (strip, strip, jax.ShapeDtypeStruct((half, length), F32)),
        11,
        [
            pltpu.VMEM((half, length), BF16),
            pltpu.VMEM((half + 8, length), F32),
            pltpu.VMEM((2, half + 128, length), BF16),
            pltpu.VMEM((half, length), BF16),
        ],
        flops=20 * cube,
    )(
        core, inner, outer, re, im, rows, cols,
        constant["right"], constant["band_rows"], constant["band_columns"],
        constant["inverse_right"],
    )

    second = swap_rows(second, 1)
    first = swap_rows(first, 0)
    column = jax.ShapeDtypeStruct((half, margin), BF16)
    block = jax.ShapeDtypeStruct((half, half), F32)
    center, outer, inner = kernel_call(
        functools.partial(fold_rows_kernel, half), "fold_rows", (block, column, column), 3,
        [pltpu.VMEM((half, length), F32)],
    )(inside, first, second)
    outer = swap_columns(outer, 1)
    inner = swap_columns(inner, 0)
    return kernel_call(functools.partial(fold_columns_kernel, half), "fold_columns", block, 3)(
        center, outer, inner
    )


def solution(mesh):
    tables = host_tables(512)
    placed = (P(None, "dec", "ra"), P("dec", "ra"))
    return jax.shard_map(
        functools.partial(shards, tables), mesh=mesh, in_specs=placed, out_specs=P("dec", "ra"), check_vma=False
    )
```

```python
import functools

import jax
import jax.numpy as jnp
import numpy as np
from jax import lax
from jax.experimental import pallas as pl
from jax.experimental.pallas import tpu as pltpu
from jax.sharding import PartitionSpec as P

import ml_dtypes

SMOOTH = 4
BF16 = jnp.bfloat16
F32 = jnp.float32


def host_tables(length):
    half = length // 2
    index = np.arange(length)
    phase = np.outer(index, index) % length
    cos = np.cos(2 * np.pi * phase / length)
    sin = np.sin(2 * np.pi * phase / length)
    sin[phase % half == 0] = 0.0
    cos = cos.astype(ml_dtypes.bfloat16).astype(np.float64)
    sin = sin.astype(ml_dtypes.bfloat16).astype(np.float64)

    def packed(rows):
        return np.ascontiguousarray(rows).astype(ml_dtypes.bfloat16)

    left = np.zeros((length + 16, length))
    left[:half] = cos[:half]
    left[half:length] = sin[:half]
    left[length] = cos[half]
    right = np.concatenate([cos[:, :half], sin[:, :half]], axis=1)
    right[:, half] = cos[:, half]
    margin = half // 2
    right = np.roll(right, -margin, axis=0)
    right = np.concatenate([right[:half], np.roll(right[half:], margin, axis=0)], axis=0)
    inverse_right = np.concatenate([2 * cos[:half], -2 * sin[:half]], axis=0)
    inverse_right[0] = cos[0]
    inverse_right[half] = cos[half]
    order = np.concatenate([index[:half], [half], -index[1:half]])

    def near(first, second):
        apart = np.abs(first[:, None] - second[None, :]) % length
        return (np.minimum(apart, length - apart) <= SMOOTH).astype(np.float64)

    band_columns = near(order, order)
    band_rows = np.zeros((half + 16, half + 128))
    targets = np.arange(half + 1)
    band_rows[: half + 1, : half + 1] = near(targets, targets)
    first, last = half + 8, half + 16
    band_rows[: half + 1, first + 1 : first + 8] = near(targets, -np.arange(1, 8))
    band_rows[: half + 1, last : last + 8] = near(targets, -np.arange(half - 8, half))
    profile = np.sin(np.pi * (index + 0.5) / length) ** 2
    energy = np.sum(profile**2) ** 2
    return dict(
        left=packed(left),
        right=packed(right),
        inverse_right=packed(inverse_right),
        band_columns=packed(band_columns),
        band_rows=packed(band_rows),
        profile=profile.astype(np.float32),
        energy=float(energy),
    )


def dot(a, b):
    return jnp.dot(a, b, preferred_element_type=F32)


def first_column(shape):
    return lax.broadcasted_iota(jnp.int32, shape, 1) == 0


def two_parts(values):
    high = values.astype(BF16)
    return high, (values - high.astype(F32)).astype(BF16)


def quarters(spectra, half):
    length = 2 * half
    return (
        spectra[:half, :half],
        spectra[:half, half:],
        spectra[half:length, :half],
        spectra[half:length, half:],
        spectra[length : length + 8, :half],
        spectra[length : length + 8, half:],
    )


def noise_kernel(half, noise_ref, left_ref, right_ref, re_ref, im_ref):
    margin = half // 2
    halves = dot(left_ref[...], noise_ref[...]).astype(BF16)
    spectra = (
        dot(halves[:, margin : margin + half], right_ref[:half])
        + dot(halves[:, :margin], right_ref[half : half + margin])
        + dot(halves[:, margin + half :], right_ref[half + margin :])
    )
    cc, cs, sc, ss, nc, ns = quarters(spectra, half)
    edge = first_column((half, half))
    re_ref[:half, :half] = jnp.where(edge, cc, cc - ss)
    re_ref[:half, half:] = jnp.where(edge, cs, cc + ss)
    im_ref[:half, :half] = -jnp.where(edge, sc, cs + sc)
    im_ref[:half, half:] = jnp.where(edge, -ss, cs - sc)
    edge = first_column((8, half))
    re_ref[half : half + 8, :half] = nc
    re_ref[half : half + 8, half:] = jnp.where(edge, ns, nc)
    im_ref[half : half + 8, :half] = jnp.where(edge, 0.0, -ns)
    im_ref[half : half + 8, half:] = jnp.where(edge, 0.0, ns)


def aligned(offset, step):
    return offset if isinstance(offset, int) else pl.multiple_of(offset, step)


def fill(tile, source, rows_ref, cols_ref, source_row, height, row, col, tile_col, exists=None):
    splits, width = source.shape[0], source.shape[2]
    step = 32
    pc = cols_ref[:1, pl.ds(aligned(col, 128), width)]
    if exists is not None:
        pc = pc * exists

    def strip(number, carry):
        start = pl.multiple_of(source_row + number * step, step)
        target = pl.multiple_of(row + number * step, step)
        members = [source[s, pl.ds(start, step), :].astype(F32) for s in range(splits)]
        mean = functools.reduce(lambda a, b: a + b, members) * (1.0 / splits)
        weights = jnp.concatenate([rows_ref[pl.ds(target, step), :]] * (width // 128), axis=1) * pc
        for s in range(splits):
            tile[s, pl.ds(target, step), pl.ds(aligned(tile_col, 128), width)] = (
                weights * (members[s] - mean)
            ).astype(BF16)
        return carry

    lax.fori_loop(0, height // step, strip, 0)


def sides(half):
    far = half + half // 2
    first = jnp.where(lax.axis_index("dec") % 2 == 0, 0, far)
    outer = jnp.where(lax.axis_index("ra") % 2 == 0, 0, far)
    return first, far - first, outer, far - outer


def inside_sky():
    flags = []
    for axis in ("dec", "ra"):
        index = lax.axis_index(axis)
        edge = jnp.logical_or(index == 0, index == lax.axis_size(axis) - 1)
        flags.append(jnp.where(edge, 0.0, 1.0).astype(F32))
    return flags


def cut_kernel(half, maps_ref, outer_first_ref, outer_second_ref, first_ref, second_ref):
    margin = half // 2
    first, second, outer, _ = sides(half)
    columns = pl.ds(pl.multiple_of(jnp.where(outer == 0, 0, margin), margin), margin)
    for piece, strip, place in (
        (outer_first_ref, first_ref, first), (outer_second_ref, second_ref, second)
    ):
        rows = pl.ds(pl.multiple_of(jnp.where(place == 0, 0, margin), margin), margin)
        for s in range(maps_ref.shape[0]):
            piece[s] = maps_ref[s, rows, columns]
            strip[s] = maps_ref[s, rows, :]


def core_kernel(
    half, core_ref, first_ref, second_ref, outer_first_ref, outer_second_ref, rows_ref, cols_ref, left_ref, right_ref,
    spectra_ref, outer_ref, tile,
):
    margin = half // 2
    splits = core_ref.shape[0]
    first, second, outer, _ = sides(half)
    has_first, has_outer = inside_sky()
    fill(tile, core_ref, rows_ref, cols_ref, 0, half, margin, margin, 0)
    fill(tile, first_ref, rows_ref, cols_ref, 0, margin, first, margin, 0, has_first)
    fill(tile, second_ref, rows_ref, cols_ref, 0, margin, second, margin, 0)
    for s in range(splits):
        halves = dot(left_ref[...], tile[s]).astype(BF16)
        spectra_ref[s] = dot(halves, right_ref[:half])
    for source, place in ((outer_first_ref, first), (outer_second_ref, second)):
        row = jnp.where(place == 0, margin, half)
        fill(outer_ref, source, rows_ref, cols_ref, 0, margin, row, outer, 0, has_outer)


def transform_pairs(tile, left_ref, halves_ref):
    splits, _, width = tile.shape
    for s in range(0, splits, 2):
        halves = dot(left_ref[...], jnp.concatenate([tile[s], tile[s + 1]], axis=1)).astype(BF16)
        halves_ref[s] = halves[:, :width]
        halves_ref[s + 1] = halves[:, width:]


def inner_kernel(half, after_ref, inner_ref, rows_ref, cols_ref, left_ref, halves_ref, tile):
    del after_ref
    margin = half // 2
    first, second, _, inner = sides(half)
    has_first, _ = inside_sky()
    fill(tile, inner_ref, rows_ref, cols_ref, 0, margin, first, inner, 0, has_first)
    fill(tile, inner_ref, rows_ref, cols_ref, margin, half, margin, inner, 0)
    fill(tile, inner_ref, rows_ref, cols_ref, margin + half, margin, second, inner, 0)
    transform_pairs(tile, left_ref, halves_ref)


def outer_kernel(
    half, after_ref, tile, first_ref, second_ref, rows_ref, cols_ref, left_ref, halves_ref, full
):
    del after_ref
    margin = half // 2
    first, second, outer, _ = sides(half)
    has_first, has_outer = inside_sky()
    full[:, margin : margin + half, :] = tile[:, margin : margin + half, :]
    fill(full, first_ref, rows_ref, cols_ref, 0, margin, first, outer, 0, has_outer * has_first)
    fill(full, second_ref, rows_ref, cols_ref, 0, margin, second, outer, 0, has_outer)
    transform_pairs(full, left_ref, halves_ref)


def main_kernel(
    half, scale,
    core_ref, inner_ref, outer_ref, re_ref, im_ref,
    rows_ref, cols_ref, right_ref, band_rows_ref, band_columns_ref,
    inverse_right_ref,
    first_out_ref, second_out_ref, inside_ref,
    table, power, stacked, strips,
):
    length = 2 * half
    margin = half // 2
    splits = core_ref.shape[0]
    first, _, _, inner = sides(half)
    place = pl.multiple_of(half + jnp.where(inner == 0, 0, margin), margin)
    table[:margin] = right_ref[pl.ds(place, margin), :]
    table[margin:] = right_ref[pl.ds(pl.multiple_of(length + margin - place, margin), margin), :]

    edge = first_column((half, half))
    edge8 = first_column((8, half))

    def accumulate(s, carry):
        halves = jnp.concatenate([inner_ref[s], outer_ref[s]], axis=1)
        spectra = core_ref[s] + dot(halves, table[...])
        cc, cs, sc, ss, nc, ns = quarters(spectra, half)
        e = jnp.where(edge, cc, cc - ss)
        f = jnp.where(edge, sc, cs + sc)
        g = jnp.where(edge, cs, cc + ss)
        h = jnp.where(edge, ss, cs - sc)
        nc, ns = nc * nc, ns * ns
        terms = (
            e * e + f * f, g * g + h * h, jnp.where(edge8, nc, nc + ns), jnp.where(edge8, ns, nc + ns)
        )
        places = (
            (slice(0, half), slice(0, half)), (slice(0, half), slice(half, length)),
            (slice(half, half + 8), slice(0, half)), (slice(half, half + 8), slice(half, length)),
        )
        for term, place in zip(terms, places):
            power[place] = term if carry else power[place] + term

    accumulate(0, True)
    for s in range(1, splits):
        accumulate(s, False)

    stacked[:, half + 24 :, :] = jnp.zeros((2, stacked.shape[1] - half - 24, length), BF16)
    for part, values in enumerate(two_parts(power[...])):
        stacked[part, : half + 8, :] = values
    for place, start in ((half + 8, 0), (half + 16, half - 8)):
        a = power[start : start + 8, :half]
        b = power[start : start + 8, half:]
        mirrored = jnp.concatenate(
            [jnp.where(edge8, a, b), jnp.where(edge8, b, a)], axis=1
        )
        for part, values in enumerate(two_parts(mirrored)):
            stacked[part, place : place + 8, :] = values
    smooth = (
        dot(band_rows_ref[...], stacked[1]) + dot(band_rows_ref[...], stacked[0])
    )
    high, low = two_parts(smooth)
    smooth = dot(low, band_columns_ref[...]) + dot(high, band_columns_ref[...])
    gain = jnp.sqrt(jnp.maximum(smooth[: half + 8], 0.0) * scale)
    gr = (gain * re_ref[...]).astype(BF16)
    gi = (gain * im_ref[...]).astype(BF16)
    er, fr = gr[:half, :half], gr[:half, half:]
    ei, fi = gi[:half, :half], gi[:half, half:]
    start = lax.broadcasted_iota(jnp.int32, (half, half), 0) == 0
    nyquist_u = gr[half : half + 1, :half]
    nyquist_v = jnp.where(edge8[:1], gr[half : half + 1, half:], gi[half : half + 1, :half])
    zero = jnp.zeros((), BF16)
    near_u = jnp.concatenate([er, jnp.where(start, nyquist_u, -ei)], axis=0)
    far_u = jnp.concatenate(
        [jnp.where(edge, er, fr), -jnp.where(edge, ei, fi)], axis=0
    )
    near_v = jnp.concatenate(
        [jnp.where(edge, fr, ei), jnp.where(start, nyquist_v, jnp.where(edge, -fi, er))], axis=0
    )
    far_v = jnp.concatenate(
        [jnp.where(edge, fr, -fi), -jnp.where(edge, fi, fr)], axis=0
    )
    start = lax.broadcasted_iota(jnp.int32, (length, half), 0) % half == 0
    far_u, far_v = jnp.where(start, zero, far_u), jnp.where(start, zero, far_v)
    u = dot(right_ref[...], near_u) + dot(right_ref[...], far_u)
    v = dot(right_ref[...], near_v) + dot(right_ref[...], far_v)
    joined = jnp.concatenate([u.astype(BF16), v.astype(BF16)], axis=1)
    real_part = dot(joined, inverse_right_ref[...])
    pc = cols_ref[:1, :] * (1.0 / (length * length))

    def windowed(row, place, count):
        profile = jnp.concatenate([rows_ref[row : row + count, :]] * (length // 128), axis=1)
        return profile * pc * real_part[place : place + count]

    inside_ref[...] = windowed(margin, 0, half)
    strips[:margin] = windowed(0, half, margin).astype(BF16)
    strips[margin:] = windowed(margin + half, half + margin, margin).astype(BF16)
    place = pl.multiple_of(jnp.where(first == 0, 0, margin), margin)
    first_out_ref[...] = strips[pl.ds(place, margin), :]
    second_out_ref[...] = strips[pl.ds(pl.multiple_of(margin - place, margin), margin), :]


def fold_rows_kernel(half, inside_ref, first_ref, second_ref, center_ref, outer_ref, inner_ref, total):
    margin = half // 2
    first, second, outer, inner = sides(half)
    has_first, _ = inside_sky()
    for source, place, exists in ((first_ref, first, has_first), (second_ref, second, 1.0)):
        rows = pl.ds(pl.multiple_of(jnp.where(place == 0, 0, margin), margin), margin)
        total[rows, :] = inside_ref[rows, :] + source[...].astype(F32) * exists
    center_ref[...] = total[:, margin : margin + half]
    outer_ref[...] = total[:, pl.ds(pl.multiple_of(outer, margin), margin)].astype(BF16)
    inner_ref[...] = total[:, pl.ds(pl.multiple_of(inner, margin), margin)].astype(BF16)


def fold_columns_kernel(half, center_ref, outer_ref, inner_ref, out_ref):
    margin = half // 2
    _, _, outer, inner = sides(half)
    _, has_outer = inside_sky()
    for source, place, exists in ((outer_ref, outer, has_outer), (inner_ref, inner, 1.0)):
        columns = pl.ds(pl.multiple_of(jnp.where(place == 0, 0, margin), margin), margin)
        out_ref[:, columns] = center_ref[:, columns] + source[...].astype(F32) * exists


def swap_rows(values, offset):
    rows, columns = lax.axis_size("dec"), lax.axis_size("ra")
    pairs = []
    for i in range(rows):
        partner = i + 1 if i % 2 == offset else i - 1
        for j in range(columns):
            target = partner * columns + j if 0 <= partner < rows else i * columns + (j ^ 1)
            pairs.append((i * columns + j, target))
    return lax.ppermute(values, ("dec", "ra"), pairs)


def swap_columns(values, offset):
    count = lax.axis_size("ra")
    pairs = [(i, (i + 1 if i % 2 == offset else i - 1) % count) for i in range(count)]
    return lax.ppermute(values, "ra", pairs)


def whole(count):
    return [pl.BlockSpec(memory_space=pltpu.VMEM)] * count


def kernel_call(body, name, outs, count, scratch=(), flops=0, vmem=16):
    return pl.pallas_call(
        body,
        out_shape=outs,
        in_specs=whole(count),
        out_specs=jax.tree.map(lambda _: pl.BlockSpec(memory_space=pltpu.VMEM), outs),
        scratch_shapes=list(scratch),
        cost_estimate=pl.CostEstimate(flops=flops, bytes_accessed=1 << 20, transcendentals=0),
        compiler_params=pltpu.CompilerParams(vmem_limit_bytes=vmem << 20),
        name=name,
    )


def shards(tables, split_maps, white_noise):
    splits, core_side, _ = split_maps.shape
    half = core_side
    margin = core_side // 2
    length = 2 * core_side
    constant = {k: jnp.asarray(v) for k, v in tables.items() if k != "energy"}
    profile = tables["profile"]
    rows = jnp.asarray(np.ascontiguousarray(np.broadcast_to(profile[:, None], (length, 128))))
    cols = jnp.asarray(np.ascontiguousarray(np.broadcast_to(profile[None, :], (8, length))))
    scale = 1.0 / ((2 * SMOOTH + 1) ** 2 * (splits - 1) * tables["energy"])
    odd_col = lax.axis_index("ra") % 2
    cube = length**3

    piece = jax.ShapeDtypeStruct((splits, margin, margin), BF16)
    strip = jax.ShapeDtypeStruct((splits, margin, half), BF16)
    outer_first, outer_second, first, second = kernel_call(
        functools.partial(cut_kernel, half), "cut", (piece, piece, strip, strip), 1, vmem=8
    )(split_maps)
    outer_first = swap_columns(outer_first, 1)
    second = swap_rows(second, 0)
    first = swap_rows(first, 1)
    outer_second = swap_columns(outer_second, 1)
    spectrum = jax.ShapeDtypeStruct((half + 8, length), F32)
    re, im = kernel_call(
        functools.partial(noise_kernel, half), "noise_spectrum", (spectrum, spectrum), 3, flops=50 * cube
    )(white_noise, constant["left"], constant["right"])

    first, second, _, _, re, im = lax.optimization_barrier((first, second, outer_first, outer_second, re, im))
    first_corner = swap_rows(outer_first, 1)
    second_corner = swap_rows(outer_second, 0)
    inner = swap_columns(
        jnp.concatenate(
            [
                lax.dynamic_slice_in_dim(block, (1 - odd_col) * margin, margin, axis=2)
                for block in (first, split_maps, second)
            ],
            axis=1,
        ),
        0,
    )
    def columns(body, name, count, flops):
        return kernel_call(
            functools.partial(body, half),
            name,
            jax.ShapeDtypeStruct((splits, length + 16, margin), BF16),
            count,
            [pltpu.VMEM((splits, length, margin), BF16)],
            flops=flops,
        )

    left, right = constant["left"], constant["right"]
    core, outer = kernel_call(
        functools.partial(core_kernel, half),
        "core_columns",
        (
            jax.ShapeDtypeStruct((splits, length + 16, length), F32),
            jax.ShapeDtypeStruct((splits, length, margin), BF16),
        ),
        9,
        [pltpu.VMEM((splits, length, half), BF16)],
        flops=cube,
    )(split_maps, first, second, outer_first, outer_second, rows, cols, left, right)
    outer = columns(outer_kernel, "outer_columns", 7, 400000 * cube // 1000)(
        core, outer, first_corner, second_corner, rows, cols, left
    )
    inner = columns(inner_kernel, "inner_columns", 5, cube)(outer, inner, rows, cols, left)

    strip = jax.ShapeDtypeStruct((margin, length), BF16)
    first, second, inside = kernel_call(
        functools.partial(main_kernel, half, scale),
        "tile_model",
        (strip, strip, jax.ShapeDtypeStruct((half, length), F32)),
        11,
        [
            pltpu.VMEM((half, length), BF16),
            pltpu.VMEM((half + 8, length), F32),
            pltpu.VMEM((2, half + 128, length), BF16),
            pltpu.VMEM((half, length), BF16),
        ],
        flops=20 * cube,
    )(
        core, inner, outer, re, im, rows, cols,
        constant["right"], constant["band_rows"], constant["band_columns"],
        constant["inverse_right"],
    )

    second = swap_rows(second, 0)
    first = swap_rows(first, 1)
    column = jax.ShapeDtypeStruct((half, margin), BF16)
    block = jax.ShapeDtypeStruct((half, half), F32)
    center, outer, inner = kernel_call(
        functools.partial(fold_rows_kernel, half), "fold_rows", (block, column, column), 3,
        [pltpu.VMEM((half, length), F32)],
    )(inside, first, second)
    outer = swap_columns(outer, 1)
    inner = swap_columns(inner, 0)
    return kernel_call(functools.partial(fold_columns_kernel, half), "fold_columns", block, 3)(
        center, outer, inner
    )


def solution(mesh):
    tables = host_tables(512)
    placed = (P(None, "dec", "ra"), P("dec", "ra"))
    return jax.shard_map(
        functools.partial(shards, tables), mesh=mesh, in_specs=placed, out_specs=P("dec", "ra"), check_vma=False
    )
```

```python
import functools

import jax
import jax.numpy as jnp
import numpy as np
from jax import lax
from jax.experimental import pallas as pl
from jax.experimental.pallas import tpu as pltpu
from jax.sharding import PartitionSpec as P

import ml_dtypes

SMOOTH = 4
BF16 = jnp.bfloat16
F32 = jnp.float32


def host_tables(length):
    half = length // 2
    index = np.arange(length)
    phase = np.outer(index, index) % length
    cos = np.cos(2 * np.pi * phase / length)
    sin = np.sin(2 * np.pi * phase / length)
    sin[phase % half == 0] = 0.0
    cos = cos.astype(ml_dtypes.bfloat16).astype(np.float64)
    sin = sin.astype(ml_dtypes.bfloat16).astype(np.float64)

    def packed(rows):
        return np.ascontiguousarray(rows).astype(ml_dtypes.bfloat16)

    left = np.zeros((length + 16, length))
    left[:half] = cos[:half]
    left[half:length] = sin[:half]
    left[length] = cos[half]
    right = np.concatenate([cos[:, :half], sin[:, :half]], axis=1)
    right[:, half] = cos[:, half]
    margin = half // 2
    right = np.roll(right, -margin, axis=0)
    right = np.concatenate([right[:half], np.roll(right[half:], margin, axis=0)], axis=0)
    inverse_right = np.concatenate([2 * cos[:half], -2 * sin[:half]], axis=0)
    inverse_right[0] = cos[0]
    inverse_right[half] = cos[half]
    order = np.concatenate([index[:half], [half], -index[1:half]])

    def near(first, second):
        apart = np.abs(first[:, None] - second[None, :]) % length
        return (np.minimum(apart, length - apart) <= SMOOTH).astype(np.float64)

    band_columns = near(order, order)
    band_rows = np.zeros((half + 16, half + 128))
    targets = np.arange(half + 1)
    band_rows[: half + 1, : half + 1] = near(targets, targets)
    first, last = half + 8, half + 16
    band_rows[: half + 1, first + 1 : first + 8] = near(targets, -np.arange(1, 8))
    band_rows[: half + 1, last : last + 8] = near(targets, -np.arange(half - 8, half))
    profile = np.sin(np.pi * (index + 0.5) / length) ** 2
    energy = np.sum(profile**2) ** 2
    return dict(
        left=packed(left),
        right=packed(right),
        inverse_right=packed(inverse_right),
        band_columns=packed(band_columns),
        band_rows=packed(band_rows),
        profile=profile.astype(np.float32),
        energy=float(energy),
    )


def dot(a, b):
    return jnp.dot(a, b, preferred_element_type=F32)


def first_column(shape):
    return lax.broadcasted_iota(jnp.int32, shape, 1) == 0


def two_parts(values):
    high = values.astype(BF16)
    return high, (values - high.astype(F32)).astype(BF16)


def quarters(spectra, half):
    length = 2 * half
    return (
        spectra[:half, :half],
        spectra[:half, half:],
        spectra[half:length, :half],
        spectra[half:length, half:],
        spectra[length : length + 8, :half],
        spectra[length : length + 8, half:],
    )


def noise_kernel(half, noise_ref, left_ref, right_ref, re_ref, im_ref):
    margin = half // 2
    halves = dot(left_ref[...], noise_ref[...]).astype(BF16)
    spectra = (
        dot(halves[:, margin : margin + half], right_ref[:half])
        + dot(halves[:, :margin], right_ref[half : half + margin])
        + dot(halves[:, margin + half :], right_ref[half + margin :])
    )
    cc, cs, sc, ss, nc, ns = quarters(spectra, half)
    edge = first_column((half, half))
    re_ref[:half, :half] = jnp.where(edge, cc, cc - ss)
    re_ref[:half, half:] = jnp.where(edge, cs, cc + ss)
    im_ref[:half, :half] = -jnp.where(edge, sc, cs + sc)
    im_ref[:half, half:] = jnp.where(edge, -ss, cs - sc)
    edge = first_column((8, half))
    re_ref[half : half + 8, :half] = nc
    re_ref[half : half + 8, half:] = jnp.where(edge, ns, nc)
    im_ref[half : half + 8, :half] = jnp.where(edge, 0.0, -ns)
    im_ref[half : half + 8, half:] = jnp.where(edge, 0.0, ns)


def aligned(offset, step):
    return offset if isinstance(offset, int) else pl.multiple_of(offset, step)


def fill(tile, source, rows_ref, cols_ref, source_row, height, row, col, tile_col, exists=None):
    sources = source if isinstance(source, tuple) else (source,)
    planes = [(ref, s) for ref in sources for s in range(ref.shape[0])]
    splits, width = len(planes), sources[0].shape[2]
    step = 32
    pc = cols_ref[:1, pl.ds(aligned(col, 128), width)]
    if exists is not None:
        pc = pc * exists

    def strip(number, carry):
        start = pl.multiple_of(source_row + number * step, step)
        target = pl.multiple_of(row + number * step, step)
        members = [ref[s, pl.ds(start, step), :].astype(F32) for ref, s in planes]
        mean = functools.reduce(lambda a, b: a + b, members) * (1.0 / splits)
        weights = jnp.concatenate([rows_ref[pl.ds(target, step), :]] * (width // 128), axis=1) * pc
        for s in range(splits):
            tile[s, pl.ds(target, step), pl.ds(aligned(tile_col, 128), width)] = (
                weights * (members[s] - mean)
            ).astype(BF16)
        return carry

    lax.fori_loop(0, height // step, strip, 0)


def sides(half):
    far = half + half // 2
    first = jnp.where(lax.axis_index("dec") % 2 == 0, 0, far)
    outer = jnp.where(lax.axis_index("ra") % 2 == 0, 0, far)
    return first, far - first, outer, far - outer


def inside_sky():
    flags = []
    for axis in ("dec", "ra"):
        index = lax.axis_index(axis)
        edge = jnp.logical_or(index == 0, index == lax.axis_size(axis) - 1)
        flags.append(jnp.where(edge, 0.0, 1.0).astype(F32))
    return flags


def cut_kernel(half, maps_ref, outer_first_ref, outer_second_ref, near_ref, far_ref, second_ref):
    margin = half // 2
    first, second, outer, _ = sides(half)
    columns = pl.ds(pl.multiple_of(jnp.where(outer == 0, 0, margin), margin), margin)
    splits, direct = maps_ref.shape[0], near_ref.shape[0]
    for piece, place in ((outer_first_ref, first), (outer_second_ref, second)):
        rows = pl.ds(pl.multiple_of(jnp.where(place == 0, 0, margin), margin), margin)
        for s in range(splits):
            piece[s] = maps_ref[s, rows, columns]
            if piece is outer_second_ref:
                second_ref[s] = maps_ref[s, rows, :]
            elif s < direct:
                near_ref[s] = maps_ref[s, rows, :]
            else:
                far_ref[s - direct] = maps_ref[s, rows, :]


def core_kernel(
    half, core_ref, near_ref, far_ref, second_ref, outer_first_ref, outer_second_ref,
    rows_ref, cols_ref, left_ref, right_ref,
    spectra_ref, outer_ref, tile,
):
    margin = half // 2
    splits = core_ref.shape[0]
    first, second, outer, _ = sides(half)
    has_first, has_outer = inside_sky()
    fill(tile, core_ref, rows_ref, cols_ref, 0, half, margin, margin, 0)
    fill(tile, (near_ref, far_ref), rows_ref, cols_ref, 0, margin, first, margin, 0, has_first)
    fill(tile, second_ref, rows_ref, cols_ref, 0, margin, second, margin, 0)

    def transform(number, carry):
        for s in (2 * number, 2 * number + 1):
            halves = dot(left_ref[...], tile[s]).astype(BF16)
            spectra_ref[s] = dot(halves, right_ref[:half])
        return carry

    lax.fori_loop(0, splits // 2, transform, 0)
    for source, place in ((outer_first_ref, first), (outer_second_ref, second)):
        row = jnp.where(place == 0, margin, half)
        fill(outer_ref, source, rows_ref, cols_ref, 0, margin, row, outer, 0, has_outer)


def transform_pairs(tile, left_ref, halves_ref):
    splits, _, width = tile.shape
    for s in range(0, splits, 2):
        halves = dot(left_ref[...], jnp.concatenate([tile[s], tile[s + 1]], axis=1)).astype(BF16)
        halves_ref[s] = halves[:, :width]
        halves_ref[s + 1] = halves[:, width:]


def inner_kernel(half, after_ref, inner_ref, rows_ref, cols_ref, left_ref, halves_ref, tile):
    del after_ref
    margin = half // 2
    first, second, _, inner = sides(half)
    has_first, _ = inside_sky()
    fill(tile, inner_ref, rows_ref, cols_ref, 0, margin, first, inner, 0, has_first)
    fill(tile, inner_ref, rows_ref, cols_ref, margin, half, margin, inner, 0)
    fill(tile, inner_ref, rows_ref, cols_ref, margin + half, margin, second, inner, 0)
    transform_pairs(tile, left_ref, halves_ref)


def outer_kernel(
    half, after_ref, tile, first_ref, second_ref, rows_ref, cols_ref, left_ref, halves_ref, full
):
    del after_ref
    margin = half // 2
    first, second, outer, _ = sides(half)
    has_first, has_outer = inside_sky()
    full[:, margin : margin + half, :] = tile[:, margin : margin + half, :]
    fill(full, first_ref, rows_ref, cols_ref, 0, margin, first, outer, 0, has_outer * has_first)
    fill(full, second_ref, rows_ref, cols_ref, 0, margin, second, outer, 0, has_outer)
    transform_pairs(full, left_ref, halves_ref)


def main_kernel(
    half, scale,
    core_ref, inner_ref, outer_ref, re_ref, im_ref,
    rows_ref, cols_ref, right_ref, band_rows_ref, band_columns_ref,
    inverse_right_ref,
    first_out_ref, second_out_ref, inside_ref,
    table, power, stacked, strips,
):
    length = 2 * half
    margin = half // 2
    splits = core_ref.shape[0]
    first, _, _, inner = sides(half)
    place = pl.multiple_of(half + jnp.where(inner == 0, 0, margin), margin)
    table[:margin] = right_ref[pl.ds(place, margin), :]
    table[margin:] = right_ref[pl.ds(pl.multiple_of(length + margin - place, margin), margin), :]

    edge = first_column((half, half))
    edge8 = first_column((8, half))

    def accumulate(s, carry):
        halves = jnp.concatenate([inner_ref[s], outer_ref[s]], axis=1)
        spectra = core_ref[s] + dot(halves, table[...])
        cc, cs, sc, ss, nc, ns = quarters(spectra, half)
        e = jnp.where(edge, cc, cc - ss)
        f = jnp.where(edge, sc, cs + sc)
        g = jnp.where(edge, cs, cc + ss)
        h = jnp.where(edge, ss, cs - sc)
        nc, ns = nc * nc, ns * ns
        terms = (
            e * e + f * f, g * g + h * h, jnp.where(edge8, nc, nc + ns), jnp.where(edge8, ns, nc + ns)
        )
        places = (
            (slice(0, half), slice(0, half)), (slice(0, half), slice(half, length)),
            (slice(half, half + 8), slice(0, half)), (slice(half, half + 8), slice(half, length)),
        )
        for term, place in zip(terms, places):
            power[place] = term if carry else power[place] + term

    accumulate(0, True)
    for s in range(1, splits):
        accumulate(s, False)

    stacked[:, half + 24 :, :] = jnp.zeros((2, stacked.shape[1] - half - 24, length), BF16)
    for part, values in enumerate(two_parts(power[...])):
        stacked[part, : half + 8, :] = values
    for place, start in ((half + 8, 0), (half + 16, half - 8)):
        a = power[start : start + 8, :half]
        b = power[start : start + 8, half:]
        mirrored = jnp.concatenate(
            [jnp.where(edge8, a, b), jnp.where(edge8, b, a)], axis=1
        )
        for part, values in enumerate(two_parts(mirrored)):
            stacked[part, place : place + 8, :] = values
    smooth = (
        dot(band_rows_ref[...], stacked[1]) + dot(band_rows_ref[...], stacked[0])
    )
    high, low = two_parts(smooth)
    smooth = dot(low, band_columns_ref[...]) + dot(high, band_columns_ref[...])
    gain = jnp.sqrt(jnp.maximum(smooth[: half + 8], 0.0) * scale)
    gr = (gain * re_ref[...]).astype(BF16)
    gi = (gain * im_ref[...]).astype(BF16)
    er, fr = gr[:half, :half], gr[:half, half:]
    ei, fi = gi[:half, :half], gi[:half, half:]
    start = lax.broadcasted_iota(jnp.int32, (half, half), 0) == 0
    nyquist_u = gr[half : half + 1, :half]
    nyquist_v = jnp.where(edge8[:1], gr[half : half + 1, half:], gi[half : half + 1, :half])
    zero = jnp.zeros((), BF16)
    near_u = jnp.concatenate([er, jnp.where(start, nyquist_u, -ei)], axis=0)
    far_u = jnp.concatenate(
        [jnp.where(edge, er, fr), -jnp.where(edge, ei, fi)], axis=0
    )
    near_v = jnp.concatenate(
        [jnp.where(edge, fr, ei), jnp.where(start, nyquist_v, jnp.where(edge, -fi, er))], axis=0
    )
    far_v = jnp.concatenate(
        [jnp.where(edge, fr, -fi), -jnp.where(edge, fi, fr)], axis=0
    )
    start = lax.broadcasted_iota(jnp.int32, (length, half), 0) % half == 0
    far_u, far_v = jnp.where(start, zero, far_u), jnp.where(start, zero, far_v)
    u = dot(right_ref[...], near_u) + dot(right_ref[...], far_u)
    v = dot(right_ref[...], near_v) + dot(right_ref[...], far_v)
    joined = jnp.concatenate([u.astype(BF16), v.astype(BF16)], axis=1)
    real_part = dot(joined, inverse_right_ref[...])
    pc = cols_ref[:1, :] * (1.0 / (length * length))

    def windowed(row, place, count):
        profile = jnp.concatenate([rows_ref[row : row + count, :]] * (length // 128), axis=1)
        return profile * pc * real_part[place : place + count]

    inside_ref[...] = windowed(margin, 0, half)
    strips[:margin] = windowed(0, half, margin).astype(BF16)
    strips[margin:] = windowed(margin + half, half + margin, margin).astype(BF16)
    place = pl.multiple_of(jnp.where(first == 0, 0, margin), margin)
    first_out_ref[...] = strips[pl.ds(place, margin), :]
    second_out_ref[...] = strips[pl.ds(pl.multiple_of(margin - place, margin), margin), :]


def fold_rows_kernel(half, inside_ref, first_ref, second_ref, center_ref, outer_ref, inner_ref, total):
    margin = half // 2
    first, second, outer, inner = sides(half)
    has_first, _ = inside_sky()
    for source, place, exists in ((first_ref, first, has_first), (second_ref, second, 1.0)):
        rows = pl.ds(pl.multiple_of(jnp.where(place == 0, 0, margin), margin), margin)
        total[rows, :] = inside_ref[rows, :] + source[...].astype(F32) * exists
    center_ref[...] = total[:, margin : margin + half]
    outer_ref[...] = total[:, pl.ds(pl.multiple_of(outer, margin), margin)].astype(BF16)
    inner_ref[...] = total[:, pl.ds(pl.multiple_of(inner, margin), margin)].astype(BF16)


def fold_columns_kernel(half, center_ref, outer_ref, inner_ref, out_ref):
    margin = half // 2
    _, _, outer, inner = sides(half)
    _, has_outer = inside_sky()
    for source, place, exists in ((outer_ref, outer, has_outer), (inner_ref, inner, 1.0)):
        columns = pl.ds(pl.multiple_of(jnp.where(place == 0, 0, margin), margin), margin)
        out_ref[:, columns] = center_ref[:, columns] + source[...].astype(F32) * exists


def partners(offset, side=False):
    rows, columns = lax.axis_size("dec"), lax.axis_size("ra")
    pairs = []
    for i in range(rows):
        partner = i + 1 if i % 2 == offset else i - 1
        for j in range(columns):
            target = (partner, j) if 0 <= partner < rows else (i, j ^ 1)
            if side and i in (rows // 2 - 1, rows // 2):
                target = (partner, j ^ 2)
            pairs.append((i * columns + j, target[0] * columns + target[1]))
    return pairs


def swap_rows(values, offset, side=False):
    return lax.ppermute(values, ("dec", "ra"), partners(offset, side))


def swap_beside(values):
    rows, columns = lax.axis_size("dec"), lax.axis_size("ra")
    pairs = []
    for i in range(rows):
        flip = 2 if i in (rows // 2 - 1, rows // 2) else 1
        pairs += [(i * columns + j, i * columns + (j ^ flip)) for j in range(columns)]
    return lax.ppermute(values, ("dec", "ra"), pairs)


def swap_columns(values, offset):
    count = lax.axis_size("ra")
    pairs = [(i, (i + 1 if i % 2 == offset else i - 1) % count) for i in range(count)]
    return lax.ppermute(values, "ra", pairs)


def whole(count):
    return [pl.BlockSpec(memory_space=pltpu.VMEM)] * count


def kernel_call(body, name, outs, count, scratch=(), flops=0, vmem=16):
    return pl.pallas_call(
        body,
        out_shape=outs,
        in_specs=whole(count),
        out_specs=jax.tree.map(lambda _: pl.BlockSpec(memory_space=pltpu.VMEM), outs),
        scratch_shapes=list(scratch),
        cost_estimate=pl.CostEstimate(flops=flops, bytes_accessed=1 << 20, transcendentals=0),
        compiler_params=pltpu.CompilerParams(vmem_limit_bytes=vmem << 20),
        name=name,
    )


def shards(tables, split_maps, white_noise):
    splits, core_side, _ = split_maps.shape
    half = core_side
    margin = core_side // 2
    length = 2 * core_side
    constant = {k: jnp.asarray(v) for k, v in tables.items() if k != "energy"}
    profile = tables["profile"]
    rows = jnp.asarray(np.ascontiguousarray(np.broadcast_to(profile[:, None], (length, 128))))
    cols = jnp.asarray(np.ascontiguousarray(np.broadcast_to(profile[None, :], (8, length))))
    scale = 1.0 / ((2 * SMOOTH + 1) ** 2 * (splits - 1) * tables["energy"])
    odd_col = lax.axis_index("ra") % 2
    cube = length**3

    piece = jax.ShapeDtypeStruct((splits, margin, margin), BF16)
    strip = jax.ShapeDtypeStruct((splits, margin, half), BF16)
    share = jax.ShapeDtypeStruct((splits // 2, margin, half), BF16)
    outer_first, outer_second, near, far, second = kernel_call(
        functools.partial(cut_kernel, half), "cut", (piece, piece, share, share, strip), 1, vmem=8
    )(split_maps)
    outer_first = swap_columns(outer_first, 1)
    second = swap_rows(second, 0)
    row = lax.axis_index("dec")
    middle = lax.axis_size("dec") // 2
    beside = swap_beside(far)
    near = swap_rows(near, 1)
    far = swap_rows(jnp.where(jnp.logical_or(row == middle - 1, row == middle), beside, far), 1, side=True)
    outer_second = swap_columns(outer_second, 1)

    spectrum = jax.ShapeDtypeStruct((half + 8, length), F32)
    re, im = kernel_call(
        functools.partial(noise_kernel, half), "noise_spectrum", (spectrum, spectrum), 3, flops=50 * cube
    )(white_noise, constant["left"], constant["right"])

    near, far, second, _, _, re, im = lax.optimization_barrier(
        (near, far, second, outer_first, outer_second, re, im)
    )
    first_corner = swap_rows(outer_first, 1)
    second_corner = swap_rows(outer_second, 0)
    inner = swap_columns(
        jnp.concatenate(
            [
                lax.dynamic_slice_in_dim(block, (1 - odd_col) * margin, margin, axis=2)
                for block in (jnp.concatenate([near, far], axis=0), split_maps, second)
            ],
            axis=1,
        ),
        0,
    )
    def columns(body, name, count, flops):
        return kernel_call(
            functools.partial(body, half),
            name,
            jax.ShapeDtypeStruct((splits, length + 16, margin), BF16),
            count,
            [pltpu.VMEM((splits, length, margin), BF16)],
            flops=flops,
        )

    left, right = constant["left"], constant["right"]
    core, outer = kernel_call(
        functools.partial(core_kernel, half),
        "core_columns",
        (
            jax.ShapeDtypeStruct((splits, length + 16, length), F32),
            jax.ShapeDtypeStruct((splits, length, margin), BF16),
        ),
        10,
        [pltpu.VMEM((splits, length, half), BF16)],
        flops=cube,
    )(split_maps, near, far, second, outer_first, outer_second, rows, cols, left, right)
    outer = columns(outer_kernel, "outer_columns", 7, 400000 * cube // 1000)(
        core, outer, first_corner, second_corner, rows, cols, left
    )
    inner = columns(inner_kernel, "inner_columns", 5, cube)(outer, inner, rows, cols, left)

    strip = jax.ShapeDtypeStruct((margin, length), BF16)
    first, second, inside = kernel_call(
        functools.partial(main_kernel, half, scale),
        "tile_model",
        (strip, strip, jax.ShapeDtypeStruct((half, length), F32)),
        11,
        [
            pltpu.VMEM((half, length), BF16),
            pltpu.VMEM((half + 8, length), F32),
            pltpu.VMEM((2, half + 128, length), BF16),
            pltpu.VMEM((half, length), BF16),
        ],
        flops=20 * cube,
    )(
        core, inner, outer, re, im, rows, cols,
        constant["right"], constant["band_rows"], constant["band_columns"],
        constant["inverse_right"],
    )

    second = swap_rows(second, 0)
    first = swap_rows(first, 1)
    column = jax.ShapeDtypeStruct((half, margin), BF16)
    block = jax.ShapeDtypeStruct((half, half), F32)
    center, outer, inner = kernel_call(
        functools.partial(fold_rows_kernel, half), "fold_rows", (block, column, column), 3,
        [pltpu.VMEM((half, length), F32)],
    )(inside, first, second)
    outer = swap_columns(outer, 1)
    inner = swap_columns(inner, 0)
    return kernel_call(functools.partial(fold_columns_kernel, half), "fold_columns", block, 3)(
        center, outer, inner
    )


def solution(mesh):
    tables = host_tables(512)
    placed = (P(None, "dec", "ra"), P("dec", "ra"))
    return jax.shard_map(
        functools.partial(shards, tables), mesh=mesh, in_specs=placed, out_specs=P("dec", "ra"), check_vma=False
    )
```

```python
import functools

import jax
import jax.numpy as jnp
import numpy as np
from jax import lax
from jax.experimental import pallas as pl
from jax.experimental.pallas import tpu as pltpu
from jax.sharding import PartitionSpec as P

import ml_dtypes

SMOOTH = 4
BF16 = jnp.bfloat16
F32 = jnp.float32


def host_tables(length):
    half = length // 2
    index = np.arange(length)
    phase = np.outer(index, index) % length
    cos = np.cos(2 * np.pi * phase / length)
    sin = np.sin(2 * np.pi * phase / length)
    sin[phase % half == 0] = 0.0
    cos = cos.astype(ml_dtypes.bfloat16).astype(np.float64)
    sin = sin.astype(ml_dtypes.bfloat16).astype(np.float64)

    def packed(rows):
        return np.ascontiguousarray(rows).astype(ml_dtypes.bfloat16)

    left = np.zeros((length + 16, length))
    left[:half] = cos[:half]
    left[half:length] = sin[:half]
    left[length] = cos[half]
    right = np.concatenate([cos[:, :half], sin[:, :half]], axis=1)
    right[:, half] = cos[:, half]
    margin = half // 2
    right = np.roll(right, -margin, axis=0)
    right = np.concatenate([right[:half], np.roll(right[half:], margin, axis=0)], axis=0)
    inverse_right = np.concatenate([2 * cos[:half], -2 * sin[:half]], axis=0)
    inverse_right[0] = cos[0]
    inverse_right[half] = cos[half]
    order = np.concatenate([index[:half], [half], -index[1:half]])

    def near(first, second):
        apart = np.abs(first[:, None] - second[None, :]) % length
        return (np.minimum(apart, length - apart) <= SMOOTH).astype(np.float64)

    band_columns = near(order, order)
    band_rows = np.zeros((half + 16, half + 128))
    targets = np.arange(half + 1)
    band_rows[: half + 1, : half + 1] = near(targets, targets)
    first, last = half + 8, half + 16
    band_rows[: half + 1, first + 1 : first + 8] = near(targets, -np.arange(1, 8))
    band_rows[: half + 1, last : last + 8] = near(targets, -np.arange(half - 8, half))
    profile = np.sin(np.pi * (index + 0.5) / length) ** 2
    energy = np.sum(profile**2) ** 2
    return dict(
        left=packed(left),
        right=packed(right),
        inverse_right=packed(inverse_right),
        band_columns=packed(band_columns),
        band_rows=packed(band_rows),
        profile=profile.astype(np.float32),
        energy=float(energy),
    )


def dot(a, b):
    return jnp.dot(a, b, preferred_element_type=F32)


def first_column(shape):
    return lax.broadcasted_iota(jnp.int32, shape, 1) == 0


def two_parts(values):
    high = values.astype(BF16)
    return high, (values - high.astype(F32)).astype(BF16)


def quarters(spectra, half):
    length = 2 * half
    return (
        spectra[:half, :half],
        spectra[:half, half:],
        spectra[half:length, :half],
        spectra[half:length, half:],
        spectra[length : length + 8, :half],
        spectra[length : length + 8, half:],
    )


def noise_kernel(half, noise_ref, left_ref, right_ref, re_ref, im_ref):
    margin = half // 2
    halves = dot(left_ref[...], noise_ref[...]).astype(BF16)
    spectra = (
        dot(halves[:, margin : margin + half], right_ref[:half])
        + dot(halves[:, :margin], right_ref[half : half + margin])
        + dot(halves[:, margin + half :], right_ref[half + margin :])
    )
    cc, cs, sc, ss, nc, ns = quarters(spectra, half)
    edge = first_column((half, half))
    re_ref[:half, :half] = jnp.where(edge, cc, cc - ss)
    re_ref[:half, half:] = jnp.where(edge, cs, cc + ss)
    im_ref[:half, :half] = -jnp.where(edge, sc, cs + sc)
    im_ref[:half, half:] = jnp.where(edge, -ss, cs - sc)
    edge = first_column((8, half))
    re_ref[half : half + 8, :half] = nc
    re_ref[half : half + 8, half:] = jnp.where(edge, ns, nc)
    im_ref[half : half + 8, :half] = jnp.where(edge, 0.0, -ns)
    im_ref[half : half + 8, half:] = jnp.where(edge, 0.0, ns)


def aligned(offset, step):
    return offset if isinstance(offset, int) else pl.multiple_of(offset, step)


def fill(tile, source, rows_ref, cols_ref, source_row, height, row, col, tile_col, exists=None):
    sources = source if isinstance(source, tuple) else (source,)
    planes = [(ref, s) for ref in sources for s in range(ref.shape[0])]
    splits, width = len(planes), sources[0].shape[2]
    step = 32
    pc = cols_ref[:1, pl.ds(aligned(col, 128), width)]
    if exists is not None:
        pc = pc * exists

    def strip(number, carry):
        start = pl.multiple_of(source_row + number * step, step)
        target = pl.multiple_of(row + number * step, step)
        members = [ref[s, pl.ds(start, step), :].astype(F32) for ref, s in planes]
        mean = functools.reduce(lambda a, b: a + b, members) * (1.0 / splits)
        weights = jnp.concatenate([rows_ref[pl.ds(target, step), :]] * (width // 128), axis=1) * pc
        for s in range(splits):
            tile[s, pl.ds(target, step), pl.ds(aligned(tile_col, 128), width)] = (
                weights * (members[s] - mean)
            ).astype(BF16)
        return carry

    lax.fori_loop(0, height // step, strip, 0)


def sides(half):
    far = half + half // 2
    first = jnp.where(lax.axis_index("dec") % 2 == 0, 0, far)
    outer = jnp.where(lax.axis_index("ra") % 2 == 0, 0, far)
    return first, far - first, outer, far - outer


def inside_sky():
    flags = []
    for axis in ("dec", "ra"):
        index = lax.axis_index(axis)
        edge = jnp.logical_or(index == 0, index == lax.axis_size(axis) - 1)
        flags.append(jnp.where(edge, 0.0, 1.0).astype(F32))
    return flags


def cut_kernel(half, maps_ref, outer_first_ref, outer_second_ref, near_ref, far_ref, second_ref):
    margin = half // 2
    first, second, outer, _ = sides(half)
    columns = pl.ds(pl.multiple_of(jnp.where(outer == 0, 0, margin), margin), margin)
    splits, direct = maps_ref.shape[0], near_ref.shape[0]
    for piece, place in ((outer_first_ref, first), (outer_second_ref, second)):
        rows = pl.ds(pl.multiple_of(jnp.where(place == 0, 0, margin), margin), margin)
        for s in range(splits):
            piece[s] = maps_ref[s, rows, columns]
            if piece is outer_second_ref:
                second_ref[s] = maps_ref[s, rows, :]
            elif s < direct:
                near_ref[s] = maps_ref[s, rows, :]
            else:
                far_ref[s - direct] = maps_ref[s, rows, :]


def core_kernel(
    half, core_ref, near_ref, far_ref, second_ref, outer_first_ref, outer_second_ref,
    rows_ref, cols_ref, left_ref, right_ref,
    spectra_ref, outer_ref, tile,
):
    margin = half // 2
    splits = core_ref.shape[0]
    first, second, outer, _ = sides(half)
    has_first, has_outer = inside_sky()
    fill(tile, core_ref, rows_ref, cols_ref, 0, half, margin, margin, 0)
    fill(tile, (near_ref, far_ref), rows_ref, cols_ref, 0, margin, first, margin, 0, has_first)
    fill(tile, second_ref, rows_ref, cols_ref, 0, margin, second, margin, 0)

    def transform(number, carry):
        for s in (2 * number, 2 * number + 1):
            halves = dot(left_ref[...], tile[s]).astype(BF16)
            spectra_ref[s] = dot(halves, right_ref[:half])
        return carry

    lax.fori_loop(0, splits // 2, transform, 0)
    for source, place in ((outer_first_ref, first), (outer_second_ref, second)):
        row = jnp.where(place == 0, margin, half)
        fill(outer_ref, source, rows_ref, cols_ref, 0, margin, row, outer, 0, has_outer)


def transform_pairs(tile, left_ref, halves_ref):
    splits, _, width = tile.shape
    for s in range(0, splits, 2):
        halves = dot(left_ref[...], jnp.concatenate([tile[s], tile[s + 1]], axis=1)).astype(BF16)
        halves_ref[s] = halves[:, :width]
        halves_ref[s + 1] = halves[:, width:]


def inner_kernel(half, after_ref, inner_ref, rows_ref, cols_ref, left_ref, halves_ref, tile):
    del after_ref
    margin = half // 2
    first, second, _, inner = sides(half)
    has_first, _ = inside_sky()
    fill(tile, inner_ref, rows_ref, cols_ref, 0, margin, first, inner, 0, has_first)
    fill(tile, inner_ref, rows_ref, cols_ref, margin, half, margin, inner, 0)
    fill(tile, inner_ref, rows_ref, cols_ref, margin + half, margin, second, inner, 0)
    transform_pairs(tile, left_ref, halves_ref)


def outer_kernel(
    half, after_ref, tile, first_ref, second_ref, rows_ref, cols_ref, left_ref, halves_ref, full
):
    del after_ref
    margin = half // 2
    first, second, outer, _ = sides(half)
    has_first, has_outer = inside_sky()
    full[:, margin : margin + half, :] = tile[:, margin : margin + half, :]
    fill(full, first_ref, rows_ref, cols_ref, 0, margin, first, outer, 0, has_outer * has_first)
    fill(full, second_ref, rows_ref, cols_ref, 0, margin, second, outer, 0, has_outer)
    transform_pairs(full, left_ref, halves_ref)


def main_kernel(
    half, scale,
    core_ref, inner_ref, outer_ref, re_ref, im_ref,
    rows_ref, cols_ref, right_ref, band_rows_ref, band_columns_ref,
    inverse_right_ref,
    first_out_ref, second_out_ref, inside_ref,
    table, power, stacked, strips,
):
    length = 2 * half
    margin = half // 2
    splits = core_ref.shape[0]
    first, _, _, inner = sides(half)
    place = pl.multiple_of(half + jnp.where(inner == 0, 0, margin), margin)
    table[:margin] = right_ref[pl.ds(place, margin), :]
    table[margin:] = right_ref[pl.ds(pl.multiple_of(length + margin - place, margin), margin), :]

    edge = first_column((half, half))
    edge8 = first_column((8, half))

    def accumulate(s, carry):
        halves = jnp.concatenate([inner_ref[s], outer_ref[s]], axis=1)
        spectra = core_ref[s] + dot(halves, table[...])
        cc, cs, sc, ss, nc, ns = quarters(spectra, half)
        e = jnp.where(edge, cc, cc - ss)
        f = jnp.where(edge, sc, cs + sc)
        g = jnp.where(edge, cs, cc + ss)
        h = jnp.where(edge, ss, cs - sc)
        nc, ns = nc * nc, ns * ns
        terms = (
            e * e + f * f, g * g + h * h, jnp.where(edge8, nc, nc + ns), jnp.where(edge8, ns, nc + ns)
        )
        places = (
            (slice(0, half), slice(0, half)), (slice(0, half), slice(half, length)),
            (slice(half, half + 8), slice(0, half)), (slice(half, half + 8), slice(half, length)),
        )
        for term, place in zip(terms, places):
            power[place] = term if carry else power[place] + term

    accumulate(0, True)
    for s in range(1, splits):
        accumulate(s, False)

    stacked[:, half + 24 :, :] = jnp.zeros((2, stacked.shape[1] - half - 24, length), BF16)
    for part, values in enumerate(two_parts(power[...])):
        stacked[part, : half + 8, :] = values
    for place, start in ((half + 8, 0), (half + 16, half - 8)):
        a = power[start : start + 8, :half]
        b = power[start : start + 8, half:]
        mirrored = jnp.concatenate(
            [jnp.where(edge8, a, b), jnp.where(edge8, b, a)], axis=1
        )
        for part, values in enumerate(two_parts(mirrored)):
            stacked[part, place : place + 8, :] = values
    smooth = (
        dot(band_rows_ref[...], stacked[1]) + dot(band_rows_ref[...], stacked[0])
    )
    high, low = two_parts(smooth)
    smooth = dot(low, band_columns_ref[...]) + dot(high, band_columns_ref[...])
    gain = jnp.sqrt(jnp.maximum(smooth[: half + 8], 0.0) * scale)
    gr = (gain * re_ref[...]).astype(BF16)
    gi = (gain * im_ref[...]).astype(BF16)
    er, fr = gr[:half, :half], gr[:half, half:]
    ei, fi = gi[:half, :half], gi[:half, half:]
    start = lax.broadcasted_iota(jnp.int32, (half, half), 0) == 0
    nyquist_u = gr[half : half + 1, :half]
    nyquist_v = jnp.where(edge8[:1], gr[half : half + 1, half:], gi[half : half + 1, :half])
    zero = jnp.zeros((), BF16)
    near_u = jnp.concatenate([er, jnp.where(start, nyquist_u, -ei)], axis=0)
    far_u = jnp.concatenate(
        [jnp.where(edge, er, fr), -jnp.where(edge, ei, fi)], axis=0
    )
    near_v = jnp.concatenate(
        [jnp.where(edge, fr, ei), jnp.where(start, nyquist_v, jnp.where(edge, -fi, er))], axis=0
    )
    far_v = jnp.concatenate(
        [jnp.where(edge, fr, -fi), -jnp.where(edge, fi, fr)], axis=0
    )
    start = lax.broadcasted_iota(jnp.int32, (length, half), 0) % half == 0
    far_u, far_v = jnp.where(start, zero, far_u), jnp.where(start, zero, far_v)
    u = dot(right_ref[...], near_u) + dot(right_ref[...], far_u)
    v = dot(right_ref[...], near_v) + dot(right_ref[...], far_v)
    joined = jnp.concatenate([u.astype(BF16), v.astype(BF16)], axis=1)
    real_part = dot(joined, inverse_right_ref[...])
    pc = cols_ref[:1, :] * (1.0 / (length * length))

    def windowed(row, place, count):
        profile = jnp.concatenate([rows_ref[row : row + count, :]] * (length // 128), axis=1)
        return profile * pc * real_part[place : place + count]

    inside_ref[...] = windowed(margin, 0, half)
    strips[:margin] = windowed(0, half, margin).astype(BF16)
    strips[margin:] = windowed(margin + half, half + margin, margin).astype(BF16)
    place = pl.multiple_of(jnp.where(first == 0, 0, margin), margin)
    first_out_ref[...] = strips[pl.ds(place, margin), :]
    second_out_ref[...] = strips[pl.ds(pl.multiple_of(margin - place, margin), margin), :]


def fold_rows_kernel(half, inside_ref, first_ref, second_ref, center_ref, outer_ref, inner_ref, total):
    margin = half // 2
    first, second, outer, inner = sides(half)
    has_first, _ = inside_sky()
    for source, place, exists in ((first_ref, first, has_first), (second_ref, second, 1.0)):
        rows = pl.ds(pl.multiple_of(jnp.where(place == 0, 0, margin), margin), margin)
        total[rows, :] = inside_ref[rows, :] + source[...].astype(F32) * exists
    center_ref[...] = total[:, margin : margin + half]
    outer_ref[...] = total[:, pl.ds(pl.multiple_of(outer, margin), margin)].astype(BF16)
    inner_ref[...] = total[:, pl.ds(pl.multiple_of(inner, margin), margin)].astype(BF16)


def fold_columns_kernel(half, center_ref, outer_ref, inner_ref, out_ref):
    margin = half // 2
    _, _, outer, inner = sides(half)
    _, has_outer = inside_sky()
    for source, place, exists in ((outer_ref, outer, has_outer), (inner_ref, inner, 1.0)):
        columns = pl.ds(pl.multiple_of(jnp.where(place == 0, 0, margin), margin), margin)
        out_ref[:, columns] = center_ref[:, columns] + source[...].astype(F32) * exists


def partners(offset, side=False):
    rows, columns = lax.axis_size("dec"), lax.axis_size("ra")
    pairs = []
    for i in range(rows):
        partner = i + 1 if i % 2 == offset else i - 1
        for j in range(columns):
            target = (partner, j) if 0 <= partner < rows else (i, j ^ 1)
            if side and i in (rows // 2 - 1, rows // 2):
                target = (partner, j ^ 2)
            pairs.append((i * columns + j, target[0] * columns + target[1]))
    return pairs


def swap_rows(values, offset, side=False):
    return lax.ppermute(values, ("dec", "ra"), partners(offset, side))


def swap_beside(values):
    rows, columns = lax.axis_size("dec"), lax.axis_size("ra")
    pairs = []
    for i in range(rows):
        flip = 2 if i in (rows // 2 - 1, rows // 2) else 1
        pairs += [(i * columns + j, i * columns + (j ^ flip)) for j in range(columns)]
    return lax.ppermute(values, ("dec", "ra"), pairs)


def swap_columns(values, offset):
    count = lax.axis_size("ra")
    pairs = [(i, (i + 1 if i % 2 == offset else i - 1) % count) for i in range(count)]
    return lax.ppermute(values, "ra", pairs)


def whole(count):
    return [pl.BlockSpec(memory_space=pltpu.VMEM)] * count


def kernel_call(body, name, outs, count, scratch=(), flops=0, vmem=16):
    return pl.pallas_call(
        body,
        out_shape=outs,
        in_specs=whole(count),
        out_specs=jax.tree.map(lambda _: pl.BlockSpec(memory_space=pltpu.VMEM), outs),
        scratch_shapes=list(scratch),
        cost_estimate=pl.CostEstimate(flops=flops, bytes_accessed=1 << 20, transcendentals=0),
        compiler_params=pltpu.CompilerParams(vmem_limit_bytes=vmem << 20),
        name=name,
    )


def shards(tables, split_maps, white_noise):
    splits, core_side, _ = split_maps.shape
    half = core_side
    margin = core_side // 2
    length = 2 * core_side
    constant = {k: jnp.asarray(v) for k, v in tables.items() if k != "energy"}
    profile = tables["profile"]
    rows = jnp.asarray(np.ascontiguousarray(np.broadcast_to(profile[:, None], (length, 128))))
    cols = jnp.asarray(np.ascontiguousarray(np.broadcast_to(profile[None, :], (8, length))))
    scale = 1.0 / ((2 * SMOOTH + 1) ** 2 * (splits - 1) * tables["energy"])
    odd_col = lax.axis_index("ra") % 2
    cube = length**3

    piece = jax.ShapeDtypeStruct((splits, margin, margin), BF16)
    strip = jax.ShapeDtypeStruct((splits, margin, half), BF16)
    share = jax.ShapeDtypeStruct((splits // 2, margin, half), BF16)
    outer_first, outer_second, near, far, second = kernel_call(
        functools.partial(cut_kernel, half), "cut", (piece, piece, share, share, strip), 1, vmem=8
    )(split_maps)
    outer_first = swap_columns(outer_first, 1)
    second = swap_rows(second, 0)
    row = lax.axis_index("dec")
    middle = lax.axis_size("dec") // 2
    beside = swap_beside(far)
    near = swap_rows(near, 1)
    outer_second = swap_columns(outer_second, 1)

    spectrum = jax.ShapeDtypeStruct((half + 8, length), F32)
    re, im = kernel_call(
        functools.partial(noise_kernel, half), "noise_spectrum", (spectrum, spectrum), 3, flops=50 * cube
    )(white_noise, constant["left"], constant["right"])
    beside, re, im = lax.optimization_barrier((beside, re, im))
    far = swap_rows(jnp.where(jnp.logical_or(row == middle - 1, row == middle), beside, far), 1, side=True)

    near, far, second, _, _, re, im = lax.optimization_barrier(
        (near, far, second, outer_first, outer_second, re, im)
    )
    first_corner = swap_rows(outer_first, 1)
    second_corner = swap_rows(outer_second, 0)
    inner = swap_columns(
        jnp.concatenate(
            [
                lax.dynamic_slice_in_dim(block, (1 - odd_col) * margin, margin, axis=2)
                for block in (jnp.concatenate([near, far], axis=0), split_maps, second)
            ],
            axis=1,
        ),
        0,
    )
    def columns(body, name, count, flops):
        return kernel_call(
            functools.partial(body, half),
            name,
            jax.ShapeDtypeStruct((splits, length + 16, margin), BF16),
            count,
            [pltpu.VMEM((splits, length, margin), BF16)],
            flops=flops,
        )

    left, right = constant["left"], constant["right"]
    core, outer = kernel_call(
        functools.partial(core_kernel, half),
        "core_columns",
        (
            jax.ShapeDtypeStruct((splits, length + 16, length), F32),
            jax.ShapeDtypeStruct((splits, length, margin), BF16),
        ),
        10,
        [pltpu.VMEM((splits, length, half), BF16)],
        flops=cube,
    )(split_maps, near, far, second, outer_first, outer_second, rows, cols, left, right)
    outer = columns(outer_kernel, "outer_columns", 7, 400000 * cube // 1000)(
        core, outer, first_corner, second_corner, rows, cols, left
    )
    inner = columns(inner_kernel, "inner_columns", 5, cube)(outer, inner, rows, cols, left)

    strip = jax.ShapeDtypeStruct((margin, length), BF16)
    first, second, inside = kernel_call(
        functools.partial(main_kernel, half, scale),
        "tile_model",
        (strip, strip, jax.ShapeDtypeStruct((half, length), F32)),
        11,
        [
            pltpu.VMEM((half, length), BF16),
            pltpu.VMEM((half + 8, length), F32),
            pltpu.VMEM((2, half + 128, length), BF16),
            pltpu.VMEM((half, length), BF16),
        ],
        flops=20 * cube,
    )(
        core, inner, outer, re, im, rows, cols,
        constant["right"], constant["band_rows"], constant["band_columns"],
        constant["inverse_right"],
    )

    second = swap_rows(second, 0)
    first = swap_rows(first, 1)
    column = jax.ShapeDtypeStruct((half, margin), BF16)
    block = jax.ShapeDtypeStruct((half, half), F32)
    center, outer, inner = kernel_call(
        functools.partial(fold_rows_kernel, half), "fold_rows", (block, column, column), 3,
        [pltpu.VMEM((half, length), F32)],
    )(inside, first, second)
    outer = swap_columns(outer, 1)
    inner = swap_columns(inner, 0)
    return kernel_call(functools.partial(fold_columns_kernel, half), "fold_columns", block, 3)(
        center, outer, inner
    )


def solution(mesh):
    tables = host_tables(512)
    placed = (P(None, "dec", "ra"), P("dec", "ra"))
    return jax.shard_map(
        functools.partial(shards, tables), mesh=mesh, in_specs=placed, out_specs=P("dec", "ra"), check_vma=False
    )
```

```python
import functools

import jax
import jax.numpy as jnp
import numpy as np
from jax import lax
from jax.experimental import pallas as pl
from jax.experimental.pallas import tpu as pltpu
from jax.sharding import PartitionSpec as P

import ml_dtypes

SMOOTH = 4
BF16 = jnp.bfloat16
F32 = jnp.float32


def host_tables(length):
    half = length // 2
    index = np.arange(length)
    phase = np.outer(index, index) % length
    cos = np.cos(2 * np.pi * phase / length)
    sin = np.sin(2 * np.pi * phase / length)
    sin[phase % half == 0] = 0.0
    cos = cos.astype(ml_dtypes.bfloat16).astype(np.float64)
    sin = sin.astype(ml_dtypes.bfloat16).astype(np.float64)

    def packed(rows):
        return np.ascontiguousarray(rows).astype(ml_dtypes.bfloat16)

    left = np.zeros((length + 16, length))
    left[:half] = cos[:half]
    left[half:length] = sin[:half]
    left[length] = cos[half]
    right = np.concatenate([cos[:, :half], sin[:, :half]], axis=1)
    right[:, half] = cos[:, half]
    margin = half // 2
    right = np.roll(right, -margin, axis=0)
    right = np.concatenate([right[:half], np.roll(right[half:], margin, axis=0)], axis=0)
    inverse_right = np.concatenate([2 * cos[:half], -2 * sin[:half]], axis=0)
    inverse_right[0] = cos[0]
    inverse_right[half] = cos[half]
    order = np.concatenate([index[:half], [half], -index[1:half]])

    def near(first, second):
        apart = np.abs(first[:, None] - second[None, :]) % length
        return (np.minimum(apart, length - apart) <= SMOOTH).astype(np.float64)

    band_columns = near(order, order)
    band_rows = np.zeros((half + 16, half + 128))
    targets = np.arange(half + 1)
    band_rows[: half + 1, : half + 1] = near(targets, targets)
    first, last = half + 8, half + 16
    band_rows[: half + 1, first + 1 : first + 8] = near(targets, -np.arange(1, 8))
    band_rows[: half + 1, last : last + 8] = near(targets, -np.arange(half - 8, half))
    profile = np.sin(np.pi * (index + 0.5) / length) ** 2
    energy = np.sum(profile**2) ** 2
    return dict(
        left=packed(left),
        right=packed(right),
        inverse_right=packed(inverse_right),
        band_columns=packed(band_columns),
        band_rows=packed(band_rows),
        profile=profile.astype(np.float32),
        energy=float(energy),
    )


def dot(a, b):
    return jnp.dot(a, b, preferred_element_type=F32)


def first_column(shape):
    return lax.broadcasted_iota(jnp.int32, shape, 1) == 0


def two_parts(values):
    high = values.astype(BF16)
    return high, (values - high.astype(F32)).astype(BF16)


def quarters(spectra, half):
    length = 2 * half
    return (
        spectra[:half, :half],
        spectra[:half, half:],
        spectra[half:length, :half],
        spectra[half:length, half:],
        spectra[length : length + 8, :half],
        spectra[length : length + 8, half:],
    )


def noise_kernel(half, noise_ref, left_ref, right_ref, re_ref, im_ref):
    margin = half // 2
    halves = dot(left_ref[...], noise_ref[...]).astype(BF16)
    spectra = (
        dot(halves[:, margin : margin + half], right_ref[:half])
        + dot(halves[:, :margin], right_ref[half : half + margin])
        + dot(halves[:, margin + half :], right_ref[half + margin :])
    )
    cc, cs, sc, ss, nc, ns = quarters(spectra, half)
    edge = first_column((half, half))
    re_ref[:half, :half] = jnp.where(edge, cc, cc - ss)
    re_ref[:half, half:] = jnp.where(edge, cs, cc + ss)
    im_ref[:half, :half] = -jnp.where(edge, sc, cs + sc)
    im_ref[:half, half:] = jnp.where(edge, -ss, cs - sc)
    edge = first_column((8, half))
    re_ref[half : half + 8, :half] = nc
    re_ref[half : half + 8, half:] = jnp.where(edge, ns, nc)
    im_ref[half : half + 8, :half] = jnp.where(edge, 0.0, -ns)
    im_ref[half : half + 8, half:] = jnp.where(edge, 0.0, ns)


def aligned(offset, step):
    return offset if isinstance(offset, int) else pl.multiple_of(offset, step)


def fill(tile, source, rows_ref, cols_ref, source_row, height, row, col, tile_col, exists=None):
    sources = source if isinstance(source, tuple) else (source,)
    planes = [(ref, s) for ref in sources for s in range(ref.shape[0])]
    splits, width = len(planes), sources[0].shape[2]
    step = 32
    pc = cols_ref[:1, pl.ds(aligned(col, 128), width)]
    if exists is not None:
        pc = pc * exists

    def strip(number, carry):
        start = pl.multiple_of(source_row + number * step, step)
        target = pl.multiple_of(row + number * step, step)
        members = [ref[s, pl.ds(start, step), :].astype(F32) for ref, s in planes]
        mean = functools.reduce(lambda a, b: a + b, members) * (1.0 / splits)
        weights = jnp.concatenate([rows_ref[pl.ds(target, step), :]] * (width // 128), axis=1) * pc
        for s in range(splits):
            tile[s, pl.ds(target, step), pl.ds(aligned(tile_col, 128), width)] = (
                weights * (members[s] - mean)
            ).astype(BF16)
        return carry

    lax.fori_loop(0, height // step, strip, 0)


def sides(half):
    far = half + half // 2
    first = jnp.where(lax.axis_index("dec") % 2 == 0, 0, far)
    outer = jnp.where(lax.axis_index("ra") % 2 == 0, 0, far)
    return first, far - first, outer, far - outer


def inside_sky():
    flags = []
    for axis in ("dec", "ra"):
        index = lax.axis_index(axis)
        edge = jnp.logical_or(index == 0, index == lax.axis_size(axis) - 1)
        flags.append(jnp.where(edge, 0.0, 1.0).astype(F32))
    return flags


def cut_kernel(half, maps_ref, outer_first_ref, outer_second_ref, near_ref, far_ref, second_ref):
    margin = half // 2
    first, second, outer, _ = sides(half)
    columns = pl.ds(pl.multiple_of(jnp.where(outer == 0, 0, margin), margin), margin)
    splits, direct = maps_ref.shape[0], near_ref.shape[0]
    for piece, place in ((outer_first_ref, first), (outer_second_ref, second)):
        rows = pl.ds(pl.multiple_of(jnp.where(place == 0, 0, margin), margin), margin)
        for s in range(splits):
            piece[s] = maps_ref[s, rows, columns]
            if piece is outer_second_ref:
                second_ref[s] = maps_ref[s, rows, :]
            elif s < direct:
                near_ref[s] = maps_ref[s, rows, :]
            else:
                far_ref[s - direct] = maps_ref[s, rows, :]


def core_kernel(
    half, core_ref, near_ref, far_ref, second_ref, outer_first_ref, outer_second_ref,
    rows_ref, cols_ref, left_ref, right_ref,
    spectra_ref, outer_ref, tile,
):
    margin = half // 2
    splits = core_ref.shape[0]
    first, second, outer, _ = sides(half)
    has_first, has_outer = inside_sky()
    fill(tile, core_ref, rows_ref, cols_ref, 0, half, margin, margin, 0)
    fill(tile, (near_ref, far_ref), rows_ref, cols_ref, 0, margin, first, margin, 0, has_first)
    fill(tile, second_ref, rows_ref, cols_ref, 0, margin, second, margin, 0)

    def transform(number, carry):
        for s in (2 * number, 2 * number + 1):
            halves = dot(left_ref[...], tile[s]).astype(BF16)
            spectra_ref[s] = dot(halves, right_ref[:half])
        return carry

    lax.fori_loop(0, splits // 2, transform, 0)
    for source, place in ((outer_first_ref, first), (outer_second_ref, second)):
        row = jnp.where(place == 0, margin, half)
        fill(outer_ref, source, rows_ref, cols_ref, 0, margin, row, outer, 0, has_outer)


def transform_pairs(tile, left_ref, halves_ref):
    splits, _, width = tile.shape
    for s in range(0, splits, 2):
        halves = dot(left_ref[...], jnp.concatenate([tile[s], tile[s + 1]], axis=1)).astype(BF16)
        halves_ref[s] = halves[:, :width]
        halves_ref[s + 1] = halves[:, width:]


def inner_kernel(half, after_ref, inner_ref, rows_ref, cols_ref, left_ref, halves_ref, tile):
    del after_ref
    margin = half // 2
    first, second, _, inner = sides(half)
    has_first, _ = inside_sky()
    fill(tile, inner_ref, rows_ref, cols_ref, 0, margin, first, inner, 0, has_first)
    fill(tile, inner_ref, rows_ref, cols_ref, margin, half, margin, inner, 0)
    fill(tile, inner_ref, rows_ref, cols_ref, margin + half, margin, second, inner, 0)
    transform_pairs(tile, left_ref, halves_ref)


def outer_kernel(
    half, after_ref, tile, first_ref, second_ref, rows_ref, cols_ref, left_ref, halves_ref, full
):
    del after_ref
    margin = half // 2
    first, second, outer, _ = sides(half)
    has_first, has_outer = inside_sky()
    full[:, margin : margin + half, :] = tile[:, margin : margin + half, :]
    fill(full, first_ref, rows_ref, cols_ref, 0, margin, first, outer, 0, has_outer * has_first)
    fill(full, second_ref, rows_ref, cols_ref, 0, margin, second, outer, 0, has_outer)
    transform_pairs(full, left_ref, halves_ref)


def main_kernel(
    half, scale,
    core_ref, inner_ref, outer_ref, re_ref, im_ref,
    rows_ref, cols_ref, right_ref, band_rows_ref, band_columns_ref,
    inverse_right_ref,
    first_out_ref, second_out_ref, inside_ref,
    table, power, stacked, strips,
):
    length = 2 * half
    margin = half // 2
    splits = core_ref.shape[0]
    first, _, _, inner = sides(half)
    place = pl.multiple_of(half + jnp.where(inner == 0, 0, margin), margin)
    table[:margin] = right_ref[pl.ds(place, margin), :]
    table[margin:] = right_ref[pl.ds(pl.multiple_of(length + margin - place, margin), margin), :]

    edge = first_column((half, half))
    edge8 = first_column((8, half))

    def accumulate(s, carry):
        halves = jnp.concatenate([inner_ref[s], outer_ref[s]], axis=1)
        spectra = core_ref[s] + dot(halves, table[...])
        cc, cs, sc, ss, nc, ns = quarters(spectra, half)
        e = jnp.where(edge, cc, cc - ss)
        f = jnp.where(edge, sc, cs + sc)
        g = jnp.where(edge, cs, cc + ss)
        h = jnp.where(edge, ss, cs - sc)
        nc, ns = nc * nc, ns * ns
        terms = (
            e * e + f * f, g * g + h * h, jnp.where(edge8, nc, nc + ns), jnp.where(edge8, ns, nc + ns)
        )
        places = (
            (slice(0, half), slice(0, half)), (slice(0, half), slice(half, length)),
            (slice(half, half + 8), slice(0, half)), (slice(half, half + 8), slice(half, length)),
        )
        for term, place in zip(terms, places):
            power[place] = term if carry else power[place] + term

    accumulate(0, True)
    for s in range(1, splits):
        accumulate(s, False)

    stacked[:, half + 24 :, :] = jnp.zeros((2, stacked.shape[1] - half - 24, length), BF16)
    for part, values in enumerate(two_parts(power[...])):
        stacked[part, : half + 8, :] = values
    for place, start in ((half + 8, 0), (half + 16, half - 8)):
        a = power[start : start + 8, :half]
        b = power[start : start + 8, half:]
        mirrored = jnp.concatenate(
            [jnp.where(edge8, a, b), jnp.where(edge8, b, a)], axis=1
        )
        for part, values in enumerate(two_parts(mirrored)):
            stacked[part, place : place + 8, :] = values
    smooth = (
        dot(band_rows_ref[...], stacked[1]) + dot(band_rows_ref[...], stacked[0])
    )
    high, low = two_parts(smooth)
    smooth = dot(low, band_columns_ref[...]) + dot(high, band_columns_ref[...])
    gain = jnp.sqrt(jnp.maximum(smooth[: half + 8], 0.0) * scale)
    gr = (gain * re_ref[...]).astype(BF16)
    gi = (gain * im_ref[...]).astype(BF16)
    er, fr = gr[:half, :half], gr[:half, half:]
    ei, fi = gi[:half, :half], gi[:half, half:]
    start = lax.broadcasted_iota(jnp.int32, (half, half), 0) == 0
    nyquist_u = gr[half : half + 1, :half]
    nyquist_v = jnp.where(edge8[:1], gr[half : half + 1, half:], gi[half : half + 1, :half])
    zero = jnp.zeros((), BF16)
    near_u = jnp.concatenate([er, jnp.where(start, nyquist_u, -ei)], axis=0)
    far_u = jnp.concatenate(
        [jnp.where(edge, er, fr), -jnp.where(edge, ei, fi)], axis=0
    )
    near_v = jnp.concatenate(
        [jnp.where(edge, fr, ei), jnp.where(start, nyquist_v, jnp.where(edge, -fi, er))], axis=0
    )
    far_v = jnp.concatenate(
        [jnp.where(edge, fr, -fi), -jnp.where(edge, fi, fr)], axis=0
    )
    start = lax.broadcasted_iota(jnp.int32, (length, half), 0) % half == 0
    far_u, far_v = jnp.where(start, zero, far_u), jnp.where(start, zero, far_v)
    u = dot(right_ref[...], near_u) + dot(right_ref[...], far_u)
    v = dot(right_ref[...], near_v) + dot(right_ref[...], far_v)
    joined = jnp.concatenate([u.astype(BF16), v.astype(BF16)], axis=1)
    real_part = dot(joined, inverse_right_ref[...])
    pc = cols_ref[:1, :] * (1.0 / (length * length))

    def windowed(row, place, count):
        profile = jnp.concatenate([rows_ref[row : row + count, :]] * (length // 128), axis=1)
        return profile * pc * real_part[place : place + count]

    inside_ref[...] = windowed(margin, 0, half)
    strips[:margin] = windowed(0, half, margin).astype(BF16)
    strips[margin:] = windowed(margin + half, half + margin, margin).astype(BF16)
    place = pl.multiple_of(jnp.where(first == 0, 0, margin), margin)
    first_out_ref[...] = strips[pl.ds(place, margin), :]
    second_out_ref[...] = strips[pl.ds(pl.multiple_of(margin - place, margin), margin), :]


def fold_rows_kernel(half, inside_ref, first_ref, second_ref, center_ref, outer_ref, inner_ref, total):
    margin = half // 2
    first, second, outer, inner = sides(half)
    has_first, _ = inside_sky()
    for source, place, exists in ((first_ref, first, has_first), (second_ref, second, 1.0)):
        rows = pl.ds(pl.multiple_of(jnp.where(place == 0, 0, margin), margin), margin)
        total[rows, :] = inside_ref[rows, :] + source[...].astype(F32) * exists
    center_ref[...] = total[:, margin : margin + half]
    outer_ref[...] = total[:, pl.ds(pl.multiple_of(outer, margin), margin)].astype(BF16)
    inner_ref[...] = total[:, pl.ds(pl.multiple_of(inner, margin), margin)].astype(BF16)


def fold_columns_kernel(half, center_ref, outer_ref, inner_ref, out_ref):
    margin = half // 2
    _, _, outer, inner = sides(half)
    _, has_outer = inside_sky()
    for source, place, exists in ((outer_ref, outer, has_outer), (inner_ref, inner, 1.0)):
        columns = pl.ds(pl.multiple_of(jnp.where(place == 0, 0, margin), margin), margin)
        out_ref[:, columns] = center_ref[:, columns] + source[...].astype(F32) * exists


def partners(offset, side=False):
    rows, columns = lax.axis_size("dec"), lax.axis_size("ra")
    pairs = []
    for i in range(rows):
        partner = i + 1 if i % 2 == offset else i - 1
        for j in range(columns):
            target = (partner, j) if 0 <= partner < rows else (i, j ^ 1)
            if side and i in (rows // 2 - 1, rows // 2):
                target = (partner, j ^ 2)
            pairs.append((i * columns + j, target[0] * columns + target[1]))
    return pairs


def swap_rows(values, offset, side=False):
    return lax.ppermute(values, ("dec", "ra"), partners(offset, side))


def swap_beside(values):
    rows, columns = lax.axis_size("dec"), lax.axis_size("ra")
    pairs = []
    for i in range(rows):
        flip = 2 if i in (rows // 2 - 1, rows // 2) else 1
        pairs += [(i * columns + j, i * columns + (j ^ flip)) for j in range(columns)]
    return lax.ppermute(values, ("dec", "ra"), pairs)


def swap_columns(values, offset):
    count = lax.axis_size("ra")
    pairs = [(i, (i + 1 if i % 2 == offset else i - 1) % count) for i in range(count)]
    return lax.ppermute(values, "ra", pairs)


def whole(count):
    return [pl.BlockSpec(memory_space=pltpu.VMEM)] * count


def kernel_call(body, name, outs, count, scratch=(), flops=0, vmem=16):
    return pl.pallas_call(
        body,
        out_shape=outs,
        in_specs=whole(count),
        out_specs=jax.tree.map(lambda _: pl.BlockSpec(memory_space=pltpu.VMEM), outs),
        scratch_shapes=list(scratch),
        cost_estimate=pl.CostEstimate(flops=flops, bytes_accessed=1 << 20, transcendentals=0),
        compiler_params=pltpu.CompilerParams(vmem_limit_bytes=vmem << 20),
        name=name,
    )


def shards(tables, split_maps, white_noise):
    splits, core_side, _ = split_maps.shape
    half = core_side
    margin = core_side // 2
    length = 2 * core_side
    constant = {k: jnp.asarray(v) for k, v in tables.items() if k != "energy"}
    profile = tables["profile"]
    rows = jnp.asarray(np.ascontiguousarray(np.broadcast_to(profile[:, None], (length, 128))))
    cols = jnp.asarray(np.ascontiguousarray(np.broadcast_to(profile[None, :], (8, length))))
    scale = 1.0 / ((2 * SMOOTH + 1) ** 2 * (splits - 1) * tables["energy"])
    odd_col = lax.axis_index("ra") % 2
    cube = length**3

    piece = jax.ShapeDtypeStruct((splits, margin, margin), BF16)
    strip = jax.ShapeDtypeStruct((splits, margin, half), BF16)
    aside = splits // 3
    direct = jax.ShapeDtypeStruct((splits - aside, margin, half), BF16)
    aside = jax.ShapeDtypeStruct((aside, margin, half), BF16)
    outer_first, outer_second, near, far, second = kernel_call(
        functools.partial(cut_kernel, half), "cut", (piece, piece, direct, aside, strip), 1, vmem=8
    )(split_maps)
    outer_first = swap_columns(outer_first, 1)
    second = swap_rows(second, 0)
    row = lax.axis_index("dec")
    middle = lax.axis_size("dec") // 2
    beside = swap_beside(far)
    near = swap_rows(near, 1)
    far = swap_rows(jnp.where(jnp.logical_or(row == middle - 1, row == middle), beside, far), 1, side=True)
    outer_second = swap_columns(outer_second, 1)

    spectrum = jax.ShapeDtypeStruct((half + 8, length), F32)
    re, im = kernel_call(
        functools.partial(noise_kernel, half), "noise_spectrum", (spectrum, spectrum), 3, flops=50 * cube
    )(white_noise, constant["left"], constant["right"])

    near, far, second, _, _, re, im = lax.optimization_barrier(
        (near, far, second, outer_first, outer_second, re, im)
    )
    first_corner = swap_rows(outer_first, 1)
    second_corner = swap_rows(outer_second, 0)
    inner = swap_columns(
        jnp.concatenate(
            [
                lax.dynamic_slice_in_dim(block, (1 - odd_col) * margin, margin, axis=2)
                for block in (jnp.concatenate([near, far], axis=0), split_maps, second)
            ],
            axis=1,
        ),
        0,
    )
    def columns(body, name, count, flops):
        return kernel_call(
            functools.partial(body, half),
            name,
            jax.ShapeDtypeStruct((splits, length + 16, margin), BF16),
            count,
            [pltpu.VMEM((splits, length, margin), BF16)],
            flops=flops,
        )

    left, right = constant["left"], constant["right"]
    core, outer = kernel_call(
        functools.partial(core_kernel, half),
        "core_columns",
        (
            jax.ShapeDtypeStruct((splits, length + 16, length), F32),
            jax.ShapeDtypeStruct((splits, length, margin), BF16),
        ),
        10,
        [pltpu.VMEM((splits, length, half), BF16)],
        flops=cube,
    )(split_maps, near, far, second, outer_first, outer_second, rows, cols, left, right)
    outer = columns(outer_kernel, "outer_columns", 7, 400000 * cube // 1000)(
        core, outer, first_corner, second_corner, rows, cols, left
    )
    inner = columns(inner_kernel, "inner_columns", 5, cube)(outer, inner, rows, cols, left)

    strip = jax.ShapeDtypeStruct((margin, length), BF16)
    first, second, inside = kernel_call(
        functools.partial(main_kernel, half, scale),
        "tile_model",
        (strip, strip, jax.ShapeDtypeStruct((half, length), F32)),
        11,
        [
            pltpu.VMEM((half, length), BF16),
            pltpu.VMEM((half + 8, length), F32),
            pltpu.VMEM((2, half + 128, length), BF16),
            pltpu.VMEM((half, length), BF16),
        ],
        flops=20 * cube,
    )(
        core, inner, outer, re, im, rows, cols,
        constant["right"], constant["band_rows"], constant["band_columns"],
        constant["inverse_right"],
    )

    second = swap_rows(second, 0)
    first = swap_rows(first, 1)
    column = jax.ShapeDtypeStruct((half, margin), BF16)
    block = jax.ShapeDtypeStruct((half, half), F32)
    center, outer, inner = kernel_call(
        functools.partial(fold_rows_kernel, half), "fold_rows", (block, column, column), 3,
        [pltpu.VMEM((half, length), F32)],
    )(inside, first, second)
    outer = swap_columns(outer, 1)
    inner = swap_columns(inner, 0)
    return kernel_call(functools.partial(fold_columns_kernel, half), "fold_columns", block, 3)(
        center, outer, inner
    )


def solution(mesh):
    tables = host_tables(512)
    placed = (P(None, "dec", "ra"), P("dec", "ra"))
    return jax.shard_map(
        functools.partial(shards, tables), mesh=mesh, in_specs=placed, out_specs=P("dec", "ra"), check_vma=False
    )
```

```python
import functools

import jax
import jax.numpy as jnp
import numpy as np
from jax import lax
from jax.experimental import pallas as pl
from jax.experimental.pallas import tpu as pltpu
from jax.sharding import PartitionSpec as P

import ml_dtypes

SMOOTH = 4
BF16 = jnp.bfloat16
F32 = jnp.float32


def host_tables(length):
    half = length // 2
    index = np.arange(length)
    phase = np.outer(index, index) % length
    cos = np.cos(2 * np.pi * phase / length)
    sin = np.sin(2 * np.pi * phase / length)
    sin[phase % half == 0] = 0.0
    cos = cos.astype(ml_dtypes.bfloat16).astype(np.float64)
    sin = sin.astype(ml_dtypes.bfloat16).astype(np.float64)

    def packed(rows):
        return np.ascontiguousarray(rows).astype(ml_dtypes.bfloat16)

    left = np.zeros((length + 16, length))
    left[:half] = cos[:half]
    left[half:length] = sin[:half]
    left[length] = cos[half]
    right = np.concatenate([cos[:, :half], sin[:, :half]], axis=1)
    right[:, half] = cos[:, half]
    margin = half // 2
    right = np.roll(right, -margin, axis=0)
    right = np.concatenate([right[:half], np.roll(right[half:], margin, axis=0)], axis=0)
    inverse_right = np.concatenate([2 * cos[:half], -2 * sin[:half]], axis=0)
    inverse_right[0] = cos[0]
    inverse_right[half] = cos[half]
    order = np.concatenate([index[:half], [half], -index[1:half]])

    def near(first, second):
        apart = np.abs(first[:, None] - second[None, :]) % length
        return (np.minimum(apart, length - apart) <= SMOOTH).astype(np.float64)

    band_columns = near(order, order)
    band_rows = np.zeros((half + 16, half + 128))
    targets = np.arange(half + 1)
    band_rows[: half + 1, : half + 1] = near(targets, targets)
    first, last = half + 8, half + 16
    band_rows[: half + 1, first + 1 : first + 8] = near(targets, -np.arange(1, 8))
    band_rows[: half + 1, last : last + 8] = near(targets, -np.arange(half - 8, half))
    profile = np.sin(np.pi * (index + 0.5) / length) ** 2
    energy = np.sum(profile**2) ** 2
    return dict(
        left=packed(left),
        right=packed(right),
        inverse_right=packed(inverse_right),
        band_columns=packed(band_columns),
        band_rows=packed(band_rows),
        profile=profile.astype(np.float32),
        energy=float(energy),
    )


def dot(a, b):
    return jnp.dot(a, b, preferred_element_type=F32)


def first_column(shape):
    return lax.broadcasted_iota(jnp.int32, shape, 1) == 0


def two_parts(values):
    high = values.astype(BF16)
    return high, (values - high.astype(F32)).astype(BF16)


def quarters(spectra, half):
    length = 2 * half
    return (
        spectra[:half, :half],
        spectra[:half, half:],
        spectra[half:length, :half],
        spectra[half:length, half:],
        spectra[length : length + 8, :half],
        spectra[length : length + 8, half:],
    )


def noise_kernel(half, noise_ref, left_ref, right_ref, re_ref, im_ref):
    margin = half // 2
    halves = dot(left_ref[...], noise_ref[...]).astype(BF16)
    spectra = (
        dot(halves[:, margin : margin + half], right_ref[:half])
        + dot(halves[:, :margin], right_ref[half : half + margin])
        + dot(halves[:, margin + half :], right_ref[half + margin :])
    )
    cc, cs, sc, ss, nc, ns = quarters(spectra, half)
    edge = first_column((half, half))
    re_ref[:half, :half] = jnp.where(edge, cc, cc - ss)
    re_ref[:half, half:] = jnp.where(edge, cs, cc + ss)
    im_ref[:half, :half] = -jnp.where(edge, sc, cs + sc)
    im_ref[:half, half:] = jnp.where(edge, -ss, cs - sc)
    edge = first_column((8, half))
    re_ref[half : half + 8, :half] = nc
    re_ref[half : half + 8, half:] = jnp.where(edge, ns, nc)
    im_ref[half : half + 8, :half] = jnp.where(edge, 0.0, -ns)
    im_ref[half : half + 8, half:] = jnp.where(edge, 0.0, ns)


def aligned(offset, step):
    return offset if isinstance(offset, int) else pl.multiple_of(offset, step)


def fill(tile, source, rows_ref, cols_ref, source_row, height, row, col, tile_col, exists=None):
    sources = source if isinstance(source, tuple) else (source,)
    planes = [(ref, s) for ref in sources for s in range(ref.shape[0])]
    splits, width = len(planes), sources[0].shape[2]
    step = 32
    pc = cols_ref[:1, pl.ds(aligned(col, 128), width)]
    if exists is not None:
        pc = pc * exists

    def strip(number, carry):
        start = pl.multiple_of(source_row + number * step, step)
        target = pl.multiple_of(row + number * step, step)
        members = [ref[s, pl.ds(start, step), :].astype(F32) for ref, s in planes]
        mean = functools.reduce(lambda a, b: a + b, members) * (1.0 / splits)
        weights = jnp.concatenate([rows_ref[pl.ds(target, step), :]] * (width // 128), axis=1) * pc
        for s in range(splits):
            tile[s, pl.ds(target, step), pl.ds(aligned(tile_col, 128), width)] = (
                weights * (members[s] - mean)
            ).astype(BF16)
        return carry

    lax.fori_loop(0, height // step, strip, 0)


def sides(half):
    far = half + half // 2
    first = jnp.where(lax.axis_index("dec") % 2 == 0, 0, far)
    outer = jnp.where(lax.axis_index("ra") % 2 == 0, 0, far)
    return first, far - first, outer, far - outer


def inside_sky():
    flags = []
    for axis in ("dec", "ra"):
        index = lax.axis_index(axis)
        edge = jnp.logical_or(index == 0, index == lax.axis_size(axis) - 1)
        flags.append(jnp.where(edge, 0.0, 1.0).astype(F32))
    return flags


def cut_kernel(half, maps_ref, outer_first_ref, outer_second_ref, near_ref, far_ref, second_ref):
    margin = half // 2
    first, second, outer, _ = sides(half)
    columns = pl.ds(pl.multiple_of(jnp.where(outer == 0, 0, margin), margin), margin)
    splits, direct = maps_ref.shape[0], near_ref.shape[0]
    for piece, place in ((outer_first_ref, first), (outer_second_ref, second)):
        rows = pl.ds(pl.multiple_of(jnp.where(place == 0, 0, margin), margin), margin)
        for s in range(splits):
            piece[s] = maps_ref[s, rows, columns]
            if piece is outer_second_ref:
                second_ref[s] = maps_ref[s, rows, :]
            elif s < direct:
                near_ref[s] = maps_ref[s, rows, :]
            else:
                far_ref[s - direct] = maps_ref[s, rows, :]


def core_kernel(
    half, core_ref, near_ref, far_ref, second_ref, outer_first_ref, outer_second_ref,
    rows_ref, cols_ref, left_ref, right_ref,
    spectra_ref, outer_ref, tile,
):
    margin = half // 2
    splits = core_ref.shape[0]
    first, second, outer, _ = sides(half)
    has_first, has_outer = inside_sky()
    fill(tile, core_ref, rows_ref, cols_ref, 0, half, margin, margin, 0)
    fill(tile, (near_ref, far_ref), rows_ref, cols_ref, 0, margin, first, margin, 0, has_first)
    fill(tile, second_ref, rows_ref, cols_ref, 0, margin, second, margin, 0)

    def transform(number, carry):
        for s in (2 * number, 2 * number + 1):
            halves = dot(left_ref[...], tile[s]).astype(BF16)
            spectra_ref[s] = dot(halves, right_ref[:half])
        return carry

    lax.fori_loop(0, splits // 2, transform, 0)
    for source, place in ((outer_first_ref, first), (outer_second_ref, second)):
        row = jnp.where(place == 0, margin, half)
        fill(outer_ref, source, rows_ref, cols_ref, 0, margin, row, outer, 0, has_outer)


def transform_pairs(tile, left_ref, halves_ref):
    splits, _, width = tile.shape
    for s in range(0, splits, 2):
        halves = dot(left_ref[...], jnp.concatenate([tile[s], tile[s + 1]], axis=1)).astype(BF16)
        halves_ref[s] = halves[:, :width]
        halves_ref[s + 1] = halves[:, width:]


def inner_kernel(half, after_ref, inner_ref, rows_ref, cols_ref, left_ref, halves_ref, tile):
    del after_ref
    margin = half // 2
    first, second, _, inner = sides(half)
    has_first, _ = inside_sky()
    fill(tile, inner_ref, rows_ref, cols_ref, 0, margin, first, inner, 0, has_first)
    fill(tile, inner_ref, rows_ref, cols_ref, margin, half, margin, inner, 0)
    fill(tile, inner_ref, rows_ref, cols_ref, margin + half, margin, second, inner, 0)
    transform_pairs(tile, left_ref, halves_ref)


def outer_kernel(
    half, after_ref, tile, first_ref, second_ref, rows_ref, cols_ref, left_ref, halves_ref, full
):
    del after_ref
    margin = half // 2
    first, second, outer, _ = sides(half)
    has_first, has_outer = inside_sky()
    full[:, margin : margin + half, :] = tile[:, margin : margin + half, :]
    fill(full, first_ref, rows_ref, cols_ref, 0, margin, first, outer, 0, has_outer * has_first)
    fill(full, second_ref, rows_ref, cols_ref, 0, margin, second, outer, 0, has_outer)
    transform_pairs(full, left_ref, halves_ref)


def main_kernel(
    half, scale,
    core_ref, inner_ref, outer_ref, re_ref, im_ref,
    rows_ref, cols_ref, right_ref, band_rows_ref, band_columns_ref,
    inverse_right_ref,
    first_out_ref, second_out_ref, inside_ref,
    table, power, stacked, strips,
):
    length = 2 * half
    margin = half // 2
    splits = core_ref.shape[0]
    first, _, _, inner = sides(half)
    place = pl.multiple_of(half + jnp.where(inner == 0, 0, margin), margin)
    table[:margin] = right_ref[pl.ds(place, margin), :]
    table[margin:] = right_ref[pl.ds(pl.multiple_of(length + margin - place, margin), margin), :]

    edge = first_column((half, half))
    edge8 = first_column((8, half))

    def accumulate(s, carry):
        halves = jnp.concatenate([inner_ref[s], outer_ref[s]], axis=1)
        spectra = core_ref[s] + dot(halves, table[...])
        cc, cs, sc, ss, nc, ns = quarters(spectra, half)
        e = jnp.where(edge, cc, cc - ss)
        f = jnp.where(edge, sc, cs + sc)
        g = jnp.where(edge, cs, cc + ss)
        h = jnp.where(edge, ss, cs - sc)
        nc, ns = nc * nc, ns * ns
        terms = (
            e * e + f * f, g * g + h * h, jnp.where(edge8, nc, nc + ns), jnp.where(edge8, ns, nc + ns)
        )
        places = (
            (slice(0, half), slice(0, half)), (slice(0, half), slice(half, length)),
            (slice(half, half + 8), slice(0, half)), (slice(half, half + 8), slice(half, length)),
        )
        for term, place in zip(terms, places):
            power[place] = term if carry else power[place] + term

    accumulate(0, True)
    for s in range(1, splits):
        accumulate(s, False)

    stacked[:, half + 24 :, :] = jnp.zeros((2, stacked.shape[1] - half - 24, length), BF16)
    for part, values in enumerate(two_parts(power[...])):
        stacked[part, : half + 8, :] = values
    for place, start in ((half + 8, 0), (half + 16, half - 8)):
        a = power[start : start + 8, :half]
        b = power[start : start + 8, half:]
        mirrored = jnp.concatenate(
            [jnp.where(edge8, a, b), jnp.where(edge8, b, a)], axis=1
        )
        for part, values in enumerate(two_parts(mirrored)):
            stacked[part, place : place + 8, :] = values
    smooth = (
        dot(band_rows_ref[...], stacked[1]) + dot(band_rows_ref[...], stacked[0])
    )
    high, low = two_parts(smooth)
    smooth = dot(low, band_columns_ref[...]) + dot(high, band_columns_ref[...])
    gain = jnp.sqrt(jnp.maximum(smooth[: half + 8], 0.0) * scale)
    gr = (gain * re_ref[...]).astype(BF16)
    gi = (gain * im_ref[...]).astype(BF16)
    er, fr = gr[:half, :half], gr[:half, half:]
    ei, fi = gi[:half, :half], gi[:half, half:]
    start = lax.broadcasted_iota(jnp.int32, (half, half), 0) == 0
    nyquist_u = gr[half : half + 1, :half]
    nyquist_v = jnp.where(edge8[:1], gr[half : half + 1, half:], gi[half : half + 1, :half])
    zero = jnp.zeros((), BF16)
    near_u = jnp.concatenate([er, jnp.where(start, nyquist_u, -ei)], axis=0)
    far_u = jnp.concatenate(
        [jnp.where(edge, er, fr), -jnp.where(edge, ei, fi)], axis=0
    )
    near_v = jnp.concatenate(
        [jnp.where(edge, fr, ei), jnp.where(start, nyquist_v, jnp.where(edge, -fi, er))], axis=0
    )
    far_v = jnp.concatenate(
        [jnp.where(edge, fr, -fi), -jnp.where(edge, fi, fr)], axis=0
    )
    start = lax.broadcasted_iota(jnp.int32, (length, half), 0) % half == 0
    far_u, far_v = jnp.where(start, zero, far_u), jnp.where(start, zero, far_v)
    u = dot(right_ref[...], near_u) + dot(right_ref[...], far_u)
    v = dot(right_ref[...], near_v) + dot(right_ref[...], far_v)
    joined = jnp.concatenate([u.astype(BF16), v.astype(BF16)], axis=1)
    real_part = dot(joined, inverse_right_ref[...])
    pc = cols_ref[:1, :] * (1.0 / (length * length))

    def windowed(row, place, count):
        profile = jnp.concatenate([rows_ref[row : row + count, :]] * (length // 128), axis=1)
        return profile * pc * real_part[place : place + count]

    inside_ref[...] = windowed(margin, 0, half)
    strips[:margin] = windowed(0, half, margin).astype(BF16)
    strips[margin:] = windowed(margin + half, half + margin, margin).astype(BF16)
    place = pl.multiple_of(jnp.where(first == 0, 0, margin), margin)
    first_out_ref[...] = strips[pl.ds(place, margin), :]
    second_out_ref[...] = strips[pl.ds(pl.multiple_of(margin - place, margin), margin), :]


def fold_rows_kernel(half, inside_ref, first_ref, second_ref, center_ref, outer_ref, inner_ref, total):
    margin = half // 2
    first, second, outer, inner = sides(half)
    has_first, _ = inside_sky()
    for source, place, exists in ((first_ref, first, has_first), (second_ref, second, 1.0)):
        rows = pl.ds(pl.multiple_of(jnp.where(place == 0, 0, margin), margin), margin)
        total[rows, :] = inside_ref[rows, :] + source[...].astype(F32) * exists
    center_ref[...] = total[:, margin : margin + half]
    outer_ref[...] = total[:, pl.ds(pl.multiple_of(outer, margin), margin)].astype(BF16)
    inner_ref[...] = total[:, pl.ds(pl.multiple_of(inner, margin), margin)].astype(BF16)


def fold_columns_kernel(half, center_ref, outer_ref, inner_ref, out_ref):
    margin = half // 2
    _, _, outer, inner = sides(half)
    _, has_outer = inside_sky()
    for source, place, exists in ((outer_ref, outer, has_outer), (inner_ref, inner, 1.0)):
        columns = pl.ds(pl.multiple_of(jnp.where(place == 0, 0, margin), margin), margin)
        out_ref[:, columns] = center_ref[:, columns] + source[...].astype(F32) * exists


def partners(offset, side=False):
    rows, columns = lax.axis_size("dec"), lax.axis_size("ra")
    pairs = []
    for i in range(rows):
        partner = i + 1 if i % 2 == offset else i - 1
        for j in range(columns):
            target = (partner, j) if 0 <= partner < rows else (i, j ^ 1)
            if side and i in (rows // 2 - 1, rows // 2):
                target = (partner, j ^ 2)
            pairs.append((i * columns + j, target[0] * columns + target[1]))
    return pairs


def swap_rows(values, offset, side=False):
    return lax.ppermute(values, ("dec", "ra"), partners(offset, side))


def swap_beside(values):
    rows, columns = lax.axis_size("dec"), lax.axis_size("ra")
    pairs = []
    for i in range(rows):
        flip = 2 if i in (rows // 2 - 1, rows // 2) else 1
        pairs += [(i * columns + j, i * columns + (j ^ flip)) for j in range(columns)]
    return lax.ppermute(values, ("dec", "ra"), pairs)


def swap_columns(values, offset):
    count = lax.axis_size("ra")
    pairs = [(i, (i + 1 if i % 2 == offset else i - 1) % count) for i in range(count)]
    return lax.ppermute(values, "ra", pairs)


def whole(count):
    return [pl.BlockSpec(memory_space=pltpu.VMEM)] * count


def kernel_call(body, name, outs, count, scratch=(), flops=0, vmem=16):
    return pl.pallas_call(
        body,
        out_shape=outs,
        in_specs=whole(count),
        out_specs=jax.tree.map(lambda _: pl.BlockSpec(memory_space=pltpu.VMEM), outs),
        scratch_shapes=list(scratch),
        cost_estimate=pl.CostEstimate(flops=flops, bytes_accessed=1 << 20, transcendentals=0),
        compiler_params=pltpu.CompilerParams(vmem_limit_bytes=vmem << 20),
        name=name,
    )


def shards(tables, split_maps, white_noise):
    splits, core_side, _ = split_maps.shape
    half = core_side
    margin = core_side // 2
    length = 2 * core_side
    constant = {k: jnp.asarray(v) for k, v in tables.items() if k != "energy"}
    profile = tables["profile"]
    rows = jnp.asarray(np.ascontiguousarray(np.broadcast_to(profile[:, None], (length, 128))))
    cols = jnp.asarray(np.ascontiguousarray(np.broadcast_to(profile[None, :], (8, length))))
    scale = 1.0 / ((2 * SMOOTH + 1) ** 2 * (splits - 1) * tables["energy"])
    odd_col = lax.axis_index("ra") % 2
    cube = length**3

    piece = jax.ShapeDtypeStruct((splits, margin, margin), BF16)
    strip = jax.ShapeDtypeStruct((splits, margin, half), BF16)
    aside = 2 * splits // 3
    direct = jax.ShapeDtypeStruct((splits - aside, margin, half), BF16)
    aside = jax.ShapeDtypeStruct((aside, margin, half), BF16)
    outer_first, outer_second, near, far, second = kernel_call(
        functools.partial(cut_kernel, half), "cut", (piece, piece, direct, aside, strip), 1, vmem=8
    )(split_maps)
    outer_first = swap_columns(outer_first, 1)
    second = swap_rows(second, 0)
    row = lax.axis_index("dec")
    middle = lax.axis_size("dec") // 2
    beside = swap_beside(far)
    near = swap_rows(near, 1)
    far = swap_rows(jnp.where(jnp.logical_or(row == middle - 1, row == middle), beside, far), 1, side=True)
    outer_second = swap_columns(outer_second, 1)

    spectrum = jax.ShapeDtypeStruct((half + 8, length), F32)
    re, im = kernel_call(
        functools.partial(noise_kernel, half), "noise_spectrum", (spectrum, spectrum), 3, flops=50 * cube
    )(white_noise, constant["left"], constant["right"])

    near, far, second, _, _, re, im = lax.optimization_barrier(
        (near, far, second, outer_first, outer_second, re, im)
    )
    first_corner = swap_rows(outer_first, 1)
    second_corner = swap_rows(outer_second, 0)
    inner = swap_columns(
        jnp.concatenate(
            [
                lax.dynamic_slice_in_dim(block, (1 - odd_col) * margin, margin, axis=2)
                for block in (jnp.concatenate([near, far], axis=0), split_maps, second)
            ],
            axis=1,
        ),
        0,
    )
    def columns(body, name, count, flops):
        return kernel_call(
            functools.partial(body, half),
            name,
            jax.ShapeDtypeStruct((splits, length + 16, margin), BF16),
            count,
            [pltpu.VMEM((splits, length, margin), BF16)],
            flops=flops,
        )

    left, right = constant["left"], constant["right"]
    core, outer = kernel_call(
        functools.partial(core_kernel, half),
        "core_columns",
        (
            jax.ShapeDtypeStruct((splits, length + 16, length), F32),
            jax.ShapeDtypeStruct((splits, length, margin), BF16),
        ),
        10,
        [pltpu.VMEM((splits, length, half), BF16)],
        flops=cube,
    )(split_maps, near, far, second, outer_first, outer_second, rows, cols, left, right)
    outer = columns(outer_kernel, "outer_columns", 7, 400000 * cube // 1000)(
        core, outer, first_corner, second_corner, rows, cols, left
    )
    inner = columns(inner_kernel, "inner_columns", 5, cube)(outer, inner, rows, cols, left)

    strip = jax.ShapeDtypeStruct((margin, length), BF16)
    first, second, inside = kernel_call(
        functools.partial(main_kernel, half, scale),
        "tile_model",
        (strip, strip, jax.ShapeDtypeStruct((half, length), F32)),
        11,
        [
            pltpu.VMEM((half, length), BF16),
            pltpu.VMEM((half + 8, length), F32),
            pltpu.VMEM((2, half + 128, length), BF16),
            pltpu.VMEM((half, length), BF16),
        ],
        flops=20 * cube,
    )(
        core, inner, outer, re, im, rows, cols,
        constant["right"], constant["band_rows"], constant["band_columns"],
        constant["inverse_right"],
    )

    second = swap_rows(second, 0)
    first = swap_rows(first, 1)
    column = jax.ShapeDtypeStruct((half, margin), BF16)
    block = jax.ShapeDtypeStruct((half, half), F32)
    center, outer, inner = kernel_call(
        functools.partial(fold_rows_kernel, half), "fold_rows", (block, column, column), 3,
        [pltpu.VMEM((half, length), F32)],
    )(inside, first, second)
    outer = swap_columns(outer, 1)
    inner = swap_columns(inner, 0)
    return kernel_call(functools.partial(fold_columns_kernel, half), "fold_columns", block, 3)(
        center, outer, inner
    )


def solution(mesh):
    tables = host_tables(512)
    placed = (P(None, "dec", "ra"), P("dec", "ra"))
    return jax.shard_map(
        functools.partial(shards, tables), mesh=mesh, in_specs=placed, out_specs=P("dec", "ra"), check_vma=False
    )
```

```python
import functools

import jax
import jax.numpy as jnp
import numpy as np
from jax import lax
from jax.experimental import pallas as pl
from jax.experimental.pallas import tpu as pltpu
from jax.sharding import PartitionSpec as P

import ml_dtypes

SMOOTH = 4
BF16 = jnp.bfloat16
F32 = jnp.float32


def host_tables(length):
    half = length // 2
    index = np.arange(length)
    phase = np.outer(index, index) % length
    cos = np.cos(2 * np.pi * phase / length)
    sin = np.sin(2 * np.pi * phase / length)
    sin[phase % half == 0] = 0.0
    cos = cos.astype(ml_dtypes.bfloat16).astype(np.float64)
    sin = sin.astype(ml_dtypes.bfloat16).astype(np.float64)

    def packed(rows):
        return np.ascontiguousarray(rows).astype(ml_dtypes.bfloat16)

    left = np.zeros((length + 16, length))
    left[:half] = cos[:half]
    left[half:length] = sin[:half]
    left[length] = cos[half]
    right = np.concatenate([cos[:, :half], sin[:, :half]], axis=1)
    right[:, half] = cos[:, half]
    margin = half // 2
    right = np.roll(right, -margin, axis=0)
    right = np.concatenate([right[:half], np.roll(right[half:], margin, axis=0)], axis=0)
    inverse_right = np.concatenate([2 * cos[:half], -2 * sin[:half]], axis=0)
    inverse_right[0] = cos[0]
    inverse_right[half] = cos[half]
    order = np.concatenate([index[:half], [half], -index[1:half]])

    def near(first, second):
        apart = np.abs(first[:, None] - second[None, :]) % length
        return (np.minimum(apart, length - apart) <= SMOOTH).astype(np.float64)

    band_columns = near(order, order)
    band_rows = np.zeros((half + 16, half + 128))
    targets = np.arange(half + 1)
    band_rows[: half + 1, : half + 1] = near(targets, targets)
    first, last = half + 8, half + 16
    band_rows[: half + 1, first + 1 : first + 8] = near(targets, -np.arange(1, 8))
    band_rows[: half + 1, last : last + 8] = near(targets, -np.arange(half - 8, half))
    profile = np.sin(np.pi * (index + 0.5) / length) ** 2
    energy = np.sum(profile**2) ** 2
    return dict(
        left=packed(left),
        right=packed(right),
        inverse_right=packed(inverse_right),
        band_columns=packed(band_columns),
        band_rows=packed(band_rows),
        profile=profile.astype(np.float32),
        energy=float(energy),
    )


def dot(a, b):
    return jnp.dot(a, b, preferred_element_type=F32)


def first_column(shape):
    return lax.broadcasted_iota(jnp.int32, shape, 1) == 0


def two_parts(values):
    high = values.astype(BF16)
    return high, (values - high.astype(F32)).astype(BF16)


def quarters(spectra, half):
    length = 2 * half
    return (
        spectra[:half, :half],
        spectra[:half, half:],
        spectra[half:length, :half],
        spectra[half:length, half:],
        spectra[length : length + 8, :half],
        spectra[length : length + 8, half:],
    )


def noise_kernel(half, noise_ref, left_ref, right_ref, re_ref, im_ref):
    margin = half // 2
    halves = dot(left_ref[...], noise_ref[...]).astype(BF16)
    spectra = (
        dot(halves[:, margin : margin + half], right_ref[:half])
        + dot(halves[:, :margin], right_ref[half : half + margin])
        + dot(halves[:, margin + half :], right_ref[half + margin :])
    )
    cc, cs, sc, ss, nc, ns = quarters(spectra, half)
    edge = first_column((half, half))
    re_ref[:half, :half] = jnp.where(edge, cc, cc - ss)
    re_ref[:half, half:] = jnp.where(edge, cs, cc + ss)
    im_ref[:half, :half] = -jnp.where(edge, sc, cs + sc)
    im_ref[:half, half:] = jnp.where(edge, -ss, cs - sc)
    edge = first_column((8, half))
    re_ref[half : half + 8, :half] = nc
    re_ref[half : half + 8, half:] = jnp.where(edge, ns, nc)
    im_ref[half : half + 8, :half] = jnp.where(edge, 0.0, -ns)
    im_ref[half : half + 8, half:] = jnp.where(edge, 0.0, ns)


def aligned(offset, step):
    return offset if isinstance(offset, int) else pl.multiple_of(offset, step)


def fill(tile, source, rows_ref, cols_ref, source_row, height, row, col, tile_col, exists=None):
    sources = source if isinstance(source, tuple) else (source,)
    planes = [(ref, s) for ref in sources for s in range(ref.shape[0])]
    splits, width = len(planes), sources[0].shape[2]
    step = 32
    pc = cols_ref[:1, pl.ds(aligned(col, 128), width)]
    if exists is not None:
        pc = pc * exists

    def strip(number, carry):
        start = pl.multiple_of(source_row + number * step, step)
        target = pl.multiple_of(row + number * step, step)
        members = [ref[s, pl.ds(start, step), :].astype(F32) for ref, s in planes]
        mean = functools.reduce(lambda a, b: a + b, members) * (1.0 / splits)
        weights = jnp.concatenate([rows_ref[pl.ds(target, step), :]] * (width // 128), axis=1) * pc
        for s in range(splits):
            tile[s, pl.ds(target, step), pl.ds(aligned(tile_col, 128), width)] = (
                weights * (members[s] - mean)
            ).astype(BF16)
        return carry

    lax.fori_loop(0, height // step, strip, 0)


def sides(half):
    far = half + half // 2
    first = jnp.where(lax.axis_index("dec") % 2 == 0, 0, far)
    outer = jnp.where(lax.axis_index("ra") % 2 == 0, 0, far)
    return first, far - first, outer, far - outer


def inside_sky():
    flags = []
    for axis in ("dec", "ra"):
        index = lax.axis_index(axis)
        edge = jnp.logical_or(index == 0, index == lax.axis_size(axis) - 1)
        flags.append(jnp.where(edge, 0.0, 1.0).astype(F32))
    return flags


def cut_kernel(half, maps_ref, outer_first_ref, outer_second_ref, near_ref, far_ref, second_ref):
    margin = half // 2
    first, second, outer, _ = sides(half)
    columns = pl.ds(pl.multiple_of(jnp.where(outer == 0, 0, margin), margin), margin)
    splits, direct = maps_ref.shape[0], near_ref.shape[0]
    for piece, place in ((outer_first_ref, first), (outer_second_ref, second)):
        rows = pl.ds(pl.multiple_of(jnp.where(place == 0, 0, margin), margin), margin)
        for s in range(splits):
            piece[s] = maps_ref[s, rows, columns]
            if piece is outer_second_ref:
                second_ref[s] = maps_ref[s, rows, :]
            elif s < direct:
                near_ref[s] = maps_ref[s, rows, :]
            else:
                far_ref[s - direct] = maps_ref[s, rows, :]


def core_kernel(
    half, core_ref, near_ref, far_ref, second_ref, outer_first_ref, outer_second_ref,
    rows_ref, cols_ref, left_ref, right_ref,
    spectra_ref, outer_ref, tile,
):
    margin = half // 2
    splits = core_ref.shape[0]
    first, second, outer, _ = sides(half)
    has_first, has_outer = inside_sky()
    fill(tile, core_ref, rows_ref, cols_ref, 0, half, margin, margin, 0)
    fill(tile, (near_ref, far_ref), rows_ref, cols_ref, 0, margin, first, margin, 0, has_first)
    fill(tile, second_ref, rows_ref, cols_ref, 0, margin, second, margin, 0)

    def transform(number, carry):
        for s in (2 * number, 2 * number + 1):
            halves = dot(left_ref[...], tile[s]).astype(BF16)
            spectra_ref[s] = dot(halves, right_ref[:half])
        return carry

    lax.fori_loop(0, splits // 2, transform, 0)
    for source, place in ((outer_first_ref, first), (outer_second_ref, second)):
        row = jnp.where(place == 0, margin, half)
        fill(outer_ref, source, rows_ref, cols_ref, 0, margin, row, outer, 0, has_outer)


def transform_pairs(tile, left_ref, halves_ref):
    splits, _, width = tile.shape
    for s in range(0, splits, 2):
        halves = dot(left_ref[...], jnp.concatenate([tile[s], tile[s + 1]], axis=1)).astype(BF16)
        halves_ref[s] = halves[:, :width]
        halves_ref[s + 1] = halves[:, width:]


def inner_kernel(half, after_ref, inner_ref, rows_ref, cols_ref, left_ref, halves_ref, tile):
    del after_ref
    margin = half // 2
    first, second, _, inner = sides(half)
    has_first, _ = inside_sky()
    fill(tile, inner_ref, rows_ref, cols_ref, 0, margin, first, inner, 0, has_first)
    fill(tile, inner_ref, rows_ref, cols_ref, margin, half, margin, inner, 0)
    fill(tile, inner_ref, rows_ref, cols_ref, margin + half, margin, second, inner, 0)
    transform_pairs(tile, left_ref, halves_ref)


def outer_kernel(
    half, after_ref, tile, first_ref, second_ref, rows_ref, cols_ref, left_ref, halves_ref, full
):
    del after_ref
    margin = half // 2
    first, second, outer, _ = sides(half)
    has_first, has_outer = inside_sky()
    full[:, margin : margin + half, :] = tile[:, margin : margin + half, :]
    fill(full, first_ref, rows_ref, cols_ref, 0, margin, first, outer, 0, has_outer * has_first)
    fill(full, second_ref, rows_ref, cols_ref, 0, margin, second, outer, 0, has_outer)
    transform_pairs(full, left_ref, halves_ref)


def main_kernel(
    half, scale,
    core_ref, inner_ref, outer_ref, re_ref, im_ref,
    rows_ref, cols_ref, right_ref, band_rows_ref, band_columns_ref,
    inverse_right_ref,
    first_out_ref, second_out_ref, inside_ref,
    table, power, stacked, strips,
):
    length = 2 * half
    margin = half // 2
    splits = core_ref.shape[0]
    first, _, _, inner = sides(half)
    place = pl.multiple_of(half + jnp.where(inner == 0, 0, margin), margin)
    table[:margin] = right_ref[pl.ds(place, margin), :]
    table[margin:] = right_ref[pl.ds(pl.multiple_of(length + margin - place, margin), margin), :]

    edge = first_column((half, half))
    edge8 = first_column((8, half))

    def accumulate(s, carry):
        halves = jnp.concatenate([inner_ref[s], outer_ref[s]], axis=1)
        spectra = core_ref[s] + dot(halves, table[...])
        cc, cs, sc, ss, nc, ns = quarters(spectra, half)
        e = jnp.where(edge, cc, cc - ss)
        f = jnp.where(edge, sc, cs + sc)
        g = jnp.where(edge, cs, cc + ss)
        h = jnp.where(edge, ss, cs - sc)
        nc, ns = nc * nc, ns * ns
        terms = (
            e * e + f * f, g * g + h * h, jnp.where(edge8, nc, nc + ns), jnp.where(edge8, ns, nc + ns)
        )
        places = (
            (slice(0, half), slice(0, half)), (slice(0, half), slice(half, length)),
            (slice(half, half + 8), slice(0, half)), (slice(half, half + 8), slice(half, length)),
        )
        for term, place in zip(terms, places):
            power[place] = term if carry else power[place] + term

    accumulate(0, True)
    for s in range(1, splits):
        accumulate(s, False)

    stacked[:, half + 24 :, :] = jnp.zeros((2, stacked.shape[1] - half - 24, length), BF16)
    for part, values in enumerate(two_parts(power[...])):
        stacked[part, : half + 8, :] = values
    for place, start in ((half + 8, 0), (half + 16, half - 8)):
        a = power[start : start + 8, :half]
        b = power[start : start + 8, half:]
        mirrored = jnp.concatenate(
            [jnp.where(edge8, a, b), jnp.where(edge8, b, a)], axis=1
        )
        for part, values in enumerate(two_parts(mirrored)):
            stacked[part, place : place + 8, :] = values
    smooth = (
        dot(band_rows_ref[...], stacked[1]) + dot(band_rows_ref[...], stacked[0])
    )
    high, low = two_parts(smooth)
    smooth = dot(low, band_columns_ref[...]) + dot(high, band_columns_ref[...])
    gain = jnp.sqrt(jnp.maximum(smooth[: half + 8], 0.0) * scale)
    gr = (gain * re_ref[...]).astype(BF16)
    gi = (gain * im_ref[...]).astype(BF16)
    er, fr = gr[:half, :half], gr[:half, half:]
    ei, fi = gi[:half, :half], gi[:half, half:]
    start = lax.broadcasted_iota(jnp.int32, (half, half), 0) == 0
    nyquist_u = gr[half : half + 1, :half]
    nyquist_v = jnp.where(edge8[:1], gr[half : half + 1, half:], gi[half : half + 1, :half])
    zero = jnp.zeros((), BF16)
    near_u = jnp.concatenate([er, jnp.where(start, nyquist_u, -ei)], axis=0)
    far_u = jnp.concatenate(
        [jnp.where(edge, er, fr), -jnp.where(edge, ei, fi)], axis=0
    )
    near_v = jnp.concatenate(
        [jnp.where(edge, fr, ei), jnp.where(start, nyquist_v, jnp.where(edge, -fi, er))], axis=0
    )
    far_v = jnp.concatenate(
        [jnp.where(edge, fr, -fi), -jnp.where(edge, fi, fr)], axis=0
    )
    start = lax.broadcasted_iota(jnp.int32, (length, half), 0) % half == 0
    far_u, far_v = jnp.where(start, zero, far_u), jnp.where(start, zero, far_v)
    u = dot(right_ref[...], near_u) + dot(right_ref[...], far_u)
    v = dot(right_ref[...], near_v) + dot(right_ref[...], far_v)
    joined = jnp.concatenate([u.astype(BF16), v.astype(BF16)], axis=1)
    real_part = dot(joined, inverse_right_ref[...])
    pc = cols_ref[:1, :] * (1.0 / (length * length))

    def windowed(row, place, count):
        profile = jnp.concatenate([rows_ref[row : row + count, :]] * (length // 128), axis=1)
        return profile * pc * real_part[place : place + count]

    inside_ref[...] = windowed(margin, 0, half)
    strips[:margin] = windowed(0, half, margin).astype(BF16)
    strips[margin:] = windowed(margin + half, half + margin, margin).astype(BF16)
    place = pl.multiple_of(jnp.where(first == 0, 0, margin), margin)
    first_out_ref[...] = strips[pl.ds(place, margin), :]
    second_out_ref[...] = strips[pl.ds(pl.multiple_of(margin - place, margin), margin), :]


def fold_rows_kernel(half, inside_ref, first_ref, second_ref, center_ref, outer_ref, inner_ref, total):
    margin = half // 2
    first, second, outer, inner = sides(half)
    has_first, _ = inside_sky()
    for source, place, exists in ((first_ref, first, has_first), (second_ref, second, 1.0)):
        rows = pl.ds(pl.multiple_of(jnp.where(place == 0, 0, margin), margin), margin)
        total[rows, :] = inside_ref[rows, :] + source[...].astype(F32) * exists
    center_ref[...] = total[:, margin : margin + half]
    outer_ref[...] = total[:, pl.ds(pl.multiple_of(outer, margin), margin)].astype(BF16)
    inner_ref[...] = total[:, pl.ds(pl.multiple_of(inner, margin), margin)].astype(BF16)


def fold_columns_kernel(half, center_ref, outer_ref, inner_ref, out_ref):
    margin = half // 2
    _, _, outer, inner = sides(half)
    _, has_outer = inside_sky()
    for source, place, exists in ((outer_ref, outer, has_outer), (inner_ref, inner, 1.0)):
        columns = pl.ds(pl.multiple_of(jnp.where(place == 0, 0, margin), margin), margin)
        out_ref[:, columns] = center_ref[:, columns] + source[...].astype(F32) * exists


def partners(offset, side=False):
    rows, columns = lax.axis_size("dec"), lax.axis_size("ra")
    pairs = []
    for i in range(rows):
        partner = i + 1 if i % 2 == offset else i - 1
        for j in range(columns):
            target = (partner, j) if 0 <= partner < rows else (i, j ^ 1)
            if side and i in (rows // 2 - 1, rows // 2):
                target = (partner, j ^ 2)
            pairs.append((i * columns + j, target[0] * columns + target[1]))
    return pairs


def swap_rows(values, offset, side=False):
    return lax.ppermute(values, ("dec", "ra"), partners(offset, side))


def swap_beside(values):
    rows, columns = lax.axis_size("dec"), lax.axis_size("ra")
    pairs = []
    for i in range(rows):
        flip = 2 if i in (rows // 2 - 1, rows // 2) else 1
        pairs += [(i * columns + j, i * columns + (j ^ flip)) for j in range(columns)]
    return lax.ppermute(values, ("dec", "ra"), pairs)


def swap_columns(values, offset):
    count = lax.axis_size("ra")
    pairs = [(i, (i + 1 if i % 2 == offset else i - 1) % count) for i in range(count)]
    return lax.ppermute(values, "ra", pairs)


def whole(count):
    return [pl.BlockSpec(memory_space=pltpu.VMEM)] * count


def kernel_call(body, name, outs, count, scratch=(), flops=0, vmem=16):
    return pl.pallas_call(
        body,
        out_shape=outs,
        in_specs=whole(count),
        out_specs=jax.tree.map(lambda _: pl.BlockSpec(memory_space=pltpu.VMEM), outs),
        scratch_shapes=list(scratch),
        cost_estimate=pl.CostEstimate(flops=flops, bytes_accessed=1 << 20, transcendentals=0),
        compiler_params=pltpu.CompilerParams(vmem_limit_bytes=vmem << 20),
        name=name,
    )


def shards(tables, split_maps, white_noise):
    splits, core_side, _ = split_maps.shape
    half = core_side
    margin = core_side // 2
    length = 2 * core_side
    constant = {k: jnp.asarray(v) for k, v in tables.items() if k != "energy"}
    profile = tables["profile"]
    rows = jnp.asarray(np.ascontiguousarray(np.broadcast_to(profile[:, None], (length, 128))))
    cols = jnp.asarray(np.ascontiguousarray(np.broadcast_to(profile[None, :], (8, length))))
    scale = 1.0 / ((2 * SMOOTH + 1) ** 2 * (splits - 1) * tables["energy"])
    odd_col = lax.axis_index("ra") % 2
    cube = length**3

    piece = jax.ShapeDtypeStruct((splits, margin, margin), BF16)
    strip = jax.ShapeDtypeStruct((splits, margin, half), BF16)
    aside = splits // 3
    direct = jax.ShapeDtypeStruct((splits - aside, margin, half), BF16)
    aside = jax.ShapeDtypeStruct((aside, margin, half), BF16)
    outer_first, outer_second, near, far, second = kernel_call(
        functools.partial(cut_kernel, half), "cut", (piece, piece, direct, aside, strip), 1, vmem=8
    )(split_maps)
    outer_first = swap_columns(outer_first, 1)
    second = swap_rows(second, 0)
    row = lax.axis_index("dec")
    middle = lax.axis_size("dec") // 2
    beside = swap_beside(far)
    near = swap_rows(near, 1)
    far = swap_rows(jnp.where(jnp.logical_or(row == middle - 1, row == middle), beside, far), 1, side=True)
    outer_second, outer_first = lax.optimization_barrier((outer_second, outer_first))
    outer_second = swap_columns(outer_second, 1)

    spectrum = jax.ShapeDtypeStruct((half + 8, length), F32)
    re, im = kernel_call(
        functools.partial(noise_kernel, half), "noise_spectrum", (spectrum, spectrum), 3, flops=50 * cube
    )(white_noise, constant["left"], constant["right"])

    near, far, second, _, _, re, im = lax.optimization_barrier(
        (near, far, second, outer_first, outer_second, re, im)
    )
    first_corner = swap_rows(outer_first, 1)
    second_corner = swap_rows(outer_second, 0)
    inner = swap_columns(
        jnp.concatenate(
            [
                lax.dynamic_slice_in_dim(block, (1 - odd_col) * margin, margin, axis=2)
                for block in (jnp.concatenate([near, far], axis=0), split_maps, second)
            ],
            axis=1,
        ),
        0,
    )
    def columns(body, name, count, flops):
        return kernel_call(
            functools.partial(body, half),
            name,
            jax.ShapeDtypeStruct((splits, length + 16, margin), BF16),
            count,
            [pltpu.VMEM((splits, length, margin), BF16)],
            flops=flops,
        )

    left, right = constant["left"], constant["right"]
    core, outer = kernel_call(
        functools.partial(core_kernel, half),
        "core_columns",
        (
            jax.ShapeDtypeStruct((splits, length + 16, length), F32),
            jax.ShapeDtypeStruct((splits, length, margin), BF16),
        ),
        10,
        [pltpu.VMEM((splits, length, half), BF16)],
        flops=cube,
    )(split_maps, near, far, second, outer_first, outer_second, rows, cols, left, right)
    outer = columns(outer_kernel, "outer_columns", 7, 400000 * cube // 1000)(
        core, outer, first_corner, second_corner, rows, cols, left
    )
    inner = columns(inner_kernel, "inner_columns", 5, cube)(outer, inner, rows, cols, left)

    strip = jax.ShapeDtypeStruct((margin, length), BF16)
    first, second, inside = kernel_call(
        functools.partial(main_kernel, half, scale),
        "tile_model",
        (strip, strip, jax.ShapeDtypeStruct((half, length), F32)),
        11,
        [
            pltpu.VMEM((half, length), BF16),
            pltpu.VMEM((half + 8, length), F32),
            pltpu.VMEM((2, half + 128, length), BF16),
            pltpu.VMEM((half, length), BF16),
        ],
        flops=20 * cube,
    )(
        core, inner, outer, re, im, rows, cols,
        constant["right"], constant["band_rows"], constant["band_columns"],
        constant["inverse_right"],
    )

    second = swap_rows(second, 0)
    first = swap_rows(first, 1)
    column = jax.ShapeDtypeStruct((half, margin), BF16)
    block = jax.ShapeDtypeStruct((half, half), F32)
    center, outer, inner = kernel_call(
        functools.partial(fold_rows_kernel, half), "fold_rows", (block, column, column), 3,
        [pltpu.VMEM((half, length), F32)],
    )(inside, first, second)
    outer = swap_columns(outer, 1)
    inner = swap_columns(inner, 0)
    return kernel_call(functools.partial(fold_columns_kernel, half), "fold_columns", block, 3)(
        center, outer, inner
    )


def solution(mesh):
    tables = host_tables(512)
    placed = (P(None, "dec", "ra"), P("dec", "ra"))
    return jax.shard_map(
        functools.partial(shards, tables), mesh=mesh, in_specs=placed, out_specs=P("dec", "ra"), check_vma=False
    )
```

```python
import functools

import jax
import jax.numpy as jnp
import numpy as np
from jax import lax
from jax.experimental import pallas as pl
from jax.experimental.pallas import tpu as pltpu
from jax.sharding import PartitionSpec as P

import ml_dtypes

SMOOTH = 4
BF16 = jnp.bfloat16
F32 = jnp.float32


def host_tables(length):
    half = length // 2
    index = np.arange(length)
    phase = np.outer(index, index) % length
    cos = np.cos(2 * np.pi * phase / length)
    sin = np.sin(2 * np.pi * phase / length)
    sin[phase % half == 0] = 0.0
    cos = cos.astype(ml_dtypes.bfloat16).astype(np.float64)
    sin = sin.astype(ml_dtypes.bfloat16).astype(np.float64)

    def packed(rows):
        return np.ascontiguousarray(rows).astype(ml_dtypes.bfloat16)

    left = np.zeros((length + 16, length))
    left[:half] = cos[:half]
    left[half:length] = sin[:half]
    left[length] = cos[half]
    right = np.concatenate([cos[:, :half], sin[:, :half]], axis=1)
    right[:, half] = cos[:, half]
    margin = half // 2
    right = np.roll(right, -margin, axis=0)
    right = np.concatenate([right[:half], np.roll(right[half:], margin, axis=0)], axis=0)
    inverse_right = np.concatenate([2 * cos[:half], -2 * sin[:half]], axis=0)
    inverse_right[0] = cos[0]
    inverse_right[half] = cos[half]
    order = np.concatenate([index[:half], [half], -index[1:half]])

    def near(first, second):
        apart = np.abs(first[:, None] - second[None, :]) % length
        return (np.minimum(apart, length - apart) <= SMOOTH).astype(np.float64)

    band_columns = near(order, order)
    band_rows = np.zeros((half + 16, half + 128))
    targets = np.arange(half + 1)
    band_rows[: half + 1, : half + 1] = near(targets, targets)
    first, last = half + 8, half + 16
    band_rows[: half + 1, first + 1 : first + 8] = near(targets, -np.arange(1, 8))
    band_rows[: half + 1, last : last + 8] = near(targets, -np.arange(half - 8, half))
    profile = np.sin(np.pi * (index + 0.5) / length) ** 2
    energy = np.sum(profile**2) ** 2
    return dict(
        left=packed(left),
        right=packed(right),
        inverse_right=packed(inverse_right),
        band_columns=packed(band_columns),
        band_rows=packed(band_rows),
        profile=profile.astype(np.float32),
        energy=float(energy),
    )


def dot(a, b):
    return jnp.dot(a, b, preferred_element_type=F32)


def first_column(shape):
    return lax.broadcasted_iota(jnp.int32, shape, 1) == 0


def two_parts(values):
    high = values.astype(BF16)
    return high, (values - high.astype(F32)).astype(BF16)


def quarters(spectra, half):
    length = 2 * half
    return (
        spectra[:half, :half],
        spectra[:half, half:],
        spectra[half:length, :half],
        spectra[half:length, half:],
        spectra[length : length + 8, :half],
        spectra[length : length + 8, half:],
    )


def noise_kernel(half, noise_ref, left_ref, right_ref, re_ref, im_ref):
    margin = half // 2
    halves = dot(left_ref[...], noise_ref[...]).astype(BF16)
    spectra = (
        dot(halves[:, margin : margin + half], right_ref[:half])
        + dot(halves[:, :margin], right_ref[half : half + margin])
        + dot(halves[:, margin + half :], right_ref[half + margin :])
    )
    cc, cs, sc, ss, nc, ns = quarters(spectra, half)
    edge = first_column((half, half))
    re_ref[:half, :half] = jnp.where(edge, cc, cc - ss)
    re_ref[:half, half:] = jnp.where(edge, cs, cc + ss)
    im_ref[:half, :half] = -jnp.where(edge, sc, cs + sc)
    im_ref[:half, half:] = jnp.where(edge, -ss, cs - sc)
    edge = first_column((8, half))
    re_ref[half : half + 8, :half] = nc
    re_ref[half : half + 8, half:] = jnp.where(edge, ns, nc)
    im_ref[half : half + 8, :half] = jnp.where(edge, 0.0, -ns)
    im_ref[half : half + 8, half:] = jnp.where(edge, 0.0, ns)


def aligned(offset, step):
    return offset if isinstance(offset, int) else pl.multiple_of(offset, step)


def fill(tile, source, rows_ref, cols_ref, source_row, height, row, col, tile_col, exists=None):
    sources = source if isinstance(source, tuple) else (source,)
    planes = [(ref, s) for ref in sources for s in range(ref.shape[0])]
    splits, width = len(planes), sources[0].shape[2]
    step = 32
    pc = cols_ref[:1, pl.ds(aligned(col, 128), width)]
    if exists is not None:
        pc = pc * exists

    def strip(number, carry):
        start = pl.multiple_of(source_row + number * step, step)
        target = pl.multiple_of(row + number * step, step)
        members = [ref[s, pl.ds(start, step), :].astype(F32) for ref, s in planes]
        mean = functools.reduce(lambda a, b: a + b, members) * (1.0 / splits)
        weights = jnp.concatenate([rows_ref[pl.ds(target, step), :]] * (width // 128), axis=1) * pc
        for s in range(splits):
            tile[s, pl.ds(target, step), pl.ds(aligned(tile_col, 128), width)] = (
                weights * (members[s] - mean)
            ).astype(BF16)
        return carry

    lax.fori_loop(0, height // step, strip, 0)


def sides(half):
    far = half + half // 2
    first = jnp.where(lax.axis_index("dec") % 2 == 0, 0, far)
    outer = jnp.where(lax.axis_index("ra") % 2 == 0, 0, far)
    return first, far - first, outer, far - outer


def inside_sky():
    flags = []
    for axis in ("dec", "ra"):
        index = lax.axis_index(axis)
        edge = jnp.logical_or(index == 0, index == lax.axis_size(axis) - 1)
        flags.append(jnp.where(edge, 0.0, 1.0).astype(F32))
    return flags


def cut_kernel(half, maps_ref, outer_first_ref, outer_second_ref, near_ref, far_ref, second_ref):
    margin = half // 2
    first, second, outer, _ = sides(half)
    columns = pl.ds(pl.multiple_of(jnp.where(outer == 0, 0, margin), margin), margin)
    splits, direct = maps_ref.shape[0], near_ref.shape[0]
    for piece, place in ((outer_first_ref, first), (outer_second_ref, second)):
        rows = pl.ds(pl.multiple_of(jnp.where(place == 0, 0, margin), margin), margin)
        for s in range(splits):
            piece[s] = maps_ref[s, rows, columns]
            if piece is outer_second_ref:
                second_ref[s] = maps_ref[s, rows, :]
            elif s < direct:
                near_ref[s] = maps_ref[s, rows, :]
            else:
                far_ref[s - direct] = maps_ref[s, rows, :]


def core_kernel(
    half, core_ref, near_ref, far_ref, second_ref, outer_first_ref, outer_second_ref,
    rows_ref, cols_ref, left_ref, right_ref,
    spectra_ref, outer_ref, tile,
):
    margin = half // 2
    splits = core_ref.shape[0]
    first, second, outer, _ = sides(half)
    has_first, has_outer = inside_sky()
    fill(tile, core_ref, rows_ref, cols_ref, 0, half, margin, margin, 0)
    fill(tile, (near_ref, far_ref), rows_ref, cols_ref, 0, margin, first, margin, 0, has_first)
    fill(tile, second_ref, rows_ref, cols_ref, 0, margin, second, margin, 0)

    def transform(number, carry):
        for s in (2 * number, 2 * number + 1):
            halves = dot(left_ref[...], tile[s]).astype(BF16)
            spectra_ref[s] = dot(halves, right_ref[:half])
        return carry

    lax.fori_loop(0, splits // 2, transform, 0)
    for source, place in ((outer_first_ref, first), (outer_second_ref, second)):
        row = jnp.where(place == 0, margin, half)
        fill(outer_ref, source, rows_ref, cols_ref, 0, margin, row, outer, 0, has_outer)


def transform_pairs(tile, left_ref, halves_ref):
    splits, _, width = tile.shape
    for s in range(0, splits, 2):
        halves = dot(left_ref[...], jnp.concatenate([tile[s], tile[s + 1]], axis=1)).astype(BF16)
        halves_ref[s] = halves[:, :width]
        halves_ref[s + 1] = halves[:, width:]


def inner_kernel(half, after_ref, inner_ref, rows_ref, cols_ref, left_ref, halves_ref, tile):
    del after_ref
    margin = half // 2
    first, second, _, inner = sides(half)
    has_first, _ = inside_sky()
    fill(tile, inner_ref, rows_ref, cols_ref, 0, margin, first, inner, 0, has_first)
    fill(tile, inner_ref, rows_ref, cols_ref, margin, half, margin, inner, 0)
    fill(tile, inner_ref, rows_ref, cols_ref, margin + half, margin, second, inner, 0)
    transform_pairs(tile, left_ref, halves_ref)


def outer_kernel(
    half, after_ref, tile, first_ref, second_ref, rows_ref, cols_ref, left_ref, halves_ref, full
):
    del after_ref
    margin = half // 2
    first, second, outer, _ = sides(half)
    has_first, has_outer = inside_sky()
    full[:, margin : margin + half, :] = tile[:, margin : margin + half, :]
    fill(full, first_ref, rows_ref, cols_ref, 0, margin, first, outer, 0, has_outer * has_first)
    fill(full, second_ref, rows_ref, cols_ref, 0, margin, second, outer, 0, has_outer)
    transform_pairs(full, left_ref, halves_ref)


def main_kernel(
    half, scale,
    core_ref, inner_ref, outer_ref, re_ref, im_ref,
    rows_ref, cols_ref, right_ref, band_rows_ref, band_columns_ref,
    inverse_right_ref,
    first_out_ref, second_out_ref, inside_ref,
    table, power, stacked, strips,
):
    length = 2 * half
    margin = half // 2
    splits = core_ref.shape[0]
    first, _, _, inner = sides(half)
    place = pl.multiple_of(half + jnp.where(inner == 0, 0, margin), margin)
    table[:margin] = right_ref[pl.ds(place, margin), :]
    table[margin:] = right_ref[pl.ds(pl.multiple_of(length + margin - place, margin), margin), :]

    edge = first_column((half, half))
    edge8 = first_column((8, half))

    def accumulate(s, carry):
        halves = jnp.concatenate([inner_ref[s], outer_ref[s]], axis=1)
        spectra = core_ref[s] + dot(halves, table[...])
        cc, cs, sc, ss, nc, ns = quarters(spectra, half)
        e = jnp.where(edge, cc, cc - ss)
        f = jnp.where(edge, sc, cs + sc)
        g = jnp.where(edge, cs, cc + ss)
        h = jnp.where(edge, ss, cs - sc)
        nc, ns = nc * nc, ns * ns
        terms = (
            e * e + f * f, g * g + h * h, jnp.where(edge8, nc, nc + ns), jnp.where(edge8, ns, nc + ns)
        )
        places = (
            (slice(0, half), slice(0, half)), (slice(0, half), slice(half, length)),
            (slice(half, half + 8), slice(0, half)), (slice(half, half + 8), slice(half, length)),
        )
        for term, place in zip(terms, places):
            power[place] = term if carry else power[place] + term

    accumulate(0, True)
    for s in range(1, splits):
        accumulate(s, False)

    stacked[:, half + 24 :, :] = jnp.zeros((2, stacked.shape[1] - half - 24, length), BF16)
    for part, values in enumerate(two_parts(power[...])):
        stacked[part, : half + 8, :] = values
    for place, start in ((half + 8, 0), (half + 16, half - 8)):
        a = power[start : start + 8, :half]
        b = power[start : start + 8, half:]
        mirrored = jnp.concatenate(
            [jnp.where(edge8, a, b), jnp.where(edge8, b, a)], axis=1
        )
        for part, values in enumerate(two_parts(mirrored)):
            stacked[part, place : place + 8, :] = values
    smooth = (
        dot(band_rows_ref[...], stacked[1]) + dot(band_rows_ref[...], stacked[0])
    )
    high, low = two_parts(smooth)
    smooth = dot(low, band_columns_ref[...]) + dot(high, band_columns_ref[...])
    gain = jnp.sqrt(jnp.maximum(smooth[: half + 8], 0.0) * scale)
    gr = (gain * re_ref[...]).astype(BF16)
    gi = (gain * im_ref[...]).astype(BF16)
    er, fr = gr[:half, :half], gr[:half, half:]
    ei, fi = gi[:half, :half], gi[:half, half:]
    start = lax.broadcasted_iota(jnp.int32, (half, half), 0) == 0
    nyquist_u = gr[half : half + 1, :half]
    nyquist_v = jnp.where(edge8[:1], gr[half : half + 1, half:], gi[half : half + 1, :half])
    zero = jnp.zeros((), BF16)
    near_u = jnp.concatenate([er, jnp.where(start, nyquist_u, -ei)], axis=0)
    far_u = jnp.concatenate(
        [jnp.where(edge, er, fr), -jnp.where(edge, ei, fi)], axis=0
    )
    near_v = jnp.concatenate(
        [jnp.where(edge, fr, ei), jnp.where(start, nyquist_v, jnp.where(edge, -fi, er))], axis=0
    )
    far_v = jnp.concatenate(
        [jnp.where(edge, fr, -fi), -jnp.where(edge, fi, fr)], axis=0
    )
    start = lax.broadcasted_iota(jnp.int32, (length, half), 0) % half == 0
    far_u, far_v = jnp.where(start, zero, far_u), jnp.where(start, zero, far_v)
    u = dot(right_ref[...], near_u) + dot(right_ref[...], far_u)
    v = dot(right_ref[...], near_v) + dot(right_ref[...], far_v)
    joined = jnp.concatenate([u.astype(BF16), v.astype(BF16)], axis=1)
    real_part = dot(joined, inverse_right_ref[...])
    pc = cols_ref[:1, :] * (1.0 / (length * length))

    def windowed(row, place, count):
        profile = jnp.concatenate([rows_ref[row : row + count, :]] * (length // 128), axis=1)
        return profile * pc * real_part[place : place + count]

    inside_ref[...] = windowed(margin, 0, half)
    strips[:margin] = windowed(0, half, margin).astype(BF16)
    strips[margin:] = windowed(margin + half, half + margin, margin).astype(BF16)
    place = pl.multiple_of(jnp.where(first == 0, 0, margin), margin)
    first_out_ref[...] = strips[pl.ds(place, margin), :]
    second_out_ref[...] = strips[pl.ds(pl.multiple_of(margin - place, margin), margin), :]


def fold_rows_kernel(half, inside_ref, second_ref, first_ref, center_ref, outer_ref, inner_ref, total):
    margin = half // 2
    first, second, outer, inner = sides(half)
    has_first, _ = inside_sky()
    for source, place, exists in ((first_ref, first, has_first), (second_ref, second, 1.0)):
        rows = pl.ds(pl.multiple_of(jnp.where(place == 0, 0, margin), margin), margin)
        total[rows, :] = inside_ref[rows, :] + source[...].astype(F32) * exists
    center_ref[...] = total[:, margin : margin + half]
    outer_ref[...] = total[:, pl.ds(pl.multiple_of(outer, margin), margin)].astype(BF16)
    inner_ref[...] = total[:, pl.ds(pl.multiple_of(inner, margin), margin)].astype(BF16)


def fold_columns_kernel(half, center_ref, outer_ref, inner_ref, out_ref):
    margin = half // 2
    _, _, outer, inner = sides(half)
    _, has_outer = inside_sky()
    for source, place, exists in ((outer_ref, outer, has_outer), (inner_ref, inner, 1.0)):
        columns = pl.ds(pl.multiple_of(jnp.where(place == 0, 0, margin), margin), margin)
        out_ref[:, columns] = center_ref[:, columns] + source[...].astype(F32) * exists


def partners(offset, side=False):
    rows, columns = lax.axis_size("dec"), lax.axis_size("ra")
    pairs = []
    for i in range(rows):
        partner = i + 1 if i % 2 == offset else i - 1
        for j in range(columns):
            target = (partner, j) if 0 <= partner < rows else (i, j ^ 1)
            if side and i in (rows // 2 - 1, rows // 2):
                target = (partner, j ^ 2)
            pairs.append((i * columns + j, target[0] * columns + target[1]))
    return pairs


def swap_rows(values, offset, side=False):
    return lax.ppermute(values, ("dec", "ra"), partners(offset, side))


def swap_beside(values):
    rows, columns = lax.axis_size("dec"), lax.axis_size("ra")
    pairs = []
    for i in range(rows):
        flip = 2 if i in (rows // 2 - 1, rows // 2) else 1
        pairs += [(i * columns + j, i * columns + (j ^ flip)) for j in range(columns)]
    return lax.ppermute(values, ("dec", "ra"), pairs)


def swap_columns(values, offset):
    count = lax.axis_size("ra")
    pairs = [(i, (i + 1 if i % 2 == offset else i - 1) % count) for i in range(count)]
    return lax.ppermute(values, "ra", pairs)


def whole(count):
    return [pl.BlockSpec(memory_space=pltpu.VMEM)] * count


def kernel_call(body, name, outs, count, scratch=(), flops=0, vmem=16):
    return pl.pallas_call(
        body,
        out_shape=outs,
        in_specs=whole(count),
        out_specs=jax.tree.map(lambda _: pl.BlockSpec(memory_space=pltpu.VMEM), outs),
        scratch_shapes=list(scratch),
        cost_estimate=pl.CostEstimate(flops=flops, bytes_accessed=1 << 20, transcendentals=0),
        compiler_params=pltpu.CompilerParams(vmem_limit_bytes=vmem << 20),
        name=name,
    )


def shards(tables, split_maps, white_noise):
    splits, core_side, _ = split_maps.shape
    half = core_side
    margin = core_side // 2
    length = 2 * core_side
    constant = {k: jnp.asarray(v) for k, v in tables.items() if k != "energy"}
    profile = tables["profile"]
    rows = jnp.asarray(np.ascontiguousarray(np.broadcast_to(profile[:, None], (length, 128))))
    cols = jnp.asarray(np.ascontiguousarray(np.broadcast_to(profile[None, :], (8, length))))
    scale = 1.0 / ((2 * SMOOTH + 1) ** 2 * (splits - 1) * tables["energy"])
    odd_col = lax.axis_index("ra") % 2
    cube = length**3

    piece = jax.ShapeDtypeStruct((splits, margin, margin), BF16)
    strip = jax.ShapeDtypeStruct((splits, margin, half), BF16)
    aside = splits // 3
    direct = jax.ShapeDtypeStruct((splits - aside, margin, half), BF16)
    aside = jax.ShapeDtypeStruct((aside, margin, half), BF16)
    outer_first, outer_second, near, far, second = kernel_call(
        functools.partial(cut_kernel, half), "cut", (piece, piece, direct, aside, strip), 1, vmem=8
    )(split_maps)
    outer_first = swap_columns(outer_first, 1)
    second = swap_rows(second, 0)
    row = lax.axis_index("dec")
    middle = lax.axis_size("dec") // 2
    beside = swap_beside(far)
    near = swap_rows(near, 1)
    far = swap_rows(jnp.where(jnp.logical_or(row == middle - 1, row == middle), beside, far), 1, side=True)
    outer_second = swap_columns(outer_second, 1)

    spectrum = jax.ShapeDtypeStruct((half + 8, length), F32)
    re, im = kernel_call(
        functools.partial(noise_kernel, half), "noise_spectrum", (spectrum, spectrum), 3, flops=50 * cube
    )(white_noise, constant["left"], constant["right"])

    near, far, second, _, _, re, im = lax.optimization_barrier(
        (near, far, second, outer_first, outer_second, re, im)
    )
    first_corner = swap_rows(outer_first, 1)
    second_corner = swap_rows(outer_second, 0)
    inner = swap_columns(
        jnp.concatenate(
            [
                lax.dynamic_slice_in_dim(block, (1 - odd_col) * margin, margin, axis=2)
                for block in (jnp.concatenate([near, far], axis=0), split_maps, second)
            ],
            axis=1,
        ),
        0,
    )
    def columns(body, name, count, flops):
        return kernel_call(
            functools.partial(body, half),
            name,
            jax.ShapeDtypeStruct((splits, length + 16, margin), BF16),
            count,
            [pltpu.VMEM((splits, length, margin), BF16)],
            flops=flops,
        )

    left, right = constant["left"], constant["right"]
    core, outer = kernel_call(
        functools.partial(core_kernel, half),
        "core_columns",
        (
            jax.ShapeDtypeStruct((splits, length + 16, length), F32),
            jax.ShapeDtypeStruct((splits, length, margin), BF16),
        ),
        10,
        [pltpu.VMEM((splits, length, half), BF16)],
        flops=cube,
    )(split_maps, near, far, second, outer_first, outer_second, rows, cols, left, right)
    outer = columns(outer_kernel, "outer_columns", 7, 400000 * cube // 1000)(
        core, outer, first_corner, second_corner, rows, cols, left
    )
    inner = columns(inner_kernel, "inner_columns", 5, cube)(outer, inner, rows, cols, left)

    strip = jax.ShapeDtypeStruct((margin, length), BF16)
    first, second, inside = kernel_call(
        functools.partial(main_kernel, half, scale),
        "tile_model",
        (strip, strip, jax.ShapeDtypeStruct((half, length), F32)),
        11,
        [
            pltpu.VMEM((half, length), BF16),
            pltpu.VMEM((half + 8, length), F32),
            pltpu.VMEM((2, half + 128, length), BF16),
            pltpu.VMEM((half, length), BF16),
        ],
        flops=20 * cube,
    )(
        core, inner, outer, re, im, rows, cols,
        constant["right"], constant["band_rows"], constant["band_columns"],
        constant["inverse_right"],
    )

    first = swap_rows(first, 1)
    second = swap_rows(second, 0)
    column = jax.ShapeDtypeStruct((half, margin), BF16)
    block = jax.ShapeDtypeStruct((half, half), F32)
    center, outer, inner = kernel_call(
        functools.partial(fold_rows_kernel, half), "fold_rows", (block, column, column), 3,
        [pltpu.VMEM((half, length), F32)],
    )(inside, second, first)
    outer = swap_columns(outer, 1)
    inner = swap_columns(inner, 0)
    return kernel_call(functools.partial(fold_columns_kernel, half), "fold_columns", block, 3)(
        center, outer, inner
    )


def solution(mesh):
    tables = host_tables(512)
    placed = (P(None, "dec", "ra"), P("dec", "ra"))
    return jax.shard_map(
        functools.partial(shards, tables), mesh=mesh, in_specs=placed, out_specs=P("dec", "ra"), check_vma=False
    )
```
